32 devices in a mesh: fsdp: 4 (over x, core), ctx: 2 (over y), tp: 4 (over z).
Axes of the slice: x: 2, y: 2, z: 4, core: 2. Of those that a mesh axis runs over, the one named last changes fastest.
Arguments:
- hidden_in: bfloat16 [4, 1024, 2048], P('fsdp', 'ctx'), may hold values from -6 to 6
- segment_ids: int32 [4, 1024], P('fsdp', 'ctx'), may hold values from 0 to 3, never falling along the last dimension, each value on 1 to 800 neighbouring positions
- adapter_ids: int32 [4], P('fsdp'), may hold values from 0 to 7
- attention_gain: bfloat16 [2048], replicated, may hold values from 0.099609375 to 1.8984375
- query_gain: bfloat16 [64], replicated, may hold values from 0.099609375 to 1.8984375
- key_gain: bfloat16 [64], replicated, may hold values from 0.099609375 to 1.8984375
- feedforward_gain: bfloat16 [2048], replicated, may hold values from 0.099609375 to 1.8984375
- query_weight: bfloat16 [2048, 2048], P('fsdp', 'tp'), may hold values from -0.125 to 0.125
- key_weight: bfloat16 [2048, 512], P('fsdp', 'tp'), may hold values from -0.125 to 0.125
- value_weight: bfloat16 [2048, 512], P('fsdp', 'tp'), may hold values from -0.125 to 0.125
- output_weight: bfloat16 [2048, 2048], P('tp', 'fsdp'), may hold values from -1 to 1
- gate_weight: bfloat16 [2048, 8192], P('fsdp', 'tp'), may hold values from -0.125 to 0.125
- linear_weight: bfloat16 [2048, 8192], P('fsdp', 'tp'), may hold values from -0.125 to 0.125
- reduce_weight: bfloat16 [8192, 2048], P('tp', 'fsdp'), may hold values from -0.0625 to 0.0625
- query_down: bfloat16 [8, 2048, 16], replicated, may hold values from -0.125 to 0.125
- query_lift: bfloat16 [8, 16, 2048], P(None, None, 'tp'), may hold values from -1.5 to 1.5
- key_down: bfloat16 [8, 2048, 16], replicated, may hold values from -0.125 to 0.125
- key_lift: bfloat16 [8, 16, 512], P(None, None, 'tp'), may hold values from -1.5 to 1.5
- value_down: bfloat16 [8, 2048, 16], replicated, may hold values from -0.125 to 0.125
- value_lift: bfloat16 [8, 16, 512], P(None, None, 'tp'), may hold values from -1.5 to 1.5
- output_down: bfloat16 [8, 2048, 16], P(None, 'tp'), may hold values from -1 to 1
- output_lift: bfloat16 [8, 16, 2048], replicated, may hold values from -1.5 to 1.5
- gate_down: bfloat16 [8, 2048, 16], replicated, may hold values from -0.125 to 0.125
- gate_lift: bfloat16 [8, 16, 8192], P(None, None, 'tp'), may hold values from -1.5 to 1.5
- linear_down: bfloat16 [8, 2048, 16], replicated, may hold values from -0.125 to 0.125
- linear_lift: bfloat16 [8, 16, 8192], P(None, None, 'tp'), may hold values from -1.5 to 1.5
- reduce_down: bfloat16 [8, 8192, 16], P(None, 'tp'), may hold values from -0.0625 to 0.0625
- reduce_lift: bfloat16 [8, 16, 2048], replicated, may hold values from -1.5 to 1.5
- output_cotangent: bfloat16 [4, 1024, 2048], P('fsdp', 'ctx'), may hold values from -6 to 6
Outputs:
- block_out: bfloat16 [4, 1024, 2048], P('fsdp', 'ctx', 'tp')
- input_grad: float32 [4, 1024, 2048], P('fsdp', 'ctx', 'tp')
- grad_query_down: float32 [8, 2048, 16], replicated
- grad_query_lift: float32 [8, 16, 2048], P(None, None, 'tp')
- grad_key_down: float32 [8, 2048, 16], replicated
- grad_key_lift: float32 [8, 16, 512], P(None, None, 'tp')
- grad_value_down: float32 [8, 2048, 16], replicated
- grad_value_lift: float32 [8, 16, 512], P(None, None, 'tp')
- grad_output_down: float32 [8, 2048, 16], P(None, 'tp')
- grad_output_lift: float32 [8, 16, 2048], replicated
- grad_gate_down: float32 [8, 2048, 16], replicated
- grad_gate_lift: float32 [8, 16, 8192], P(None, None, 'tp')
- grad_linear_down: float32 [8, 2048, 16], replicated
- grad_linear_lift: float32 [8, 16, 8192], P(None, None, 'tp')
- grad_reduce_down: float32 [8, 8192, 16], P(None, 'tp')
- grad_reduce_lift: float32 [8, 16, 2048], replicated
The draws below stay inside these ranges and needn't reach their ends.
Inputs may be any that keep to these rules, and one draw needn't show every extreme that they name: `segment_ids`: within each sequence the ids start at 0 and never fall; each of the 4 documents holds 1 to 800 consecutive tokens, and one holds exactly 800.
All inputs are finite; a program needn't handle non-finite values.
Results may differ from the reference program's by a relative error of at most 0.02.
Values may be sent and summed in bfloat16 or wider, within the bound.
No kernel may reach another device: no remote copies, remote signals or barrier semaphores. Data moves between devices by JAX's collectives and lax.ppermute only.
A program may use at most 192 MiB of HBM per device.

```python
import math
import jax
import jax.numpy as jnp
import numpy as np
from jax import lax

D = 2048
HEADS = 32
KV = 8
HD = 64
FF = 8192
RANK = 16
ADAPTERS = 8
LEN = 1024
DOCS = 4
DOC_MOST = 800
SEQS = 4


def set_ends(values, stream_key, smallest, largest):
    extent = values.shape
    place = [jax.random.randint(jax.random.fold_in(stream_key, axis), (), 0, extent[axis]) for axis in range(len(extent))]
    values = values.at[tuple(place)].set(smallest)
    longest = extent.index(max(extent))
    place[longest] = (place[longest] + 1) % extent[longest]
    return values.at[tuple(place)].set(largest)


def shard_levels(stream_key, shape, cuts, least, largest):
    level = 1.0
    for dim, shards_of in cuts:
        draws = jax.random.uniform(jax.random.fold_in(jax.random.fold_in(stream_key, 6), dim), (shards_of,), jnp.float32, least / len(cuts), largest / len(cuts))
        level = level * jnp.repeat(jnp.exp(draws), shape[dim] // shards_of).reshape((-1,) + (1,) * (len(shape) - 1 - dim))
    return level


def length_profile(number_of, total, limit, slope):
    weights = [(1 << 20) // math.isqrt(standing ** slope) + 1 for standing in range(2, number_of + 1)]
    surplus, given = total - limit - (number_of - 1), [1] * (number_of - 1)
    while surplus > 0:
        free = [i for i in range(number_of - 1) if given[i] < limit]
        whole, remaining = sum([weights[i] for i in free]), surplus
        for i in free:
            addition = min(limit - given[i], max(1, remaining * weights[i] // whole), surplus)
            given[i] = given[i] + addition
            surplus = surplus - addition
    return np.array([limit] + given)


def ragged_sizes(key, amount, total, reach, slope):
    if amount == 2:
        one = jax.random.randint(key, (), max(1, total - reach), min(reach, total - 1) + 1)
        return jnp.stack([one, total - one])
    tallies = jnp.asarray(length_profile(amount, total, reach, slope), jnp.int32)
    couples = (amount - 1) // 2
    donor, taker = tallies[1:1 + 2 * couples:2], tallies[2:2 + 2 * couples:2]
    room = jnp.minimum(donor - 1, reach - taker)
    shifted = jax.random.randint(jax.random.fold_in(key, 1), (couples,), 0, 1 << 20) % (room + 1)
    tallies = tallies.at[1:1 + 2 * couples:2].set(donor - shifted).at[2:2 + 2 * couples:2].set(taker + shifted)
    return tallies[jax.random.permutation(jax.random.fold_in(key, 2), amount)]


def noise(stream_key, extent, width, bound, split=(), dtype=jnp.bfloat16):
    drawn = jax.random.normal(stream_key, extent, jnp.float32) * width
    if len(split) > 0:
        drawn = shard_levels(stream_key, extent, split, -0.22, 0.18) * drawn
    return jnp.clip(drawn, min=-bound, max=bound).astype(dtype)


def setup_inputs(seed: int = 0) -> dict:
    key_of = jax.random.split(jax.random.key(seed), 30)
    hidden_in = noise(key_of[0], (SEQS, LEN, D), 1.0, 6.0, ((0, 4), (1, 2)))
    segment_ids = jax.vmap(lambda own: jnp.searchsorted(jnp.cumsum(ragged_sizes(own, DOCS, LEN, DOC_MOST, 0)), jnp.arange(LEN), side="right"))(jax.random.split(key_of[1], SEQS)).reshape((SEQS, LEN)).astype(jnp.int32)
    adapter_ids = set_ends(jax.random.randint(key_of[2], (SEQS,), 0, ADAPTERS), jax.random.fold_in(key_of[2], 1), 0, ADAPTERS - 1).astype(jnp.int32)
    attention_gain = jnp.clip(1.0 + 0.18 * jax.random.normal(key_of[3], (D,), jnp.float32), 0.099609375, 1.8984375).astype(jnp.bfloat16)
    query_gain = jnp.clip(1.0 + 0.18 * jax.random.normal(key_of[4], (HD,), jnp.float32), 0.099609375, 1.8984375).astype(jnp.bfloat16)
    key_gain = jnp.clip(1.0 + 0.18 * jax.random.normal(key_of[5], (HD,), jnp.float32), 0.099609375, 1.8984375).astype(jnp.bfloat16)
    feedforward_gain = jnp.clip(1.0 + 0.18 * jax.random.normal(key_of[6], (D,), jnp.float32), 0.099609375, 1.8984375).astype(jnp.bfloat16)
    query_weight = noise(key_of[7], (D, HEADS * HD), D ** -0.5, 0.125, ((0, 4), (1, 4)))
    key_weight = noise(key_of[8], (D, KV * HD), D ** -0.5, 0.125, ((0, 4), (1, 4)))
    value_weight = noise(key_of[9], (D, KV * HD), D ** -0.5, 0.125, ((0, 4), (1, 4)))
    output_weight = noise(key_of[10], (HEADS * HD, D), (HEADS * HD // 64) ** -0.5, 1.0, ((0, 4), (1, 4)))
    gate_weight = noise(key_of[11], (D, FF), D ** -0.5, 0.125, ((0, 4), (1, 4)))
    linear_weight = noise(key_of[12], (D, FF), D ** -0.5, 0.125, ((0, 4), (1, 4)))
    reduce_weight = noise(key_of[13], (FF, D), FF ** -0.5, 0.0625, ((0, 4), (1, 4)))
    query_down = noise(key_of[14], (ADAPTERS, D, RANK), D ** -0.5, 0.125)
    query_lift = noise(key_of[15], (ADAPTERS, RANK, HEADS * HD), RANK ** -0.5, 1.5, ((2, 4),))
    key_down = noise(key_of[16], (ADAPTERS, D, RANK), D ** -0.5, 0.125)
    key_lift = noise(key_of[17], (ADAPTERS, RANK, KV * HD), RANK ** -0.5, 1.5, ((2, 4),))
    value_down = noise(key_of[18], (ADAPTERS, D, RANK), D ** -0.5, 0.125)
    value_lift = noise(key_of[19], (ADAPTERS, RANK, KV * HD), RANK ** -0.5, 1.5, ((2, 4),))
    output_down = noise(key_of[20], (ADAPTERS, HEADS * HD, RANK), (HEADS * HD // 64) ** -0.5, 1.0, ((1, 4),))
    output_lift = noise(key_of[21], (ADAPTERS, RANK, D), RANK ** -0.5, 1.5)
    gate_down = noise(key_of[22], (ADAPTERS, D, RANK), D ** -0.5, 0.125)
    gate_lift = noise(key_of[23], (ADAPTERS, RANK, FF), RANK ** -0.5, 1.5, ((2, 4),))
    linear_down = noise(key_of[24], (ADAPTERS, D, RANK), D ** -0.5, 0.125)
    linear_lift = noise(key_of[25], (ADAPTERS, RANK, FF), RANK ** -0.5, 1.5, ((2, 4),))
    reduce_down = noise(key_of[26], (ADAPTERS, FF, RANK), FF ** -0.5, 0.0625, ((1, 4),))
    reduce_lift = noise(key_of[27], (ADAPTERS, RANK, D), RANK ** -0.5, 1.5)
    output_cotangent = noise(key_of[28], (SEQS, LEN, D), 1.0, 6.0, ((0, 4), (1, 2)))
    return {"hidden_in": hidden_in, "segment_ids": segment_ids, "adapter_ids": adapter_ids, "attention_gain": attention_gain, "query_gain": query_gain, "key_gain": key_gain, "feedforward_gain": feedforward_gain, "query_weight": query_weight, "key_weight": key_weight, "value_weight": value_weight, "output_weight": output_weight, "gate_weight": gate_weight, "linear_weight": linear_weight, "reduce_weight": reduce_weight, "query_down": query_down, "query_lift": query_lift, "key_down": key_down, "key_lift": key_lift, "value_down": value_down, "value_lift": value_lift, "output_down": output_down, "output_lift": output_lift, "gate_down": gate_down, "gate_lift": gate_lift, "linear_down": linear_down, "linear_lift": linear_lift, "reduce_down": reduce_down, "reduce_lift": reduce_lift, "output_cotangent": output_cotangent}


@jax.custom_vjp
def low(v):
    return lax.optimization_barrier(v.astype(jnp.bfloat16)).astype(jnp.float32)

@jax.custom_vjp
def low_back(v):
    return v

def low_keep(v):
    return (low(v), None)

def low_pass(kept, grad):
    return (grad,)

def back_keep(v):
    return (v, None)

def back_low(kept, grad):
    return (low(grad),)
low.defvjp(low_keep, low_pass)
low_back.defvjp(back_keep, back_low)
epsilon = 1e-05
rope_base = 1000000.0
masked_score = -1e+30

def product(left_side, right_side):
    return jnp.dot(left_side, right_side, precision=lax.Precision.HIGHEST, preferred_element_type=jnp.float32)

def root_norm(hidden, norm_gain):
    return hidden * lax.rsqrt(lax.optimization_barrier(jnp.mean(hidden * hidden, axis=-1, keepdims=True)) + epsilon) * norm_gain

def rotate(hidden, cosine, sine_table):
    half_width = hidden.shape[-1] // 2
    first_half = hidden[..., :half_width]
    second_half = hidden[..., half_width:]
    return jnp.concatenate([first_half * cosine - second_half * sine_table, second_half * cosine + first_half * sine_table], axis=-1)

def block_forward(hidden_all, adapters, segment_ids, adapter_ids, frozen):
    attention_gain, query_gain, key_gain, feedforward_gain, query_weight, key_weight, value_weight, output_weight, gate_weight, linear_weight, reduce_weight = frozen
    query_down, query_lift, key_down, key_lift, value_down, value_lift, output_down, output_lift, gate_down, gate_lift, linear_down, linear_lift, reduce_down, reduce_lift = adapters
    positions = jnp.arange(LEN).astype(jnp.float32)
    frequency = rope_base ** (-2.0 * jnp.arange(HD // 2).astype(jnp.float32) / HD)
    angles = positions[:, None] * frequency[None, :]
    cosine = jnp.cos(angles)[:, None, :]
    sine_table = jnp.sin(angles)[:, None, :]
    token_index = jnp.arange(LEN)
    causal = token_index[:, None] >= token_index[None, :]
    group_share = HEADS // KV

    def one_sequence(packed):
        hidden, segments, adapter = packed

        def project(inputs, weight, down_table, lift_table):
            return product(inputs, weight) + product(product(inputs, down_table[adapter]), lift_table[adapter])
        normed = low(root_norm(hidden, attention_gain))
        query = low_back(project(normed, query_weight, query_down, query_lift)).reshape(LEN, HEADS, HD)
        key_heads = low_back(project(normed, key_weight, key_down, key_lift)).reshape(LEN, KV, HD)
        value_heads = low(low_back(project(normed, value_weight, value_down, value_lift))).reshape(LEN, KV, HD)
        query_rot = low(rotate(root_norm(query, query_gain), cosine, sine_table)).reshape(LEN, KV, group_share, HD)
        key_rot = low(rotate(root_norm(key_heads, key_gain), cosine, sine_table))
        raw_scores = low_back(jnp.einsum('qgsd,kgd->gsqk', query_rot, key_rot, precision=lax.Precision.HIGHEST) * HD ** (-0.5))
        allowed = causal & (segments[:, None] == segments[None, :])
        scores = jnp.where(allowed[None, None], raw_scores, masked_score)
        row_max = lax.optimization_barrier(jnp.max(scores, axis=-1, keepdims=True))
        exponent = jnp.exp(scores - row_max)
        prob_rows = low(exponent / lax.optimization_barrier(jnp.sum(exponent, axis=-1, keepdims=True)))
        attended = jnp.einsum('gsqk,kgd->qgsd', prob_rows, value_heads, precision=lax.Precision.HIGHEST).reshape(LEN, HEADS * HD)
        attended = low(low_back(attended))
        middle = hidden + low_back(project(attended, output_weight, output_down, output_lift))
        ffn_normed = low(root_norm(middle, feedforward_gain))
        gate = low_back(project(ffn_normed, gate_weight, gate_down, gate_lift))
        linear = low_back(project(ffn_normed, linear_weight, linear_down, linear_lift))
        inner = low(jax.nn.silu(gate) * linear)
        return middle + project(inner, reduce_weight, reduce_down, reduce_lift)
    return lax.map(jax.checkpoint(one_sequence), (hidden_all, segment_ids, adapter_ids))

def reference(hidden_in, segment_ids, adapter_ids, attention_gain, query_gain, key_gain, feedforward_gain, query_weight, key_weight, value_weight, output_weight, gate_weight, linear_weight, reduce_weight, query_down, query_lift, key_down, key_lift, value_down, value_lift, output_down, output_lift, gate_down, gate_lift, linear_down, linear_lift, reduce_down, reduce_lift, output_cotangent):
    frozen = tuple((tensor.astype(jnp.float32) for tensor in (attention_gain, query_gain, key_gain, feedforward_gain, query_weight, key_weight, value_weight, output_weight, gate_weight, linear_weight, reduce_weight)))
    adapters = tuple((tensor.astype(jnp.float32) for tensor in (query_down, query_lift, key_down, key_lift, value_down, value_lift, output_down, output_lift, gate_down, gate_lift, linear_down, linear_lift, reduce_down, reduce_lift)))

    def forward(hidden_all, adapter_all):
        return block_forward(hidden_all, adapter_all, segment_ids, adapter_ids, frozen)
    block_out, pull_back = jax.vjp(forward, hidden_in.astype(jnp.float32), adapters)
    input_grad, adapter_grads = pull_back(output_cotangent.astype(jnp.float32))
    return (block_out.astype(jnp.bfloat16), input_grad, adapter_grads[0], adapter_grads[1], adapter_grads[2], adapter_grads[3], adapter_grads[4], adapter_grads[5], adapter_grads[6], adapter_grads[7], adapter_grads[8], adapter_grads[9], adapter_grads[10], adapter_grads[11], adapter_grads[12], adapter_grads[13])
```

```python
from functools import partial

import jax
import jax.numpy as jnp
from jax import lax
from jax.experimental import pallas as pl
from jax.experimental.pallas import tpu as pltpu
from jax.sharding import PartitionSpec as P

epsilon = 1e-05
rope_base = 1000000.0
masked = -1e30
f32 = jnp.float32
bf16 = jnp.bfloat16
lanes = 128
half = 64
rank = 16
vmem_bytes = 58 * 1024 * 1024


def nn(left, right):
    return lax.dot_general(left, right, (((1,), (0,)), ((), ())), preferred_element_type=f32)


def nt(left, right):
    return lax.dot_general(left, right, (((1,), (1,)), ((), ())), preferred_element_type=f32)


def at(ref, index):
    return pl.multiple_of(ref[index], lanes)


def fixed(shape):
    return pl.BlockSpec(shape, lambda *_: (0,) * len(shape), pipeline_mode=pl.Buffered(1))


def result(shape, dtype):
    return jax.ShapeDtypeStruct(shape, dtype)


def lane_of(shape):
    return lax.broadcasted_iota(jnp.int32, shape, len(shape) - 1)


def head_mean_matrix():
    row = lax.broadcasted_iota(jnp.int32, (lanes, lanes), 0)
    col = lax.broadcasted_iota(jnp.int32, (lanes, lanes), 1)
    return jnp.where((row // half) == (col // half), 1.0 / half, 0.0).astype(bf16)


def head_mean(values, matrix):
    high = values.astype(bf16)
    low = (values - high.astype(f32)).astype(bf16)
    return nn(high, matrix) + nn(low, matrix)


def partner(values):
    first = (lane_of(values.shape) % half) < (half // 2)
    return jnp.where(
        first,
        pltpu.roll(values, lanes - half // 2, values.ndim - 1),
        pltpu.roll(values, half // 2, values.ndim - 1),
    )


def swap_halves(values):
    return pltpu.roll(values, half, values.ndim - 1)


def qkv_kernel(
    meta, hid, gain, q0, q1, q2, q3, kv0, kv1, kv2, kv3, aq, ak, av, bq, bk, bv, qg, kg, cos, sin,
    seg, normed, narrow, pre, qrot, kv, a_all, b_all,
):
    q_width, kv_width = bq.shape[2], bk.shape[2]

    @pl.when(pl.program_id(0) == 0)
    def _():
        a_all[...] = jnp.zeros_like(a_all)
        b_all[...] = jnp.zeros_like(b_all)
        a_all[0:rank, :] = aq[0]
        a_all[rank : 2 * rank, :] = ak[0]
        a_all[2 * rank : 3 * rank, :] = av[0]
        b_all[0:rank, 0:q_width] = bq[0]
        b_all[rank : 2 * rank, q_width : q_width + kv_width] = bk[0]
        b_all[2 * rank : 3 * rank, q_width + kv_width :] = bv[0]

    wide = hid[...].astype(f32)
    inverse = lax.rsqrt(jnp.mean(wide * wide, axis=-1, keepdims=True) + epsilon)
    normed[...] = (wide * inverse * gain[...].astype(f32)).astype(bf16)
    low = nt(normed[...], a_all[...]).astype(bf16)
    narrow[...] = low
    total = nn(low, b_all[...])
    q_total, kv_total = total[:, :q_width], total[:, q_width:]
    for index, (q_weight, kv_weight) in enumerate(((q0, kv0), (q1, kv1), (q2, kv2), (q3, kv3))):
        part = normed[:, pl.ds(at(meta, index), q_weight.shape[0])]
        q_total = q_total + nn(part, q_weight[...])
        kv_total = kv_total + nn(part, kv_weight[...])
    total = jnp.concatenate([q_total, kv_total], axis=1)
    pre[...] = total[:, : q_width + kv_width]
    matrix = head_mean_matrix()
    for start in range(0, q_width + kv_width, lanes):
        part = total[:, start : start + lanes]
        head_gain = qg if start < q_width else kg
        scaled = part * lax.rsqrt(head_mean(part * part, matrix) + epsilon) * head_gain[...]
        turned = (scaled * cos[...] + partner(scaled) * sin[...]).astype(bf16)
        if start < q_width:
            qrot[:, start : start + lanes] = turned
        else:
            kv[:, start - q_width : start - q_width + lanes] = turned
    kv[:, kv_width : 2 * kv_width] = total[:, q_width + kv_width :].astype(bf16)
    kv[:, 2 * kv_width :] = jnp.broadcast_to(seg[...].astype(f32), (seg.shape[0], lanes)).astype(bf16)


def qkv_forward(meta, hid, gain, weights, downs, lifts, q_gain, k_gain, cos, sin, seg):
    length, width = hid.shape
    q_width, kv_width = lifts[0].shape[2], lifts[1].shape[2]
    block = 256
    tile = lambda w: pl.BlockSpec((block, w), lambda i, m: (i, 0))
    pick = lambda a: pl.BlockSpec(
        (1,) + a.shape[1:], lambda i, m: (m[7], 0, 0), pipeline_mode=pl.Buffered(1)
    )
    return pl.pallas_call(
        qkv_kernel,
        name="qkv_forward",
        grid_spec=pltpu.PrefetchScalarGridSpec(
            num_scalar_prefetch=1,
            grid=(length // block,),
            in_specs=[tile(width), fixed(gain.shape)]
            + [fixed(w.shape) for w in weights]
            + [pick(a) for a in downs]
            + [pick(a) for a in lifts]
            + [fixed(q_gain.shape), fixed(k_gain.shape), tile(lanes), tile(lanes), tile(1)],
            out_specs=[
                tile(width), tile(lanes), tile(q_width + kv_width), tile(q_width),
                tile(2 * kv_width + lanes),
            ],
            scratch_shapes=[
                pltpu.VMEM((lanes, width), bf16),
                pltpu.VMEM((lanes, q_width + 2 * kv_width), bf16),
            ],
        ),
        out_shape=[
            result((length, width), bf16),
            result((length, lanes), bf16),
            result((length, q_width + kv_width), f32),
            result((length, q_width), bf16),
            result((length, 2 * kv_width + lanes), bf16),
        ],
        cost_estimate=pl.CostEstimate(flops=1024, transcendentals=0, bytes_accessed=1024),
        compiler_params=pltpu.CompilerParams(vmem_limit_bytes=vmem_bytes),
    )(meta, hid, gain, *weights, *downs, *lifts, q_gain, k_gain, cos, sin, seg)


def spread_keys(kv, kd, v0, v1, rows, size):
    lane = lane_of((size, lanes))
    key = kv[:, 0:lanes].astype(f32)
    other = swap_halves(key)
    kd[0, rows : rows + size, :] = jnp.where(lane < half, key, other).astype(bf16)
    kd[1, rows : rows + size, :] = jnp.where(lane < half, other, key).astype(bf16)
    value = kv[:, lanes : 2 * lanes].astype(f32)
    other = swap_halves(value)
    v0[0, rows : rows + size, :] = jnp.where(lane < half, value, 1.0).astype(bf16)
    v0[1, rows : rows + size, :] = jnp.where(lane < half, other, 1.0).astype(bf16)
    v1[0, rows : rows + size, :] = jnp.where(lane < half, 1.0, other).astype(bf16)
    v1[1, rows : rows + size, :] = jnp.where(lane < half, 1.0, value).astype(bf16)


def attention_kernel(
    meta, qrot, kvf, kvn, kvq, att, wide, inv, kd, v0, v1, bias, segk, *, log_scale, block,
):
    far = kvf.shape[0]
    pairs = qrot.shape[1] // lanes
    share = pairs // 2
    step = pl.program_id(0)

    @pl.when(step == 0)
    def _():
        spread_keys(kvf, kd, v0, v1, 0, far)
        spread_keys(kvn, kd, v0, v1, far, kvn.shape[0])
        away = kvf[:, 2 * lanes :].astype(f32).T[0:8]
        segk[:, 0:far] = jnp.where(meta[5] > 0, away, -1.0)
        segk[:, far:] = kvn[:, 2 * lanes :].astype(f32).T[0:8]

    def queries(number):
        keys = far + (number + 1) * block
        key = lax.broadcasted_iota(jnp.int32, (block, keys), 1)
        query = lax.broadcasted_iota(jnp.int32, (block, keys), 0) + (far + number * block)
        segq = kvq[:, 2 * lanes :].astype(f32)[:, 0:1]
        allowed = (segq == segk[0:1, 0:keys]) & (key <= query)
        bias[:, 0:keys] = jnp.where(allowed, 0.0, masked)
        lane = lane_of((block, lanes))

        def body(pair, carry):
            group = pair // share
            place = pl.ds(pl.multiple_of(pair * lanes, lanes), lanes)
            q = qrot[:, place].astype(f32)
            q0 = jnp.where(lane < half, q, 0.0).astype(bf16)
            q1 = jnp.where(lane < half, 0.0, q).astype(bf16)
            k = kd[group, 0:keys, :]
            e0 = jnp.exp2(nt(q0, k) * log_scale + bias[:, 0:keys]).astype(bf16)
            r0 = nn(e0, v0[group, 0:keys, :])
            e1 = jnp.exp2(nt(q1, k) * log_scale + bias[:, 0:keys]).astype(bf16)
            r1 = nn(e1, v1[group, 0:keys, :])
            inverse = 1.0 / jnp.where(lane < half, swap_halves(r0), swap_halves(r1))
            out = jnp.where(lane < half, r0, r1) * inverse
            wide[:, place] = out
            inv[:, place] = inverse
            att[:, place] = out.astype(bf16)
            return carry

        lax.fori_loop(0, pairs, body, 0)

    for number in range(kvn.shape[0] // block):
        pl.when(step == number)(partial(queries, number))


def attention_forward(meta, qrot, kvf, kvn, log_scale):
    length, q_width = qrot.shape
    block = 256
    keys = kvf.shape[0] + length
    tile = lambda w: pl.BlockSpec((block, w), lambda i, m: (i, 0))
    return pl.pallas_call(
        partial(attention_kernel, log_scale=log_scale, block=block),
        name="attention_forward",
        grid_spec=pltpu.PrefetchScalarGridSpec(
            num_scalar_prefetch=1,
            grid=(length // block,),
            in_specs=[tile(q_width), fixed(kvf.shape), fixed(kvn.shape), tile(kvn.shape[1])],
            out_specs=[tile(q_width), tile(q_width), tile(q_width)],
            scratch_shapes=[
                pltpu.VMEM((2, keys, lanes), bf16),
                pltpu.VMEM((2, keys, lanes), bf16),
                pltpu.VMEM((2, keys, lanes), bf16),
                pltpu.VMEM((block, keys), f32),
                pltpu.VMEM((8, keys), f32),
            ],
        ),
        out_shape=[
            result((length, q_width), bf16),
            result((length, q_width), f32),
            result((length, q_width), f32),
        ],
        cost_estimate=pl.CostEstimate(flops=1024, transcendentals=0, bytes_accessed=1024),
        compiler_params=pltpu.CompilerParams(vmem_limit_bytes=vmem_bytes),
    )(meta, qrot, kvf, kvn, kvn)


def output_kernel(meta, att, w0, w1, w2, w3, ao, bo, branch, narrow, a_all, b_all):
    @pl.when(pl.program_id(0) == 0)
    def _():
        a_all[...] = jnp.zeros_like(a_all)
        b_all[...] = jnp.zeros_like(b_all)
        a_all[0:rank, :] = ao[0]
        b_all[0:rank, :] = bo[0]

    own = att[...]
    low = nt(own, a_all[...]).astype(bf16)
    narrow[...] = low
    for index, weight in enumerate((w0, w1, w2, w3)):
        columns = pl.ds(at(meta, index), weight.shape[1])
        branch[:, columns] = (nn(own, weight[...]) + nn(low, b_all[:, columns])).astype(bf16)


def output_forward(meta, att, weights, down, lift):
    length, q_width = att.shape
    model = lift.shape[2]
    block = 256
    tile = lambda w: pl.BlockSpec((block, w), lambda i, m: (i, 0))
    pick = lambda a: pl.BlockSpec(
        (1,) + a.shape[1:], lambda i, m: (m[7], 0, 0), pipeline_mode=pl.Buffered(1)
    )
    return pl.pallas_call(
        output_kernel,
        name="output_forward",
        grid_spec=pltpu.PrefetchScalarGridSpec(
            num_scalar_prefetch=1,
            grid=(length // block,),
            in_specs=[tile(q_width)] + [fixed(w.shape) for w in weights] + [pick(down), pick(lift)],
            out_specs=[tile(model), tile(lanes)],
            scratch_shapes=[pltpu.VMEM((lanes, q_width), bf16), pltpu.VMEM((lanes, model), bf16)],
        ),
        out_shape=[result((length, model), bf16), result((length, lanes), bf16)],
        cost_estimate=pl.CostEstimate(flops=1024, transcendentals=0, bytes_accessed=1024),
        compiler_params=pltpu.CompilerParams(vmem_limit_bytes=vmem_bytes),
    )(meta, att, *weights, down, lift)


def picked(array):
    return pl.BlockSpec(
        (1,) + array.shape[1:], lambda i, m: (m[7], 0, 0), pipeline_mode=pl.Buffered(1)
    )


def strip(array, width):
    return pl.BlockSpec((1, rank, width), lambda j, m: (m[7], 0, j))


def params():
    return pltpu.CompilerParams(vmem_limit_bytes=vmem_bytes)


def ffn_kernel(meta, hid, branch, cot, gain, *refs, shards, chunk):
    gates, linears, reduces = (refs[i:j] for i, j in zip((0,) + shards[:-1], shards))
    refs = refs[shards[-1] :]
    ag, al, ar, bg, bl, br = refs[:6]
    back, inner_out, gate_out, linear_out, n_gl_t, m_gl_t, m_r_t = refs[6:13]
    x, grad_sum, n_gl, m_gl, m_r, a_gl, b_r, b_g, b_l, a_r = refs[13:]
    step = pl.program_id(0)
    length = hid.shape[0]
    count = length // chunk

    def rows_of(index):
        return pl.ds(pl.multiple_of(index * chunk, chunk), chunk)

    def chunks(body):
        def run(index, carry):
            body(rows_of(index))
            return carry

        lax.fori_loop(0, count, run, 0)

    def normal(rows):
        middle = hid[rows, :].astype(f32) + branch[rows, :].astype(f32)
        inverse = lax.rsqrt(jnp.mean(middle * middle, axis=-1, keepdims=True) + epsilon)
        return middle, inverse

    @pl.when(step == 0)
    def _():
        for ref in (a_gl, b_r, b_g, b_l, a_r):
            ref[...] = jnp.zeros_like(ref)
        a_gl[0:rank, :] = ag[0]
        a_gl[rank : 2 * rank, :] = al[0]
        b_r[0:rank, :] = br[0]

        def body(rows):
            back_low = nt(cot[rows, :], b_r[...])
            m_r[rows, :] = back_low.astype(bf16)
            m_r_t[:, rows] = back_low.T[0:rank].astype(bf16)
            middle, inverse = normal(rows)
            x[rows, :] = (middle * inverse * gain[...].astype(f32)).astype(bf16)
            low = nt(x[rows, :], a_gl[...])
            n_gl[rows, :] = low.astype(bf16)
            n_gl_t[:, rows] = low.T[0 : 2 * rank].astype(bf16)
            m_gl[rows, :] = jnp.zeros((chunk, lanes), f32)

        chunks(body)

    b_g[0:rank, :] = bg[0]
    b_l[rank : 2 * rank, :] = bl[0]
    a_r[0:rank, :] = ar[0]

    def place(index, weight, axis):
        return pl.ds(at(meta, index), weight.shape[axis])

    def body(rows, first):
        low = n_gl[rows, :]
        gate = nn(low, b_g[...])
        linear = nn(low, b_l[...])
        for index, weight in enumerate(gates):
            gate = gate + nn(x[rows, place(8 + index, weight, 0)], weight[...])
        for index, weight in enumerate(linears):
            linear = linear + nn(x[rows, place(index, weight, 0)], weight[...])
        upstream = nn(m_r[rows, :], a_r[...])
        for index, weight in enumerate(reduces):
            upstream = upstream + nt(cot[rows, place(index, weight, 1)], weight[...])
        sigmoid = jax.nn.sigmoid(gate)
        active = gate * sigmoid
        gate_grad = (upstream * linear * sigmoid * (1.0 + gate * (1.0 - sigmoid))).astype(bf16)
        linear_grad = (upstream * active).astype(bf16)
        inner_out[rows, :] = (active * linear).astype(bf16)
        gate_out[rows, :] = gate_grad
        linear_out[rows, :] = linear_grad
        m_gl[rows, :] += nt(gate_grad, b_g[...]) + nt(linear_grad, b_l[...])
        for index, weight in enumerate(linears):
            columns = place(index, weight, 0)
            backward = nt(linear_grad, weight[...])
            if first:
                grad_sum[rows, columns] = backward
            else:
                grad_sum[rows, columns] += backward
        for index, weight in enumerate(gates):
            grad_sum[rows, place(8 + index, weight, 0)] += nt(gate_grad, weight[...])

    pl.when(step == 0)(partial(chunks, partial(body, first=True)))
    pl.when(step > 0)(partial(chunks, partial(body, first=False)))

    @pl.when(step == pl.num_programs(0) - 1)
    def _():
        def finish(rows):
            upstream = grad_sum[rows, :] + nn(m_gl[rows, :].astype(bf16), a_gl[...])
            middle, inverse = normal(rows)
            weighted = upstream * gain[...].astype(f32)
            mean = jnp.mean(weighted * middle, axis=-1, keepdims=True)
            back[rows, :] = (
                inverse * weighted - middle * (inverse * inverse * inverse * mean)
            ).astype(bf16)

        chunks(finish)
        m_gl_t[...] = m_gl[...].T[0 : 2 * rank].astype(bf16)


def ffn(
    meta, hid, branch, cot, gain, gates, linears, reduces, downs, lifts, width=512, chunk=512
):
    length, model = hid.shape
    hidden = gates[0].shape[1]
    rows = [*gates, *linears]
    shards = (len(gates), len(rows), len(rows) + len(reduces))
    column = lambda: pl.BlockSpec((length, width), lambda j, m: (0, j))
    return pl.pallas_call(
        partial(ffn_kernel, shards=shards, chunk=chunk),
        name="feed_forward",
        grid_spec=pltpu.PrefetchScalarGridSpec(
            num_scalar_prefetch=1,
            grid=(hidden // width,),
            in_specs=[fixed(hid.shape), fixed(branch.shape), fixed(cot.shape), fixed(gain.shape)]
            + [pl.BlockSpec((w.shape[0], width), lambda j, m: (0, j)) for w in rows]
            + [pl.BlockSpec((width, w.shape[1]), lambda j, m: (j, 0)) for w in reduces]
            + [picked(downs[0]), picked(downs[1]), strip(downs[2], width)]
            + [strip(lifts[0], width), strip(lifts[1], width), picked(lifts[2])],
            out_specs=[
                fixed((length, model)), column(), column(), column(),
                fixed((2 * rank, length)), fixed((2 * rank, length)), fixed((rank, length)),
            ],
            scratch_shapes=[
                pltpu.VMEM((length, model), bf16),
                pltpu.VMEM((length, model), f32),
                pltpu.VMEM((length, lanes), bf16),
                pltpu.VMEM((length, lanes), f32),
                pltpu.VMEM((length, lanes), bf16),
                pltpu.VMEM((lanes, model), bf16),
                pltpu.VMEM((lanes, model), bf16),
                pltpu.VMEM((lanes, width), bf16),
                pltpu.VMEM((lanes, width), bf16),
                pltpu.VMEM((lanes, width), bf16),
            ],
        ),
        out_shape=[result((length, model), bf16)]
        + [result((length, hidden), bf16)] * 3
        + [result((2 * rank, length), bf16)] * 2
        + [result((rank, length), bf16)],
        cost_estimate=pl.CostEstimate(
            flops=8 * length * model * hidden, transcendentals=length * hidden,
            bytes_accessed=4 * model * hidden + 14 * length * model,
        ),
        compiler_params=params(),
    )(meta, hid, branch, cot, gain, *rows, *reduces, *downs, *lifts)


def ffn_adapter_kernel(
    meta, hid, branch, cot, gain, inner, gate_grad, linear_grad, n_gl_t, m_gl_t, m_r_t, ar,
    part_pack, full_pack, n_r, low_sum, a_r,
):
    step = pl.program_id(0)

    @pl.when(step == 0)
    def _():
        a_r[...] = jnp.zeros_like(a_r)
        low_sum[...] = jnp.zeros_like(low_sum)

    a_r[0:rank, :] = ar[0]
    part_pack[0:rank, :] = nn(n_gl_t[...], gate_grad[...])[0:rank].astype(bf16)
    part_pack[rank : 2 * rank, :] = nn(n_gl_t[...], linear_grad[...])[rank:].astype(bf16)
    part_pack[2 * rank :, :] = nn(m_r_t[...], inner[...]).astype(bf16)
    low_sum[...] += nt(inner[...], a_r[...])

    @pl.when(step == pl.num_programs(0) - 1)
    def _():
        low = low_sum[...]
        n_r[...] = low.astype(bf16)
        full_pack[2 * rank :, :] = nn(low.T[0:rank].astype(bf16), cot[...]).astype(bf16)
        middle = hid[...].astype(f32) + branch[...].astype(f32)
        inverse = lax.rsqrt(jnp.mean(middle * middle, axis=-1, keepdims=True) + epsilon)
        x = (middle * inverse * gain[...].astype(f32)).astype(bf16)
        full_pack[0 : 2 * rank, :] = nn(m_gl_t[...], x).astype(bf16)


def ffn_adapters(meta, hid, branch, cot, gain, inner, gate_grad, linear_grad, n_gl_t, m_gl_t, m_r_t, down):
    length, model = hid.shape
    hidden = inner.shape[1]
    width = 512
    column = lambda: pl.BlockSpec((length, width), lambda j, m: (0, j))
    return pl.pallas_call(
        ffn_adapter_kernel,
        name="feed_forward_adapters",
        grid_spec=pltpu.PrefetchScalarGridSpec(
            num_scalar_prefetch=1,
            grid=(hidden // width,),
            in_specs=[fixed(hid.shape), fixed(branch.shape), fixed(cot.shape), fixed(gain.shape)]
            + [column(), column(), column()]
            + [fixed(n_gl_t.shape), fixed(m_gl_t.shape), fixed(m_r_t.shape), strip(down, width)],
            out_specs=[
                pl.BlockSpec((3 * rank, width), lambda j, m: (0, j)),
                fixed((3 * rank, model)),
                fixed((length, lanes)),
            ],
            scratch_shapes=[pltpu.VMEM((length, lanes), f32), pltpu.VMEM((lanes, width), bf16)],
        ),
        out_shape=[
            result((3 * rank, hidden), bf16),
            result((3 * rank, model), bf16),
            result((length, lanes), bf16),
        ],
        cost_estimate=pl.CostEstimate(
            flops=512 * length * hidden, transcendentals=0, bytes_accessed=12 * length * model
        ),
        compiler_params=params(),
    )(meta, hid, branch, cot, gain, inner, gate_grad, linear_grad, n_gl_t, m_gl_t, m_r_t, down)


def reduce_kernel(meta, inner, n_r, *refs):
    *weights, br, out, b_r = refs
    b_r[...] = jnp.zeros_like(b_r)
    b_r[0:rank, :] = br[0]
    for index, weight in enumerate(weights):
        columns = pl.ds(at(meta, index), weight.shape[1])
        out[:, columns] = (nn(inner[...], weight[...]) + nn(n_r[...], b_r[:, columns])).astype(bf16)


def reduce_forward(meta, inner, n_r, reduces, lift):
    length = inner.shape[0]
    model = lift.shape[2]
    return pl.pallas_call(
        reduce_kernel,
        name="reduce_forward",
        grid_spec=pltpu.PrefetchScalarGridSpec(
            num_scalar_prefetch=1,
            grid=(1,),
            in_specs=[fixed(inner.shape), fixed(n_r.shape)]
            + [fixed(w.shape) for w in reduces]
            + [picked(lift)],
            out_specs=fixed((length, model)),
            scratch_shapes=[pltpu.VMEM((lanes, model), bf16)],
        ),
        out_shape=result((length, model), bf16),
        cost_estimate=pl.CostEstimate(
            flops=2 * length * model * inner.shape[1], transcendentals=0,
            bytes_accessed=12 * 1024 * 1024,
        ),
        compiler_params=params(),
    )(meta, inner, n_r, *reduces, lift)


def attention_back(
    qrot, dop, mixed, kd, v0, v1, kt, bias, dq_t, dk, dv, rows, block, keys, log_scale, fresh,
):
    pairs = qrot.shape[1] // lanes
    share = pairs // 2
    lane = lane_of((block, lanes))
    queries = pl.ds(rows, block)

    def body(pair, carry):
        group = pair // share
        start = pl.multiple_of(pair * lanes, lanes)
        place = pl.ds(start, lanes)
        q = qrot[queries, place].astype(f32)
        up = dop[queries, place].astype(f32)
        mix = mixed[queries, place].astype(f32)
        k = kd[group, 0:keys, :]
        k_t = kt[group, :, 0:keys]
        dk_sum = dk[group, 0:keys, :]
        dv_sum = dv[group, 0:keys, :]
        for head, values in enumerate((v0, v1)):
            own = (lane < half) if head == 0 else (lane >= half)
            q_head = jnp.where(own, q, 0.0).astype(bf16)
            up_head = jnp.where(own, up, 0.0).astype(bf16)
            seen = jnp.where(own, up, mix).astype(bf16)
            e = jnp.exp2(nt(k, q_head) * log_scale + bias[0:keys, queries])
            ds = (e * nt(values[group, 0:keys, :], seen)).astype(bf16)
            dv_sum = dv_sum + nn(e.astype(bf16), up_head)
            dk_sum = dk_sum + nn(ds, q_head)
            piece = nn(k_t, ds)
            target = pl.ds(pl.multiple_of(start + head * half, half), half)
            if fresh:
                dq_t[target, queries] = piece
            else:
                dq_t[target, queries] += piece
        dk[group, 0:keys, :] = dk_sum
        dv[group, 0:keys, :] = dv_sum
        return carry

    lax.fori_loop(0, pairs, body, 0)


def fold_pairs(sums):
    lane = lane_of(sums.shape[1:])
    first = sums[0]
    second = sums[1]
    return jnp.where(lane < half, first + swap_halves(first), second + swap_halves(second))


def transposed_keys(kv, kt):
    key = kv[:, 0:lanes].astype(f32).T
    kt[0] = key[0:half].astype(bf16)
    kt[1] = key[half:].astype(bf16)


def far_kernel(
    meta, cot, summed, att, wide, inv, narrow, qrot, kv, segq, w0, w1, w2, w3, ao, bo,
    dop, mixed, dq_t, dkv, part_pack, full_pack,
    up, a_all, b_all, kd, v0, v1, kt, bias, dk, dv, *, log_scale, block,
):
    length = cot.shape[0]
    a_all[...] = jnp.zeros_like(a_all)
    b_all[...] = jnp.zeros_like(b_all)
    a_all[0:rank, :] = ao[0]
    b_all[0:rank, :] = bo[0]

    def body(index, carry):
        part_sum, full_sum = carry
        rows = pl.ds(pl.multiple_of(index * block, block), block)
        up[rows, :] = (cot[rows, :].astype(f32) + summed[rows, :].astype(f32)).astype(bf16)
        low = nt(up[rows, :], b_all[...])
        grad = nn(low.astype(bf16), a_all[...])
        for number, weight in enumerate((w0, w1, w2, w3)):
            columns = pl.ds(at(meta, number), weight.shape[1])
            grad = grad + nt(up[rows, columns], weight[...])
        scaled = (grad.astype(bf16).astype(f32) * inv[rows, :]).astype(bf16)
        dop[rows, :] = scaled
        inner = scaled.astype(f32) * wide[rows, :]
        for start in range(0, inner.shape[1], lanes):
            mixed[rows, start : start + lanes] = (
                -swap_halves(inner[:, start : start + lanes])
            ).astype(bf16)
        part_sum = part_sum + nn(low.T[0:rank].astype(bf16), att[rows, :])
        full_sum = full_sum + nn(narrow[rows, :].astype(f32).T[0:rank].astype(bf16), up[rows, :])
        return part_sum, full_sum

    part_sum, full_sum = lax.fori_loop(
        0,
        length // block,
        body,
        (jnp.zeros((rank, att.shape[1]), f32), jnp.zeros((rank, cot.shape[1]), f32)),
    )
    part_pack[...] = part_sum.astype(bf16)
    full_pack[...] = full_sum.astype(bf16)
    spread_keys(kv, kd, v0, v1, 0, length)
    transposed_keys(kv, kt)
    segk = jnp.where(meta[5] > 0, kv[:, 2 * lanes :].astype(f32)[:, 0:1], -1.0)
    bias[...] = jnp.where(segk == segq[...].astype(f32), 0.0, masked)
    dk[...] = jnp.zeros_like(dk)
    dv[...] = jnp.zeros_like(dv)
    for start in range(0, length, block):
        attention_back(
            qrot, dop, mixed, kd, v0, v1, kt, bias, dq_t, dk, dv, start, block, length, log_scale, True
        )
    dkv[:, 0:lanes] = (fold_pairs(dk[...]) * (half**-0.5)).astype(bf16)
    dkv[:, lanes:] = fold_pairs(dv[...]).astype(bf16)


def near_kernel(
    meta, dop, mixed, qrot, kv, segq, dq_far,
    dq_t, dkv, kd, v0, v1, kt, bias, dk, dv, *, log_scale, block,
):
    length = qrot.shape[0]
    spread_keys(kv, kd, v0, v1, 0, length)
    transposed_keys(kv, kt)
    key = lax.broadcasted_iota(jnp.int32, (length, length), 0)
    query = lax.broadcasted_iota(jnp.int32, (length, length), 1)
    segk = kv[:, 2 * lanes :].astype(f32)[:, 0:1]
    bias[...] = jnp.where((segk == segq[...].astype(f32)) & (key <= query), 0.0, masked)
    dk[...] = jnp.zeros_like(dk)
    dv[...] = jnp.zeros_like(dv)
    dq_t[...] = dq_far[...]
    for start in range(0, length, block):
        attention_back(
            qrot, dop, mixed, kd, v0, v1, kt, bias, dq_t, dk, dv, start, block, start + block,
            log_scale, False,
        )
    dkv[:, 0:lanes] = fold_pairs(dk[...]) * (half**-0.5)
    dkv[:, lanes:] = fold_pairs(dv[...])


def back_scratch(length):
    return [
        pltpu.VMEM((2, length, lanes), bf16),
        pltpu.VMEM((2, length, lanes), bf16),
        pltpu.VMEM((2, length, lanes), bf16),
        pltpu.VMEM((2, half, length), bf16),
        pltpu.VMEM((length, length), f32),
        pltpu.VMEM((2, length, lanes), f32),
        pltpu.VMEM((2, length, lanes), f32),
    ]


def attention_backward_far(
    meta, cot, summed, att, wide, inv, narrow, qrot, kv, segq, weights, down, lift, log_scale
):
    length, model = cot.shape
    q_width = qrot.shape[1]
    pick = lambda a: pl.BlockSpec(
        (1,) + a.shape[1:], lambda i, m: (m[7], 0, 0), pipeline_mode=pl.Buffered(1)
    )
    plain = (cot, summed, att, wide, inv, narrow, qrot, kv, segq, *weights)
    shapes = [
        result((length, q_width), bf16),
        result((length, q_width), bf16),
        result((q_width, length), f32),
        result((length, 2 * lanes), bf16),
        result((rank, q_width), bf16),
        result((rank, model), bf16),
    ]
    return pl.pallas_call(
        partial(far_kernel, log_scale=log_scale, block=256),
        name="attention_backward_far",
        grid_spec=pltpu.PrefetchScalarGridSpec(
            num_scalar_prefetch=1,
            grid=(1,),
            in_specs=[fixed(a.shape) for a in plain] + [pick(down), pick(lift)],
            out_specs=[fixed(s.shape) for s in shapes],
            scratch_shapes=[
                pltpu.VMEM((length, model), bf16),
                pltpu.VMEM((lanes, q_width), bf16),
                pltpu.VMEM((lanes, model), bf16),
            ]
            + back_scratch(length),
        ),
        out_shape=shapes,
        cost_estimate=pl.CostEstimate(
            flops=20 * length * length * q_width, transcendentals=length * length * 8,
            bytes_accessed=16 * 1024 * 1024,
        ),
        compiler_params=pltpu.CompilerParams(vmem_limit_bytes=vmem_bytes),
    )(meta, *plain, down, lift)


def attention_backward_near(meta, dop, mixed, qrot, kv, segq, dq_far, log_scale):
    length, q_width = qrot.shape
    plain = (dop, mixed, qrot, kv, segq, dq_far)
    shapes = [result((q_width, length), f32), result((length, 2 * lanes), f32)]
    return pl.pallas_call(
        partial(near_kernel, log_scale=log_scale, block=256),
        name="attention_backward_near",
        grid_spec=pltpu.PrefetchScalarGridSpec(
            num_scalar_prefetch=1,
            grid=(1,),
            in_specs=[fixed(a.shape) for a in plain],
            out_specs=[fixed(s.shape) for s in shapes],
            scratch_shapes=back_scratch(length),
        ),
        out_shape=shapes,
        cost_estimate=pl.CostEstimate(
            flops=20 * length * length * q_width, transcendentals=length * length * 8,
            bytes_accessed=6 * 1024 * 1024,
        ),
        compiler_params=pltpu.CompilerParams(vmem_limit_bytes=vmem_bytes),
    )(meta, *plain)


def qkv_grad_kernel(
    meta, normed, narrow, pre, dq_t, dkv_near, dkv_back, bq, bk, bv, qg, kg, cos, sin,
    grad, low_out, down_pack, q_lift, kv_lift, b_all, down_sum, lift_sum,
):
    q_width, kv_width = bq.shape[2], bk.shape[2]
    step = pl.program_id(0)

    @pl.when(step == 0)
    def _():
        b_all[...] = jnp.zeros_like(b_all)
        b_all[0:rank, 0:q_width] = bq[0]
        b_all[rank : 2 * rank, q_width : q_width + kv_width] = bk[0]
        b_all[2 * rank : 3 * rank, q_width + kv_width :] = bv[0]
        down_sum[...] = jnp.zeros_like(down_sum)
        lift_sum[...] = jnp.zeros_like(lift_sum)

    matrix = head_mean_matrix()
    dkv = dkv_near[...] + dkv_back[...].astype(f32)
    for start in range(0, q_width + kv_width, lanes):
        if start < q_width:
            upstream = dq_t[start : start + lanes, :].T * (half**-0.5)
        else:
            upstream = dkv[:, start - q_width : start - q_width + lanes]
        upstream = upstream * cos[...] - partner(upstream) * sin[...]
        value = pre[:, start : start + lanes]
        inverse = lax.rsqrt(head_mean(value * value, matrix) + epsilon)
        weighted = upstream * (qg if start < q_width else kg)[...]
        mean = head_mean(weighted * value, matrix)
        grad[:, start : start + lanes] = (
            inverse * weighted - value * (inverse * inverse * inverse * mean)
        ).astype(bf16)
    grad[:, q_width + kv_width :] = dkv[:, kv_width:].astype(bf16)
    own = grad[...]
    low = nt(own, b_all[...])
    low_out[...] = low.astype(bf16)
    down_sum[...] += nn(low.T[0 : 3 * rank].astype(bf16), normed[...])
    lift_sum[...] += nn(narrow[...].astype(f32).T[0 : 3 * rank].astype(bf16), own)

    @pl.when(step == pl.num_programs(0) - 1)
    def _():
        down_pack[...] = down_sum[...].astype(bf16)
        q_lift[...] = lift_sum[0:rank, 0:q_width].astype(bf16)
        kv_lift[:, 0:kv_width] = lift_sum[rank : 2 * rank, q_width : q_width + kv_width].astype(bf16)
        kv_lift[:, kv_width:] = lift_sum[2 * rank :, q_width + kv_width :].astype(bf16)


def qkv_grads(
    meta, normed, narrow, pre, dq_t, dkv_near, dkv_back, lifts, q_gain, k_gain, cos, sin
):
    length, width = normed.shape
    q_width, kv_width = lifts[0].shape[2], lifts[1].shape[2]
    every = q_width + 2 * kv_width
    block = 256
    tile = lambda w: pl.BlockSpec((block, w), lambda i, m: (i, 0))
    return pl.pallas_call(
        qkv_grad_kernel,
        name="qkv_grads",
        grid_spec=pltpu.PrefetchScalarGridSpec(
            num_scalar_prefetch=1,
            grid=(length // block,),
            in_specs=[
                tile(width), tile(lanes), tile(q_width + kv_width),
                pl.BlockSpec((q_width, block), lambda i, m: (0, i)), tile(2 * kv_width),
                tile(2 * kv_width),
            ]
            + [picked(a) for a in lifts]
            + [fixed(q_gain.shape), fixed(k_gain.shape), tile(lanes), tile(lanes)],
            out_specs=[
                tile(every), tile(lanes), fixed((3 * rank, width)), fixed((rank, q_width)),
                fixed((rank, 2 * kv_width)),
            ],
            scratch_shapes=[
                pltpu.VMEM((lanes, every), bf16),
                pltpu.VMEM((3 * rank, width), f32),
                pltpu.VMEM((3 * rank, every), f32),
            ],
        ),
        out_shape=[
            result((length, every), bf16),
            result((length, lanes), bf16),
            result((3 * rank, width), bf16),
            result((rank, q_width), bf16),
            result((rank, 2 * kv_width), bf16),
        ],
        cost_estimate=pl.CostEstimate(
            flops=2 * length * width * every // 8, transcendentals=0, bytes_accessed=8 * 1024 * 1024
        ),
        compiler_params=params(),
    )(
        meta, normed, narrow, pre, dq_t, dkv_near, dkv_back, *lifts, q_gain, k_gain, cos, sin
    )


def qkv_back_kernel(
    meta, hid, gain, grad, low, q0, q1, q2, q3, kv0, kv1, kv2, kv3, aq, ak, av, back, a_all, total,
):
    @pl.when(pl.program_id(0) == 0)
    def _():
        a_all[...] = jnp.zeros_like(a_all)
        a_all[0:rank, :] = aq[0]
        a_all[rank : 2 * rank, :] = ak[0]
        a_all[2 * rank : 3 * rank, :] = av[0]

    q_width = q0.shape[1]
    q_own, kv_own = grad[:, :q_width], grad[:, q_width:]
    for index, (q_weight, kv_weight) in enumerate(((q0, kv0), (q1, kv1), (q2, kv2), (q3, kv3))):
        columns = pl.ds(at(meta, index), q_weight.shape[0])
        total[:, columns] = (
            nt(q_own, q_weight[...]) + nt(kv_own, kv_weight[...]) + nn(low[...], a_all[:, columns])
        )
    wide = hid[...].astype(f32)
    inverse = lax.rsqrt(jnp.mean(wide * wide, axis=-1, keepdims=True) + epsilon)
    weighted = total[...] * gain[...].astype(f32)
    mean = jnp.mean(weighted * wide, axis=-1, keepdims=True)
    back[...] = (inverse * weighted - wide * (inverse * inverse * inverse * mean)).astype(bf16)


def qkv_backward(meta, hid, gain, grad, low, weights, downs):
    length, width = hid.shape
    every = grad.shape[1]
    block = 256
    tile = lambda w: pl.BlockSpec((block, w), lambda i, m: (i, 0))
    return pl.pallas_call(
        qkv_back_kernel,
        name="qkv_backward",
        grid_spec=pltpu.PrefetchScalarGridSpec(
            num_scalar_prefetch=1,
            grid=(length // block,),
            in_specs=[tile(width), fixed(gain.shape), tile(every), tile(lanes)]
            + [fixed(w.shape) for w in weights]
            + [picked(a) for a in downs],
            out_specs=tile(width),
            scratch_shapes=[pltpu.VMEM((lanes, width), bf16), pltpu.VMEM((block, width), f32)],
        ),
        out_shape=result((length, width), bf16),
        cost_estimate=pl.CostEstimate(
            flops=2 * length * width * every, transcendentals=0, bytes_accessed=8 * 1024 * 1024
        ),
        compiler_params=params(),
    )(meta, hid, gain, grad, low, *weights, *downs)


def place_kernel(sets, *refs, pieces):
    inputs = refs[: len(refs) - len(pieces)]
    outputs = refs[len(inputs) :]
    slot = pl.program_id(0)
    for (source, row, column), out in zip(pieces, outputs):
        width = out.shape[2]
        total = jnp.zeros((rank, width), f32)
        for sequence in range(inputs[source].shape[0]):
            share = jnp.where(sets[sequence] == slot, 1.0, 0.0)
            piece = inputs[source][sequence, row : row + rank, column : column + width]
            total = total + piece.astype(f32) * share
        out[0] = total


def place_sets(sets, gathered, pieces, slots):
    shapes = [result((slots, rank, width), f32) for _, _, _, width in pieces]
    return pl.pallas_call(
        partial(place_kernel, pieces=[p[:3] for p in pieces]),
        name="place_sets",
        grid_spec=pltpu.PrefetchScalarGridSpec(
            num_scalar_prefetch=1,
            grid=(slots,),
            in_specs=[fixed(g.shape) for g in gathered],
            out_specs=[pl.BlockSpec((1,) + s.shape[1:], lambda i, m: (i, 0, 0)) for s in shapes],
        ),
        out_shape=shapes,
        cost_estimate=pl.CostEstimate(flops=0, transcendentals=0, bytes_accessed=8 * 1024 * 1024),
        compiler_params=params(),
    )(sets, *gathered)


def close_kernel(meta, first, second, reduced, out):
    out[...] = (
        first[...].astype(f32) + second[...].astype(f32) + reduced[...].astype(f32)
    ).astype(out.dtype)


def close(meta, first, second, reduced, dtype):
    length, width = reduced.shape
    columns = pl.BlockSpec((length, width), lambda i, m: (0, m[4]))
    return pl.pallas_call(
        close_kernel,
        name="close",
        grid_spec=pltpu.PrefetchScalarGridSpec(
            num_scalar_prefetch=1,
            grid=(1,),
            in_specs=[columns, columns, fixed(reduced.shape)],
            out_specs=fixed(reduced.shape),
        ),
        out_shape=result(reduced.shape, dtype),
        cost_estimate=pl.CostEstimate(flops=0, transcendentals=0, bytes_accessed=4 * 1024 * 1024),
        compiler_params=params(),
    )(meta, first, second, reduced)


def flip(array, axis, bit):
    count = lax.axis_size(axis)
    return lax.ppermute(array, axis, [(i, i ^ bit) for i in range(count)])


def quarters(weight, axis):
    full = lax.all_gather(weight, "fsdp", axis=axis, tiled=True)
    return jnp.split(full, 4, axis=axis)


def after(array, *others):
    return lax.optimization_barrier((array, *others))[0]


def own_half(weight, axis):
    size = weight.shape[axis] // 2
    return lax.dynamic_slice_in_dim(weight, lax.axis_index("ctx") * size, size, axis)


def six_parts(weight, axis):
    shards = quarters(weight, axis)
    return shards[:2] + jnp.split(shards[2], 2, axis=axis) + jnp.split(shards[3], 2, axis=axis)


def shard_places(width, direct):
    unit = width // 4
    part = unit // 2
    if direct:
        four = [(lax.axis_index("fsdp") ^ bit) * unit for bit in range(4)]
        near = lax.axis_index("ctx") * part
    else:
        four, near = [0, unit, 2 * unit, 3 * unit], 0
    away = part - near
    return four, [four[0], four[1], four[2] + near, four[2] + away, four[3] + near, four[3] + away]


def pick_side(low, high, bit, axis):
    return jnp.where(
        bit == 0, jnp.concatenate([low, high], axis=axis), jnp.concatenate([high, low], axis=axis)
    )


def halve(array, axis, bit, stride):
    size = array.shape[-1] // 2
    keep = lax.dynamic_slice_in_dim(array, bit * size, size, array.ndim - 1)
    give = lax.dynamic_slice_in_dim(array, (1 - bit) * size, size, array.ndim - 1)
    taken = flip(give, axis, stride)
    return (keep.astype(f32) + taken.astype(f32)).astype(bf16)


def double(array, axis, bit, stride):
    taken = flip(array, axis, stride)
    return pick_side(array, taken, bit, array.ndim - 1)


def gather_sequences(full, part):
    fsdp = lax.axis_size("fsdp")
    if fsdp != 4 or lax.axis_size("ctx") != 2 or lax.axis_size("tp") != 4:
        full = lax.psum(full, ("ctx", "tp"))
        part = [lax.psum(p, "ctx") for p in part]
        return (
            lax.all_gather(full, "fsdp", axis=0),
            [lax.all_gather(p, "fsdp", axis=0) for p in part],
        )
    own, side, place = lax.axis_index("fsdp"), lax.axis_index("ctx"), lax.axis_index("tp")
    full = halve(full, "ctx", side, 1)
    part = [halve(p, "ctx", side, 1) for p in part]
    full = halve(full, "tp", place % 2, 1)
    full = halve(full, "tp", place // 2, 2)

    def both(array, bit, stride):
        taken = flip(array, "fsdp", stride)
        return pick_side(array, taken, bit, 0)

    full = both(full[None], own // 2, 2)
    part = [both(p[None], own // 2, 2) for p in part]
    full = double(full, "tp", place // 2, 2)
    full = double(full, "tp", place % 2, 1)
    full = double(full, "ctx", side, 1)
    part = [double(p, "ctx", side, 1) for p in part]

    def cores(array):
        taken = flip(array, "fsdp", 1)
        even = own % 2 == 0
        pairs = [jnp.where(even, array[i], taken[i]) for i in range(2)]
        others = [jnp.where(even, taken[i], array[i]) for i in range(2)]
        return jnp.stack([pairs[0], others[0], pairs[1], others[1]])

    return cores(full), [cores(p) for p in part]


def gather_ids(ids):
    if lax.axis_size("fsdp") != 4:
        return lax.all_gather(ids, "fsdp", tiled=True)
    own = lax.axis_index("fsdp")
    two = pick_side(ids, flip(ids, "fsdp", 1), own % 2, 0)
    return pick_side(two, flip(two, "fsdp", 2), own // 2, 0)


def on_device(
    hidden_in, segment_ids, adapter_ids, attention_gain, query_gain, key_gain, feedforward_gain,
    query_weight, key_weight, value_weight, output_weight, gate_weight, linear_weight, reduce_weight,
    query_down, query_lift, key_down, key_lift, value_down, value_lift, output_down, output_lift,
    gate_down, gate_lift, linear_down, linear_lift, reduce_down, reduce_lift, output_cotangent,
):
    _, length, model = hidden_in.shape
    head_dim = query_gain.shape[0]
    log_scale = head_dim**-0.5 * 1.4426950408889634
    context_index = lax.axis_index("ctx")
    tensor_index = lax.axis_index("tp")
    hid = hidden_in[0]
    cot = output_cotangent[0]
    direct = lax.axis_size("fsdp") == 4 and lax.axis_size("ctx") == 2
    four, six = shard_places(model, direct)
    values = (*four, tensor_index, context_index, 0, adapter_ids[0], *six, 0, 0)
    meta = jnp.stack([jnp.asarray(value, jnp.int32) for value in values])

    positions = (context_index * length + jnp.arange(length)).astype(f32)
    frequency = rope_base ** (-2.0 * jnp.arange(head_dim // 2).astype(f32) / head_dim)
    angles = positions[:, None] * frequency[None, :]
    cosine, sine = jnp.cos(angles), jnp.sin(angles)
    cos = jnp.concatenate([cosine] * 4, axis=1)
    sin = jnp.concatenate([-sine, sine] * 2, axis=1)
    q_gain = jnp.tile(query_gain.astype(f32), 2)[None]
    k_gain = jnp.tile(key_gain.astype(f32), 2)[None]
    a_gain = attention_gain[None]
    f_gain = feedforward_gain[None]
    seg_own = segment_ids.reshape(length, 1)
    count = lax.axis_size("ctx")
    onward = [(i, i + 1) for i in range(count - 1)]
    backward = [(i + 1, i) for i in range(count - 1)]
    turn = lambda table: jnp.swapaxes(table, 1, 2)
    qkv_downs = [turn(query_down), turn(key_down), turn(value_down)]
    qkv_lifts = [query_lift, key_lift, value_lift]
    output_first = turn(output_down)
    reduce_first = turn(reduce_down)

    kv_own = jnp.concatenate([key_weight, value_weight], axis=1)
    if direct:
        q_across = flip(query_weight, "fsdp", 2)
        kv_across = flip(kv_own, "fsdp", 2)
        gate_half = own_half(gate_weight, 0)
        cores = [flip(w, "fsdp", 1) for w in (gate_weight, linear_weight, reduce_weight)]
        q_side = flip(after(query_weight, q_across), "fsdp", 1)
        kv_side = flip(after(kv_own, kv_across), "fsdp", 1)
        tables = (*cores, cos, sin, meta, q_gain, k_gain, a_gain, f_gain, seg_own, gate_half)
        qkv_weights = [
            query_weight, q_side, q_across,
            flip(after(q_across, *tables), "fsdp", 1),
            kv_own, kv_side, kv_across, flip(after(kv_across, *tables), "fsdp", 1),
        ]
        output_across = flip(after(output_weight, q_across, kv_across), "fsdp", 2)
        gate_across = flip(after(gate_half, q_across, kv_across), "fsdp", 2)
    else:
        qkv_weights = quarters(query_weight, 0) + quarters(kv_own, 0)
        output_weights = quarters(output_weight, 1)
        gates = six_parts(gate_weight, 0)
        linears = quarters(linear_weight, 0)
        reduces = quarters(reduce_weight, 1)

    normed, qkv_narrow, pre, qrot, kv = qkv_forward(
        meta, hid, a_gain, qkv_weights, qkv_downs, qkv_lifts, q_gain, k_gain, cos, sin, seg_own
    )
    kv_far = lax.ppermute(kv, "ctx", onward)
    ready = after(qrot, gate_across, output_across) if direct else qrot
    att, wide, inv = attention_forward(meta, ready, kv_far, kv, log_scale)
    if direct:
        gate_other = flip(after(gate_across, att), "ctx", 1)
        linear_across = flip(after(linear_weight, att), "fsdp", 2)
        reduce_across = flip(after(reduce_weight, att), "fsdp", 2)
        output_weights = [
            output_weight, flip(after(output_weight, kv_far), "fsdp", 1), output_across,
            flip(after(output_across, kv_far), "fsdp", 1),
        ]
    branch, output_narrow = output_forward(meta, att, output_weights, output_first, output_lift)
    if direct:
        gates = [
            gate_weight, cores[0], gate_across, gate_other, flip(after(gate_across, gate_other), "fsdp", 1),
            flip(gate_other, "fsdp", 1),
        ]
        linears = [linear_weight, cores[1], linear_across, flip(linear_across, "fsdp", 1)]
        reduces = [reduce_weight, cores[2], reduce_across, flip(reduce_across, "fsdp", 1)]
    branch = lax.psum(branch, "tp")

    back, inner, gate_grad, linear_grad, n_gl_t, m_gl_t, m_r_t = ffn(
        meta, hid, branch, cot, f_gain, gates, linears, reduces,
        [turn(gate_down), turn(linear_down), reduce_first], [gate_lift, linear_lift, reduce_lift],
    )
    summed = lax.psum(back, "tp")
    ffn_part, ffn_full, n_r = ffn_adapters(
        meta, hid, branch, cot, f_gain, inner, gate_grad, linear_grad, n_gl_t, m_gl_t, m_r_t,
        reduce_first,
    )
    sets = gather_ids(after(adapter_ids, inner))
    slots = query_down.shape[0]
    ffn_full, (ffn_part,) = gather_sequences(ffn_full, [ffn_part])
    hidden = gate_lift.shape[2]
    ffn_pieces = [(0, rank * i, 0, model) for i in range(3)] + [(1, rank * i, 0, hidden) for i in range(3)]
    ffn_grads = place_sets(sets, [ffn_full, ffn_part], ffn_pieces, slots)
    out = reduce_forward(meta, inner, n_r, reduces, reduce_lift)
    out_columns = lax.psum_scatter(out, "tp", scatter_dimension=1, tiled=True)
    block_out = close(meta, hid, branch, out_columns, bf16)

    dop, mixed, dq_far, dkv_far, output_part, output_full = attention_backward_far(
        meta, cot, summed, att, wide, inv, output_narrow, qrot, kv_far, segment_ids,
        output_weights, output_first, output_lift, log_scale,
    )
    dkv_back = lax.ppermute(dkv_far, "ctx", backward)
    dq_t, dkv_near = attention_backward_near(
        meta, dop, mixed, qrot, kv, segment_ids, dq_far, log_scale
    )
    grad, low, qkv_full, q_part, kv_part = qkv_grads(
        meta, normed, qkv_narrow, pre, dq_t, dkv_near, dkv_back, qkv_lifts, q_gain, k_gain, cos, sin
    )
    last = qkv_backward(meta, hid, a_gain, grad, low, qkv_weights, qkv_downs)
    last_columns = lax.psum_scatter(last, "tp", scatter_dimension=1, tiled=True)
    input_grad = close(meta, cot, summed, last_columns, f32)

    q_width, kv_width = query_lift.shape[2], key_lift.shape[2]
    att_full, (att_part,) = gather_sequences(
        jnp.concatenate([qkv_full, output_full], axis=0),
        [jnp.concatenate([q_part, kv_part, output_part], axis=1)],
    )

    att_pieces = [(0, rank * i, 0, model) for i in range(4)] + [
        (1, 0, 0, q_width),
        (1, 0, q_width, kv_width),
        (1, 0, q_width + kv_width, kv_width),
        (1, 0, q_width + 2 * kv_width, q_width),
    ]
    att_grads = place_sets(sets, [att_full, att_part], att_pieces, slots)
    return (
        block_out[None],
        input_grad[None],
        turn(att_grads[0]),
        att_grads[4],
        turn(att_grads[1]),
        att_grads[5],
        turn(att_grads[2]),
        att_grads[6],
        turn(att_grads[7]),
        att_grads[3],
        turn(ffn_grads[0]),
        ffn_grads[3],
        turn(ffn_grads[1]),
        ffn_grads[4],
        turn(ffn_grads[5]),
        ffn_grads[2],
    )


def solution(mesh):
    tokens = P("fsdp", "ctx", None)
    rows_split = P("fsdp", "tp")
    lift_split = P(None, None, "tp")
    down_split = P(None, "tp", None)
    in_specs = (
        tokens, P("fsdp", "ctx"), P("fsdp"), P(), P(), P(), P(),
        rows_split, rows_split, rows_split, P("tp", "fsdp"), rows_split, rows_split, P("tp", "fsdp"),
        P(), lift_split, P(), lift_split, P(), lift_split, down_split, P(),
        P(), lift_split, P(), lift_split, down_split, P(), tokens,
    )
    cut = P("fsdp", "ctx", "tp")
    out_specs = (
        cut, cut, P(), lift_split, P(), lift_split, P(), lift_split, down_split, P(),
        P(), lift_split, P(), lift_split, down_split, P(),
    )
    return jax.shard_map(
        on_device, mesh=mesh, in_specs=in_specs, out_specs=out_specs, check_vma=False
    )
```

```python
from functools import partial

import jax
import jax.numpy as jnp
from jax import lax
from jax.experimental import pallas as pl
from jax.experimental.pallas import tpu as pltpu
from jax.sharding import PartitionSpec as P

epsilon = 1e-05
rope_base = 1000000.0
masked = -1e30
f32 = jnp.float32
bf16 = jnp.bfloat16
lanes = 128
half = 64
rank = 16
vmem_bytes = 58 * 1024 * 1024


def nn(left, right):
    return lax.dot_general(left, right, (((1,), (0,)), ((), ())), preferred_element_type=f32)


def nt(left, right):
    return lax.dot_general(left, right, (((1,), (1,)), ((), ())), preferred_element_type=f32)


def at(ref, index):
    return pl.multiple_of(ref[index], lanes)


def fixed(shape):
    return pl.BlockSpec(shape, lambda *_: (0,) * len(shape), pipeline_mode=pl.Buffered(1))


def picked(array):
    return pl.BlockSpec(
        (1,) + array.shape[1:], lambda i, m: (m[7], 0, 0), pipeline_mode=pl.Buffered(1)
    )


def params():
    return pltpu.CompilerParams(vmem_limit_bytes=vmem_bytes)


def result(shape, dtype):
    return jax.ShapeDtypeStruct(shape, dtype)


def lane_of(shape):
    return lax.broadcasted_iota(jnp.int32, shape, len(shape) - 1)


def head_mean_matrix():
    row = lax.broadcasted_iota(jnp.int32, (lanes, lanes), 0)
    col = lax.broadcasted_iota(jnp.int32, (lanes, lanes), 1)
    return jnp.where((row // half) == (col // half), 1.0 / half, 0.0).astype(bf16)


def head_mean(values, matrix):
    high = values.astype(bf16)
    low = (values - high.astype(f32)).astype(bf16)
    return nn(high, matrix) + nn(low, matrix)


def partner(values):
    first = (lane_of(values.shape) % half) < (half // 2)
    return jnp.where(
        first,
        pltpu.roll(values, lanes - half // 2, values.ndim - 1),
        pltpu.roll(values, half // 2, values.ndim - 1),
    )


def swap_halves(values):
    return pltpu.roll(values, half, values.ndim - 1)


def norm_kernel(meta, hid, gain, aq, ak, av, normed, narrow, a_all):
    @pl.when(pl.program_id(0) == 0)
    def _():
        a_all[...] = jnp.zeros_like(a_all)
        a_all[0:rank, :] = aq[0]
        a_all[rank : 2 * rank, :] = ak[0]
        a_all[2 * rank : 3 * rank, :] = av[0]

    wide = hid[...].astype(f32)
    inverse = lax.rsqrt(jnp.mean(wide * wide, axis=-1, keepdims=True) + epsilon)
    normed[...] = (wide * inverse * gain[...].astype(f32)).astype(bf16)
    narrow[...] = nt(normed[...], a_all[...]).astype(bf16)


def attention_norm(meta, hid, gain, downs):
    length, width = hid.shape
    block = 128
    tile = lambda w: pl.BlockSpec((block, w), lambda i, m: (i, 0))
    return pl.pallas_call(
        norm_kernel,
        name="attention_norm",
        grid_spec=pltpu.PrefetchScalarGridSpec(
            num_scalar_prefetch=1,
            grid=(length // block,),
            in_specs=[tile(width), fixed(gain.shape)] + [picked(a) for a in downs],
            out_specs=[tile(width), tile(lanes)],
            scratch_shapes=[pltpu.VMEM((lanes, width), bf16)],
        ),
        out_shape=[result((length, width), bf16), result((length, lanes), bf16)],
        cost_estimate=pl.CostEstimate(flops=1024, transcendentals=0, bytes_accessed=1024),
        compiler_params=params(),
    )(meta, hid, gain, *downs)


def qkv_kernel(
    meta, normed, narrow, q0, q1, q2, q3, kv0, kv1, kv2, kv3, bq, bk, bv, qg, kg, cos, sin,
    seg, pre, qrot, kv, b_all,
):
    q_width, kv_width = bq.shape[2], bk.shape[2]

    @pl.when(pl.program_id(0) == 0)
    def _():
        b_all[...] = jnp.zeros_like(b_all)
        b_all[0:rank, 0:q_width] = bq[0]
        b_all[rank : 2 * rank, q_width : q_width + kv_width] = bk[0]
        b_all[2 * rank : 3 * rank, q_width + kv_width :] = bv[0]

    total = nn(narrow[...], b_all[...])
    q_total, kv_total = total[:, :q_width], total[:, q_width:]
    for index, (q_weight, kv_weight) in enumerate(((q0, kv0), (q1, kv1), (q2, kv2), (q3, kv3))):
        part = normed[:, pl.ds(at(meta, index), q_weight.shape[0])]
        q_total = q_total + nn(part, q_weight[...])
        kv_total = kv_total + nn(part, kv_weight[...])
    total = jnp.concatenate([q_total, kv_total], axis=1)
    pre[...] = total[:, : q_width + kv_width]
    matrix = head_mean_matrix()
    for start in range(0, q_width + kv_width, lanes):
        part = total[:, start : start + lanes]
        head_gain = qg if start < q_width else kg
        scaled = part * lax.rsqrt(head_mean(part * part, matrix) + epsilon) * head_gain[...]
        turned = (scaled * cos[...] + partner(scaled) * sin[...]).astype(bf16)
        if start < q_width:
            qrot[:, start : start + lanes] = turned
        else:
            kv[:, start - q_width : start - q_width + lanes] = turned
    kv[:, kv_width : 2 * kv_width] = total[:, q_width + kv_width :].astype(bf16)
    kv[:, 2 * kv_width :] = jnp.broadcast_to(seg[...].astype(f32), (seg.shape[0], lanes)).astype(bf16)


def qkv_forward(meta, normed, narrow, weights, lifts, q_gain, k_gain, cos, sin, seg):
    length, width = normed.shape
    q_width, kv_width = lifts[0].shape[2], lifts[1].shape[2]
    block = 256
    tile = lambda w: pl.BlockSpec((block, w), lambda i, m: (i, 0))
    return pl.pallas_call(
        qkv_kernel,
        name="qkv_forward",
        grid_spec=pltpu.PrefetchScalarGridSpec(
            num_scalar_prefetch=1,
            grid=(length // block,),
            in_specs=[tile(width), tile(lanes)]
            + [fixed(w.shape) for w in weights]
            + [picked(a) for a in lifts]
            + [fixed(q_gain.shape), fixed(k_gain.shape), tile(lanes), tile(lanes), tile(1)],
            out_specs=[tile(q_width + kv_width), tile(q_width), tile(2 * kv_width + lanes)],
            scratch_shapes=[pltpu.VMEM((lanes, q_width + 2 * kv_width), bf16)],
        ),
        out_shape=[
            result((length, q_width + kv_width), f32),
            result((length, q_width), bf16),
            result((length, 2 * kv_width + lanes), bf16),
        ],
        cost_estimate=pl.CostEstimate(flops=1024, transcendentals=0, bytes_accessed=1024),
        compiler_params=params(),
    )(meta, normed, narrow, *weights, *lifts, q_gain, k_gain, cos, sin, seg)


def spread_keys(kv, kd, v0, v1, rows, size):
    lane = lane_of((size, lanes))
    key = kv[:, 0:lanes].astype(f32)
    other = swap_halves(key)
    kd[0, rows : rows + size, :] = jnp.where(lane < half, key, other).astype(bf16)
    kd[1, rows : rows + size, :] = jnp.where(lane < half, other, key).astype(bf16)
    value = kv[:, lanes : 2 * lanes].astype(f32)
    other = swap_halves(value)
    v0[0, rows : rows + size, :] = jnp.where(lane < half, value, 1.0).astype(bf16)
    v0[1, rows : rows + size, :] = jnp.where(lane < half, other, 1.0).astype(bf16)
    v1[0, rows : rows + size, :] = jnp.where(lane < half, 1.0, other).astype(bf16)
    v1[1, rows : rows + size, :] = jnp.where(lane < half, 1.0, value).astype(bf16)


def attention_kernel(
    meta, qrot, kvf, kvn, kvq, att, wide, inv, kd, v0, v1, bias, segk, *, log_scale, block,
):
    far = kvf.shape[0]
    pairs = qrot.shape[1] // lanes
    share = pairs // 2
    step = pl.program_id(0)

    @pl.when(step == 0)
    def _():
        spread_keys(kvf, kd, v0, v1, 0, far)
        spread_keys(kvn, kd, v0, v1, far, kvn.shape[0])
        away = kvf[:, 2 * lanes :].astype(f32).T[0:8]
        segk[:, 0:far] = jnp.where(meta[5] > 0, away, -1.0)
        segk[:, far:] = kvn[:, 2 * lanes :].astype(f32).T[0:8]

    def queries(number):
        keys = far + (number + 1) * block
        key = lax.broadcasted_iota(jnp.int32, (block, keys), 1)
        query = lax.broadcasted_iota(jnp.int32, (block, keys), 0) + (far + number * block)
        segq = kvq[:, 2 * lanes :].astype(f32)[:, 0:1]
        allowed = (segq == segk[0:1, 0:keys]) & (key <= query)
        bias[:, 0:keys] = jnp.where(allowed, 0.0, masked)
        lane = lane_of((block, lanes))

        def body(pair, carry):
            group = pair // share
            place = pl.ds(pl.multiple_of(pair * lanes, lanes), lanes)
            q = qrot[:, place].astype(f32)
            q0 = jnp.where(lane < half, q, 0.0).astype(bf16)
            q1 = jnp.where(lane < half, 0.0, q).astype(bf16)
            k = kd[group, 0:keys, :]
            e0 = jnp.exp2(nt(q0, k) * log_scale + bias[:, 0:keys]).astype(bf16)
            r0 = nn(e0, v0[group, 0:keys, :])
            e1 = jnp.exp2(nt(q1, k) * log_scale + bias[:, 0:keys]).astype(bf16)
            r1 = nn(e1, v1[group, 0:keys, :])
            inverse = 1.0 / jnp.where(lane < half, swap_halves(r0), swap_halves(r1))
            out = jnp.where(lane < half, r0, r1) * inverse
            wide[:, place] = out
            inv[:, place] = inverse
            att[:, place] = out.astype(bf16)
            return carry

        lax.fori_loop(0, pairs, body, 0)

    for number in range(kvn.shape[0] // block):
        pl.when(step == number)(partial(queries, number))


def attention_forward(meta, qrot, kvf, kvn, log_scale):
    length, q_width = qrot.shape
    block = 256
    keys = kvf.shape[0] + length
    tile = lambda w: pl.BlockSpec((block, w), lambda i, m: (i, 0))
    return pl.pallas_call(
        partial(attention_kernel, log_scale=log_scale, block=block),
        name="attention_forward",
        grid_spec=pltpu.PrefetchScalarGridSpec(
            num_scalar_prefetch=1,
            grid=(length // block,),
            in_specs=[tile(q_width), fixed(kvf.shape), fixed(kvn.shape), tile(kvn.shape[1])],
            out_specs=[tile(q_width), tile(q_width), tile(q_width)],
            scratch_shapes=[
                pltpu.VMEM((2, keys, lanes), bf16),
                pltpu.VMEM((2, keys, lanes), bf16),
                pltpu.VMEM((2, keys, lanes), bf16),
                pltpu.VMEM((block, keys), f32),
                pltpu.VMEM((8, keys), f32),
            ],
        ),
        out_shape=[
            result((length, q_width), bf16),
            result((length, q_width), f32),
            result((length, q_width), f32),
        ],
        cost_estimate=pl.CostEstimate(
            flops=64 * length * keys * q_width, transcendentals=length * keys * 8,
            bytes_accessed=64 * 1024 * 1024,
        ),
        compiler_params=pltpu.CompilerParams(vmem_limit_bytes=vmem_bytes),
    )(meta, qrot, kvf, kvn, kvn)


def output_kernel(meta, att, w0, w1, w2, w3, ao, bo, branch, narrow, a_all, b_all):
    @pl.when(pl.program_id(0) == 0)
    def _():
        a_all[...] = jnp.zeros_like(a_all)
        b_all[...] = jnp.zeros_like(b_all)
        a_all[0:rank, :] = ao[0]
        b_all[0:rank, :] = bo[0]

    own = att[...]
    low = nt(own, a_all[...]).astype(bf16)
    narrow[...] = low
    for index, weight in enumerate((w0, w1, w2, w3)):
        columns = pl.ds(at(meta, index), weight.shape[1])
        branch[:, columns] = (nn(own, weight[...]) + nn(low, b_all[:, columns])).astype(bf16)


def output_forward(meta, att, weights, down, lift):
    length, q_width = att.shape
    model = lift.shape[2]
    block = 256
    tile = lambda w: pl.BlockSpec((block, w), lambda i, m: (i, 0))
    pick = lambda a: pl.BlockSpec(
        (1,) + a.shape[1:], lambda i, m: (m[7], 0, 0), pipeline_mode=pl.Buffered(1)
    )
    return pl.pallas_call(
        output_kernel,
        name="output_forward",
        grid_spec=pltpu.PrefetchScalarGridSpec(
            num_scalar_prefetch=1,
            grid=(length // block,),
            in_specs=[tile(q_width)] + [fixed(w.shape) for w in weights] + [pick(down), pick(lift)],
            out_specs=[tile(model), tile(lanes)],
            scratch_shapes=[pltpu.VMEM((lanes, q_width), bf16), pltpu.VMEM((lanes, model), bf16)],
        ),
        out_shape=[result((length, model), bf16), result((length, lanes), bf16)],
        cost_estimate=pl.CostEstimate(flops=1024, transcendentals=0, bytes_accessed=1024),
        compiler_params=pltpu.CompilerParams(vmem_limit_bytes=vmem_bytes),
    )(meta, att, *weights, down, lift)


def strip(array, width):
    return pl.BlockSpec((1, rank, width), lambda j, m: (m[7], 0, j))


def ffn_kernel(meta, hid, branch, cot, gain, *refs, shards, chunk):
    gates, linears, reduces = (refs[i:j] for i, j in zip((0,) + shards[:-1], shards))
    refs = refs[shards[-1] :]
    ag, al, ar, bg, bl, br = refs[:6]
    back, inner_out, gate_out, linear_out, n_gl_t, m_gl_t, m_r_t = refs[6:13]
    x, grad_sum, n_gl, m_gl, m_r, a_gl, b_r, b_g, b_l, a_r = refs[13:]
    step = pl.program_id(0)
    length = hid.shape[0]
    count = length // chunk

    def rows_of(index):
        return pl.ds(pl.multiple_of(index * chunk, chunk), chunk)

    def chunks(body):
        def run(index, carry):
            body(rows_of(index))
            return carry

        lax.fori_loop(0, count, run, 0)

    def normal(rows):
        middle = hid[rows, :].astype(f32) + branch[rows, :].astype(f32)
        inverse = lax.rsqrt(jnp.mean(middle * middle, axis=-1, keepdims=True) + epsilon)
        return middle, inverse

    @pl.when(step == 0)
    def _():
        for ref in (a_gl, b_r, b_g, b_l, a_r):
            ref[...] = jnp.zeros_like(ref)
        a_gl[0:rank, :] = ag[0]
        a_gl[rank : 2 * rank, :] = al[0]
        b_r[0:rank, :] = br[0]

        def body(rows):
            back_low = nt(cot[rows, :], b_r[...])
            m_r[rows, :] = back_low.astype(bf16)
            m_r_t[:, rows] = back_low.T[0:rank].astype(bf16)
            middle, inverse = normal(rows)
            x[rows, :] = (middle * inverse * gain[...].astype(f32)).astype(bf16)
            low = nt(x[rows, :], a_gl[...])
            n_gl[rows, :] = low.astype(bf16)
            n_gl_t[:, rows] = low.T[0 : 2 * rank].astype(bf16)
            m_gl[rows, :] = jnp.zeros((chunk, lanes), f32)

        chunks(body)

    b_g[0:rank, :] = bg[0]
    b_l[rank : 2 * rank, :] = bl[0]
    a_r[0:rank, :] = ar[0]

    def place(index, weight, axis):
        return pl.ds(at(meta, index), weight.shape[axis])

    def body(rows, first):
        low = n_gl[rows, :]
        gate = nn(low, b_g[...])
        linear = nn(low, b_l[...])
        for index, weight in enumerate(gates):
            gate = gate + nn(x[rows, place(8 + index, weight, 0)], weight[...])
        for index, weight in enumerate(linears):
            linear = linear + nn(x[rows, place(index, weight, 0)], weight[...])
        upstream = nn(m_r[rows, :], a_r[...])
        for index, weight in enumerate(reduces):
            upstream = upstream + nt(cot[rows, place(index, weight, 1)], weight[...])
        sigmoid = jax.nn.sigmoid(gate)
        active = gate * sigmoid
        gate_grad = (upstream * linear * sigmoid * (1.0 + gate * (1.0 - sigmoid))).astype(bf16)
        linear_grad = (upstream * active).astype(bf16)
        inner_out[rows, :] = (active * linear).astype(bf16)
        gate_out[rows, :] = gate_grad
        linear_out[rows, :] = linear_grad
        m_gl[rows, :] += nt(gate_grad, b_g[...]) + nt(linear_grad, b_l[...])
        for index, weight in enumerate(linears):
            columns = place(index, weight, 0)
            backward = nt(linear_grad, weight[...])
            if first:
                grad_sum[rows, columns] = backward
            else:
                grad_sum[rows, columns] += backward
        for index, weight in enumerate(gates):
            grad_sum[rows, place(8 + index, weight, 0)] += nt(gate_grad, weight[...])

    pl.when(step == 0)(partial(chunks, partial(body, first=True)))
    pl.when(step > 0)(partial(chunks, partial(body, first=False)))

    @pl.when(step == pl.num_programs(0) - 1)
    def _():
        def finish(rows):
            upstream = grad_sum[rows, :] + nn(m_gl[rows, :].astype(bf16), a_gl[...])
            middle, inverse = normal(rows)
            weighted = upstream * gain[...].astype(f32)
            mean = jnp.mean(weighted * middle, axis=-1, keepdims=True)
            back[rows, :] = (
                inverse * weighted - middle * (inverse * inverse * inverse * mean)
            ).astype(bf16)

        chunks(finish)
        m_gl_t[...] = m_gl[...].T[0 : 2 * rank].astype(bf16)


def ffn(
    meta, hid, branch, cot, gain, gates, linears, reduces, downs, lifts, width=512, chunk=512
):
    length, model = hid.shape
    hidden = gates[0].shape[1]
    rows = [*gates, *linears]
    shards = (len(gates), len(rows), len(rows) + len(reduces))
    column = lambda: pl.BlockSpec((length, width), lambda j, m: (0, j))
    return pl.pallas_call(
        partial(ffn_kernel, shards=shards, chunk=chunk),
        name="feed_forward",
        grid_spec=pltpu.PrefetchScalarGridSpec(
            num_scalar_prefetch=1,
            grid=(hidden // width,),
            in_specs=[fixed(hid.shape), fixed(branch.shape), fixed(cot.shape), fixed(gain.shape)]
            + [pl.BlockSpec((w.shape[0], width), lambda j, m: (0, j)) for w in rows]
            + [pl.BlockSpec((width, w.shape[1]), lambda j, m: (j, 0)) for w in reduces]
            + [picked(downs[0]), picked(downs[1]), strip(downs[2], width)]
            + [strip(lifts[0], width), strip(lifts[1], width), picked(lifts[2])],
            out_specs=[
                fixed((length, model)), column(), column(), column(),
                fixed((2 * rank, length)), fixed((2 * rank, length)), fixed((rank, length)),
            ],
            scratch_shapes=[
                pltpu.VMEM((length, model), bf16),
                pltpu.VMEM((length, model), f32),
                pltpu.VMEM((length, lanes), bf16),
                pltpu.VMEM((length, lanes), f32),
                pltpu.VMEM((length, lanes), bf16),
                pltpu.VMEM((lanes, model), bf16),
                pltpu.VMEM((lanes, model), bf16),
                pltpu.VMEM((lanes, width), bf16),
                pltpu.VMEM((lanes, width), bf16),
                pltpu.VMEM((lanes, width), bf16),
            ],
        ),
        out_shape=[result((length, model), bf16)]
        + [result((length, hidden), bf16)] * 3
        + [result((2 * rank, length), bf16)] * 2
        + [result((rank, length), bf16)],
        cost_estimate=pl.CostEstimate(
            flops=8 * length * model * hidden, transcendentals=length * hidden,
            bytes_accessed=4 * model * hidden + 14 * length * model,
        ),
        compiler_params=params(),
    )(meta, hid, branch, cot, gain, *rows, *reduces, *downs, *lifts)


def ffn_adapter_kernel(
    meta, hid, branch, cot, gain, inner, gate_grad, linear_grad, n_gl_t, m_gl_t, m_r_t, ar,
    part_pack, full_pack, n_r, low_sum, a_r,
):
    step = pl.program_id(0)

    @pl.when(step == 0)
    def _():
        a_r[...] = jnp.zeros_like(a_r)
        low_sum[...] = jnp.zeros_like(low_sum)

    a_r[0:rank, :] = ar[0]
    part_pack[0:rank, :] = nn(n_gl_t[...], gate_grad[...])[0:rank].astype(bf16)
    part_pack[rank : 2 * rank, :] = nn(n_gl_t[...], linear_grad[...])[rank:].astype(bf16)
    part_pack[2 * rank :, :] = nn(m_r_t[...], inner[...]).astype(bf16)
    low_sum[...] += nt(inner[...], a_r[...])

    @pl.when(step == pl.num_programs(0) - 1)
    def _():
        low = low_sum[...]
        n_r[...] = low.astype(bf16)
        full_pack[2 * rank :, :] = nn(low.T[0:rank].astype(bf16), cot[...]).astype(bf16)
        middle = hid[...].astype(f32) + branch[...].astype(f32)
        inverse = lax.rsqrt(jnp.mean(middle * middle, axis=-1, keepdims=True) + epsilon)
        x = (middle * inverse * gain[...].astype(f32)).astype(bf16)
        full_pack[0 : 2 * rank, :] = nn(m_gl_t[...], x).astype(bf16)


def ffn_adapters(meta, hid, branch, cot, gain, inner, gate_grad, linear_grad, n_gl_t, m_gl_t, m_r_t, down):
    length, model = hid.shape
    hidden = inner.shape[1]
    width = 512
    column = lambda: pl.BlockSpec((length, width), lambda j, m: (0, j))
    return pl.pallas_call(
        ffn_adapter_kernel,
        name="feed_forward_adapters",
        grid_spec=pltpu.PrefetchScalarGridSpec(
            num_scalar_prefetch=1,
            grid=(hidden // width,),
            in_specs=[fixed(hid.shape), fixed(branch.shape), fixed(cot.shape), fixed(gain.shape)]
            + [column(), column(), column()]
            + [fixed(n_gl_t.shape), fixed(m_gl_t.shape), fixed(m_r_t.shape), strip(down, width)],
            out_specs=[
                pl.BlockSpec((3 * rank, width), lambda j, m: (0, j)),
                fixed((3 * rank, model)),
                fixed((length, lanes)),
            ],
            scratch_shapes=[pltpu.VMEM((length, lanes), f32), pltpu.VMEM((lanes, width), bf16)],
        ),
        out_shape=[
            result((3 * rank, hidden), bf16),
            result((3 * rank, model), bf16),
            result((length, lanes), bf16),
        ],
        cost_estimate=pl.CostEstimate(
            flops=512 * length * hidden, transcendentals=0, bytes_accessed=12 * length * model
        ),
        compiler_params=params(),
    )(meta, hid, branch, cot, gain, inner, gate_grad, linear_grad, n_gl_t, m_gl_t, m_r_t, down)


def reduce_kernel(meta, inner, n_r, *refs):
    *weights, br, out, b_r = refs
    b_r[...] = jnp.zeros_like(b_r)
    b_r[0:rank, :] = br[0]
    for index, weight in enumerate(weights):
        columns = pl.ds(at(meta, index), weight.shape[1])
        out[:, columns] = (nn(inner[...], weight[...]) + nn(n_r[...], b_r[:, columns])).astype(bf16)


def reduce_forward(meta, inner, n_r, reduces, lift):
    length = inner.shape[0]
    model = lift.shape[2]
    return pl.pallas_call(
        reduce_kernel,
        name="reduce_forward",
        grid_spec=pltpu.PrefetchScalarGridSpec(
            num_scalar_prefetch=1,
            grid=(1,),
            in_specs=[fixed(inner.shape), fixed(n_r.shape)]
            + [fixed(w.shape) for w in reduces]
            + [picked(lift)],
            out_specs=fixed((length, model)),
            scratch_shapes=[pltpu.VMEM((lanes, model), bf16)],
        ),
        out_shape=result((length, model), bf16),
        cost_estimate=pl.CostEstimate(
            flops=2 * length * model * inner.shape[1], transcendentals=0,
            bytes_accessed=12 * 1024 * 1024,
        ),
        compiler_params=params(),
    )(meta, inner, n_r, *reduces, lift)


def attention_back(
    qrot, dop, mixed, kd, v0, v1, kt, bias, dq_t, dk, dv, rows, block, keys, log_scale, fresh,
):
    pairs = qrot.shape[1] // lanes
    share = pairs // 2
    lane = lane_of((block, lanes))
    queries = pl.ds(rows, block)

    def body(pair, carry):
        group = pair // share
        start = pl.multiple_of(pair * lanes, lanes)
        place = pl.ds(start, lanes)
        q = qrot[queries, place].astype(f32)
        up = dop[queries, place].astype(f32)
        mix = mixed[queries, place].astype(f32)
        k = kd[group, 0:keys, :]
        k_t = kt[group, :, 0:keys]
        dk_sum = dk[group, 0:keys, :]
        dv_sum = dv[group, 0:keys, :]
        for head, values in enumerate((v0, v1)):
            own = (lane < half) if head == 0 else (lane >= half)
            q_head = jnp.where(own, q, 0.0).astype(bf16)
            up_head = jnp.where(own, up, 0.0).astype(bf16)
            seen = jnp.where(own, up, mix).astype(bf16)
            e = jnp.exp2(nt(k, q_head) * log_scale + bias[0:keys, queries])
            ds = (e * nt(values[group, 0:keys, :], seen)).astype(bf16)
            dv_sum = dv_sum + nn(e.astype(bf16), up_head)
            dk_sum = dk_sum + nn(ds, q_head)
            piece = nn(k_t, ds)
            target = pl.ds(pl.multiple_of(start + head * half, half), half)
            if fresh:
                dq_t[target, queries] = piece
            else:
                dq_t[target, queries] += piece
        dk[group, 0:keys, :] = dk_sum
        dv[group, 0:keys, :] = dv_sum
        return carry

    lax.fori_loop(0, pairs, body, 0)


def fold_pairs(sums):
    lane = lane_of(sums.shape[1:])
    first = sums[0]
    second = sums[1]
    return jnp.where(lane < half, first + swap_halves(first), second + swap_halves(second))


def transposed_keys(kv, kt):
    key = kv[:, 0:lanes].astype(f32).T
    kt[0] = key[0:half].astype(bf16)
    kt[1] = key[half:].astype(bf16)


def far_kernel(
    meta, cot, summed, att, wide, inv, narrow, qrot, kv, segq, w0, w1, w2, w3, ao, bo,
    dop, mixed, dq_t, dkv, part_pack, full_pack,
    up, a_all, b_all, kd, v0, v1, kt, bias, dk, dv, *, log_scale, block,
):
    length = cot.shape[0]
    a_all[...] = jnp.zeros_like(a_all)
    b_all[...] = jnp.zeros_like(b_all)
    a_all[0:rank, :] = ao[0]
    b_all[0:rank, :] = bo[0]

    def body(index, carry):
        part_sum, full_sum = carry
        rows = pl.ds(pl.multiple_of(index * block, block), block)
        up[rows, :] = (cot[rows, :].astype(f32) + summed[rows, :].astype(f32)).astype(bf16)
        low = nt(up[rows, :], b_all[...])
        grad = nn(low.astype(bf16), a_all[...])
        for number, weight in enumerate((w0, w1, w2, w3)):
            columns = pl.ds(at(meta, number), weight.shape[1])
            grad = grad + nt(up[rows, columns], weight[...])
        scaled = (grad.astype(bf16).astype(f32) * inv[rows, :]).astype(bf16)
        dop[rows, :] = scaled
        inner = scaled.astype(f32) * wide[rows, :]
        for start in range(0, inner.shape[1], lanes):
            mixed[rows, start : start + lanes] = (
                -swap_halves(inner[:, start : start + lanes])
            ).astype(bf16)
        part_sum = part_sum + nn(low.T[0:rank].astype(bf16), att[rows, :])
        full_sum = full_sum + nn(narrow[rows, :].astype(f32).T[0:rank].astype(bf16), up[rows, :])
        return part_sum, full_sum

    part_sum, full_sum = lax.fori_loop(
        0,
        length // block,
        body,
        (jnp.zeros((rank, att.shape[1]), f32), jnp.zeros((rank, cot.shape[1]), f32)),
    )
    part_pack[...] = part_sum.astype(bf16)
    full_pack[...] = full_sum.astype(bf16)
    spread_keys(kv, kd, v0, v1, 0, length)
    transposed_keys(kv, kt)
    segk = jnp.where(meta[5] > 0, kv[:, 2 * lanes :].astype(f32)[:, 0:1], -1.0)
    bias[...] = jnp.where(segk == segq[...].astype(f32), 0.0, masked)
    dk[...] = jnp.zeros_like(dk)
    dv[...] = jnp.zeros_like(dv)
    for start in range(0, length, block):
        attention_back(
            qrot, dop, mixed, kd, v0, v1, kt, bias, dq_t, dk, dv, start, block, length, log_scale, True
        )
    dkv[:, 0:lanes] = (fold_pairs(dk[...]) * (half**-0.5)).astype(bf16)
    dkv[:, lanes:] = fold_pairs(dv[...]).astype(bf16)


def near_kernel(
    meta, dop, mixed, qrot, kv, segq, dq_far,
    dq_t, dkv, kd, v0, v1, kt, bias, dk, dv, *, log_scale, block,
):
    length = qrot.shape[0]
    spread_keys(kv, kd, v0, v1, 0, length)
    transposed_keys(kv, kt)
    key = lax.broadcasted_iota(jnp.int32, (length, length), 0)
    query = lax.broadcasted_iota(jnp.int32, (length, length), 1)
    segk = kv[:, 2 * lanes :].astype(f32)[:, 0:1]
    bias[...] = jnp.where((segk == segq[...].astype(f32)) & (key <= query), 0.0, masked)
    dk[...] = jnp.zeros_like(dk)
    dv[...] = jnp.zeros_like(dv)
    dq_t[...] = dq_far[...]
    for start in range(0, length, block):
        attention_back(
            qrot, dop, mixed, kd, v0, v1, kt, bias, dq_t, dk, dv, start, block, start + block,
            log_scale, False,
        )
    dkv[:, 0:lanes] = fold_pairs(dk[...]) * (half**-0.5)
    dkv[:, lanes:] = fold_pairs(dv[...])


def back_scratch(length):
    return [
        pltpu.VMEM((2, length, lanes), bf16),
        pltpu.VMEM((2, length, lanes), bf16),
        pltpu.VMEM((2, length, lanes), bf16),
        pltpu.VMEM((2, half, length), bf16),
        pltpu.VMEM((length, length), f32),
        pltpu.VMEM((2, length, lanes), f32),
        pltpu.VMEM((2, length, lanes), f32),
    ]


def attention_backward_far(
    meta, cot, summed, att, wide, inv, narrow, qrot, kv, segq, weights, down, lift, log_scale
):
    length, model = cot.shape
    q_width = qrot.shape[1]
    pick = lambda a: pl.BlockSpec(
        (1,) + a.shape[1:], lambda i, m: (m[7], 0, 0), pipeline_mode=pl.Buffered(1)
    )
    plain = (cot, summed, att, wide, inv, narrow, qrot, kv, segq, *weights)
    shapes = [
        result((length, q_width), bf16),
        result((length, q_width), bf16),
        result((q_width, length), f32),
        result((length, 2 * lanes), bf16),
        result((rank, q_width), bf16),
        result((rank, model), bf16),
    ]
    return pl.pallas_call(
        partial(far_kernel, log_scale=log_scale, block=256),
        name="attention_backward_far",
        grid_spec=pltpu.PrefetchScalarGridSpec(
            num_scalar_prefetch=1,
            grid=(1,),
            in_specs=[fixed(a.shape) for a in plain] + [pick(down), pick(lift)],
            out_specs=[fixed(s.shape) for s in shapes],
            scratch_shapes=[
                pltpu.VMEM((length, model), bf16),
                pltpu.VMEM((lanes, q_width), bf16),
                pltpu.VMEM((lanes, model), bf16),
            ]
            + back_scratch(length),
        ),
        out_shape=shapes,
        cost_estimate=pl.CostEstimate(
            flops=20 * length * length * q_width, transcendentals=length * length * 8,
            bytes_accessed=16 * 1024 * 1024,
        ),
        compiler_params=pltpu.CompilerParams(vmem_limit_bytes=vmem_bytes),
    )(meta, *plain, down, lift)


def attention_backward_near(meta, dop, mixed, qrot, kv, segq, dq_far, log_scale):
    length, q_width = qrot.shape
    plain = (dop, mixed, qrot, kv, segq, dq_far)
    shapes = [result((q_width, length), f32), result((length, 2 * lanes), f32)]
    return pl.pallas_call(
        partial(near_kernel, log_scale=log_scale, block=256),
        name="attention_backward_near",
        grid_spec=pltpu.PrefetchScalarGridSpec(
            num_scalar_prefetch=1,
            grid=(1,),
            in_specs=[fixed(a.shape) for a in plain],
            out_specs=[fixed(s.shape) for s in shapes],
            scratch_shapes=back_scratch(length),
        ),
        out_shape=shapes,
        cost_estimate=pl.CostEstimate(
            flops=20 * length * length * q_width, transcendentals=length * length * 8,
            bytes_accessed=6 * 1024 * 1024,
        ),
        compiler_params=pltpu.CompilerParams(vmem_limit_bytes=vmem_bytes),
    )(meta, *plain)


def qkv_grad_kernel(
    meta, normed, narrow, pre, dq_t, dkv_near, dkv_back, bq, bk, bv, qg, kg, cos, sin,
    grad, low_out, down_pack, q_lift, kv_lift, b_all, down_sum, lift_sum,
):
    q_width, kv_width = bq.shape[2], bk.shape[2]
    step = pl.program_id(0)

    @pl.when(step == 0)
    def _():
        b_all[...] = jnp.zeros_like(b_all)
        b_all[0:rank, 0:q_width] = bq[0]
        b_all[rank : 2 * rank, q_width : q_width + kv_width] = bk[0]
        b_all[2 * rank : 3 * rank, q_width + kv_width :] = bv[0]
        down_sum[...] = jnp.zeros_like(down_sum)
        lift_sum[...] = jnp.zeros_like(lift_sum)

    matrix = head_mean_matrix()
    dkv = dkv_near[...] + dkv_back[...].astype(f32)
    for start in range(0, q_width + kv_width, lanes):
        if start < q_width:
            upstream = dq_t[start : start + lanes, :].T * (half**-0.5)
        else:
            upstream = dkv[:, start - q_width : start - q_width + lanes]
        upstream = upstream * cos[...] - partner(upstream) * sin[...]
        value = pre[:, start : start + lanes]
        inverse = lax.rsqrt(head_mean(value * value, matrix) + epsilon)
        weighted = upstream * (qg if start < q_width else kg)[...]
        mean = head_mean(weighted * value, matrix)
        grad[:, start : start + lanes] = (
            inverse * weighted - value * (inverse * inverse * inverse * mean)
        ).astype(bf16)
    grad[:, q_width + kv_width :] = dkv[:, kv_width:].astype(bf16)
    own = grad[...]
    low = nt(own, b_all[...])
    low_out[...] = low.astype(bf16)
    down_sum[...] += nn(low.T[0 : 3 * rank].astype(bf16), normed[...])
    lift_sum[...] += nn(narrow[...].astype(f32).T[0 : 3 * rank].astype(bf16), own)

    @pl.when(step == pl.num_programs(0) - 1)
    def _():
        down_pack[...] = down_sum[...].astype(bf16)
        q_lift[...] = lift_sum[0:rank, 0:q_width].astype(bf16)
        kv_lift[:, 0:kv_width] = lift_sum[rank : 2 * rank, q_width : q_width + kv_width].astype(bf16)
        kv_lift[:, kv_width:] = lift_sum[2 * rank :, q_width + kv_width :].astype(bf16)


def qkv_grads(
    meta, normed, narrow, pre, dq_t, dkv_near, dkv_back, lifts, q_gain, k_gain, cos, sin
):
    length, width = normed.shape
    q_width, kv_width = lifts[0].shape[2], lifts[1].shape[2]
    every = q_width + 2 * kv_width
    block = 256
    tile = lambda w: pl.BlockSpec((block, w), lambda i, m: (i, 0))
    return pl.pallas_call(
        qkv_grad_kernel,
        name="qkv_grads",
        grid_spec=pltpu.PrefetchScalarGridSpec(
            num_scalar_prefetch=1,
            grid=(length // block,),
            in_specs=[
                tile(width), tile(lanes), tile(q_width + kv_width),
                pl.BlockSpec((q_width, block), lambda i, m: (0, i)), tile(2 * kv_width),
                tile(2 * kv_width),
            ]
            + [picked(a) for a in lifts]
            + [fixed(q_gain.shape), fixed(k_gain.shape), tile(lanes), tile(lanes)],
            out_specs=[
                tile(every), tile(lanes), fixed((3 * rank, width)), fixed((rank, q_width)),
                fixed((rank, 2 * kv_width)),
            ],
            scratch_shapes=[
                pltpu.VMEM((lanes, every), bf16),
                pltpu.VMEM((3 * rank, width), f32),
                pltpu.VMEM((3 * rank, every), f32),
            ],
        ),
        out_shape=[
            result((length, every), bf16),
            result((length, lanes), bf16),
            result((3 * rank, width), bf16),
            result((rank, q_width), bf16),
            result((rank, 2 * kv_width), bf16),
        ],
        cost_estimate=pl.CostEstimate(
            flops=2 * length * width * every // 8, transcendentals=0, bytes_accessed=8 * 1024 * 1024
        ),
        compiler_params=params(),
    )(
        meta, normed, narrow, pre, dq_t, dkv_near, dkv_back, *lifts, q_gain, k_gain, cos, sin
    )


def qkv_back_kernel(
    meta, hid, gain, grad, low, q0, q1, q2, q3, kv0, kv1, kv2, kv3, aq, ak, av, back, a_all, total,
):
    @pl.when(pl.program_id(0) == 0)
    def _():
        a_all[...] = jnp.zeros_like(a_all)
        a_all[0:rank, :] = aq[0]
        a_all[rank : 2 * rank, :] = ak[0]
        a_all[2 * rank : 3 * rank, :] = av[0]

    q_width = q0.shape[1]
    q_own, kv_own = grad[:, :q_width], grad[:, q_width:]
    for index, (q_weight, kv_weight) in enumerate(((q0, kv0), (q1, kv1), (q2, kv2), (q3, kv3))):
        columns = pl.ds(at(meta, index), q_weight.shape[0])
        total[:, columns] = (
            nt(q_own, q_weight[...]) + nt(kv_own, kv_weight[...]) + nn(low[...], a_all[:, columns])
        )
    wide = hid[...].astype(f32)
    inverse = lax.rsqrt(jnp.mean(wide * wide, axis=-1, keepdims=True) + epsilon)
    weighted = total[...] * gain[...].astype(f32)
    mean = jnp.mean(weighted * wide, axis=-1, keepdims=True)
    back[...] = (inverse * weighted - wide * (inverse * inverse * inverse * mean)).astype(bf16)


def qkv_backward(meta, hid, gain, grad, low, weights, downs):
    length, width = hid.shape
    every = grad.shape[1]
    block = 256
    tile = lambda w: pl.BlockSpec((block, w), lambda i, m: (i, 0))
    return pl.pallas_call(
        qkv_back_kernel,
        name="qkv_backward",
        grid_spec=pltpu.PrefetchScalarGridSpec(
            num_scalar_prefetch=1,
            grid=(length // block,),
            in_specs=[tile(width), fixed(gain.shape), tile(every), tile(lanes)]
            + [fixed(w.shape) for w in weights]
            + [picked(a) for a in downs],
            out_specs=tile(width),
            scratch_shapes=[pltpu.VMEM((lanes, width), bf16), pltpu.VMEM((block, width), f32)],
        ),
        out_shape=result((length, width), bf16),
        cost_estimate=pl.CostEstimate(
            flops=2 * length * width * every, transcendentals=0, bytes_accessed=8 * 1024 * 1024
        ),
        compiler_params=params(),
    )(meta, hid, gain, grad, low, *weights, *downs)


def place_kernel(sets, *refs, pieces):
    inputs = refs[: len(refs) - len(pieces)]
    outputs = refs[len(inputs) :]
    slot = pl.program_id(0)
    for out in outputs:
        out[...] = jnp.zeros_like(out)
    for sequence in range(inputs[0].shape[0]):

        @pl.when(sets[sequence] == slot)
        def _():
            for (source, row, column), out in zip(pieces, outputs):
                piece = inputs[source][sequence, row : row + rank, column : column + out.shape[2]]
                out[0] += piece.astype(f32)


def place_sets(sets, gathered, pieces, slots, weight):
    shapes = [result((slots, rank, width), f32) for _, _, _, width in pieces]
    return pl.pallas_call(
        partial(place_kernel, pieces=[p[:3] for p in pieces]),
        name="place_sets",
        grid_spec=pltpu.PrefetchScalarGridSpec(
            num_scalar_prefetch=1,
            grid=(slots,),
            in_specs=[fixed(g.shape) for g in gathered],
            out_specs=[pl.BlockSpec((1,) + s.shape[1:], lambda i, m: (i, 0, 0)) for s in shapes],
        ),
        out_shape=shapes,
        cost_estimate=pl.CostEstimate(flops=weight, transcendentals=0, bytes_accessed=8 * 1024 * 1024),
        compiler_params=params(),
    )(sets, *gathered)


def close_kernel(meta, first, second, reduced, out):
    out[...] = (
        first[...].astype(f32) + second[...].astype(f32) + reduced[...].astype(f32)
    ).astype(out.dtype)


def close(meta, first, second, reduced, dtype):
    length, width = reduced.shape
    block = 256
    columns = pl.BlockSpec((block, width), lambda i, m: (i, m[4]))
    tile = pl.BlockSpec((block, width), lambda i, m: (i, 0))
    return pl.pallas_call(
        close_kernel,
        name="close",
        grid_spec=pltpu.PrefetchScalarGridSpec(
            num_scalar_prefetch=1,
            grid=(length // block,),
            in_specs=[columns, columns, tile],
            out_specs=tile,
        ),
        out_shape=result(reduced.shape, dtype),
        cost_estimate=pl.CostEstimate(flops=0, transcendentals=0, bytes_accessed=4 * 1024 * 1024),
        compiler_params=params(),
    )(meta, first, second, reduced)


def flip(array, axis, bit):
    count = lax.axis_size(axis)
    return lax.ppermute(array, axis, [(i, i ^ bit) for i in range(count)])


def quarters(weight, axis):
    full = lax.all_gather(weight, "fsdp", axis=axis, tiled=True)
    return jnp.split(full, 4, axis=axis)


def after(array, *others):
    return lax.optimization_barrier((array, *others))[0]


def own_half(weight, axis):
    size = weight.shape[axis] // 2
    return lax.dynamic_slice_in_dim(weight, lax.axis_index("ctx") * size, size, axis)


def six_parts(weight, axis):
    shards = quarters(weight, axis)
    return shards[:2] + jnp.split(shards[2], 2, axis=axis) + jnp.split(shards[3], 2, axis=axis)


def shard_places(width, direct):
    unit = width // 4
    part = unit // 2
    if direct:
        four = [(lax.axis_index("fsdp") ^ bit) * unit for bit in range(4)]
        near = lax.axis_index("ctx") * part
    else:
        four, near = [0, unit, 2 * unit, 3 * unit], 0
    away = part - near
    return four, [four[0], four[1], four[2] + near, four[2] + away, four[3] + near, four[3] + away]


def pick_side(low, high, bit, axis):
    return jnp.where(
        bit == 0, jnp.concatenate([low, high], axis=axis), jnp.concatenate([high, low], axis=axis)
    )


def halve(array, axis, bit, stride):
    size = array.shape[-1] // 2
    keep = lax.dynamic_slice_in_dim(array, bit * size, size, array.ndim - 1)
    give = lax.dynamic_slice_in_dim(array, (1 - bit) * size, size, array.ndim - 1)
    taken = flip(give, axis, stride)
    return (keep.astype(f32) + taken.astype(f32)).astype(bf16)


def double(array, axis, bit, stride):
    taken = flip(array, axis, stride)
    return pick_side(array, taken, bit, array.ndim - 1)


def gather_sequences(full, part, *others):
    fsdp = lax.axis_size("fsdp")
    if fsdp != 4 or lax.axis_size("ctx") != 2 or lax.axis_size("tp") != 4:
        full = lax.psum(full, ("ctx", "tp"))
        part = [lax.psum(p, "ctx") for p in part]
        return (
            lax.all_gather(full, "fsdp", axis=0),
            [lax.all_gather(p, "fsdp", axis=0) for p in part],
        )
    own, side, place = lax.axis_index("fsdp"), lax.axis_index("ctx"), lax.axis_index("tp")
    full = halve(full, "ctx", side, 1)
    part = [halve(p, "ctx", side, 1) for p in part]
    full = halve(full, "tp", place % 2, 1)
    full = halve(full, "tp", place // 2, 2)

    def both(array, bit, stride):
        taken = flip(array, "fsdp", stride)
        return pick_side(array, taken, bit, 0)

    full = after(full, *others) if others else full
    full = both(full[None], own // 2, 2)
    part = [both(p[None], own // 2, 2) for p in part]
    full = double(full, "tp", place // 2, 2)
    full = double(full, "tp", place % 2, 1)
    full = double(full, "ctx", side, 1)
    part = [double(p, "ctx", side, 1) for p in part]

    def cores(array):
        taken = flip(array, "fsdp", 1)
        even = own % 2 == 0
        pairs = [jnp.where(even, array[i], taken[i]) for i in range(2)]
        others = [jnp.where(even, taken[i], array[i]) for i in range(2)]
        return jnp.stack([pairs[0], others[0], pairs[1], others[1]])

    return cores(full), [cores(p) for p in part]


def gather_ids(ids):
    if lax.axis_size("fsdp") != 4:
        return lax.all_gather(ids, "fsdp", tiled=True)
    own = lax.axis_index("fsdp")
    two = pick_side(ids, flip(ids, "fsdp", 1), own % 2, 0)
    return pick_side(two, flip(two, "fsdp", 2), own // 2, 0)


def on_device(
    hidden_in, segment_ids, adapter_ids, attention_gain, query_gain, key_gain, feedforward_gain,
    query_weight, key_weight, value_weight, output_weight, gate_weight, linear_weight, reduce_weight,
    query_down, query_lift, key_down, key_lift, value_down, value_lift, output_down, output_lift,
    gate_down, gate_lift, linear_down, linear_lift, reduce_down, reduce_lift, output_cotangent,
):
    _, length, model = hidden_in.shape
    head_dim = query_gain.shape[0]
    log_scale = head_dim**-0.5 * 1.4426950408889634
    context_index = lax.axis_index("ctx")
    tensor_index = lax.axis_index("tp")
    hid = hidden_in[0]
    cot = output_cotangent[0]
    direct = lax.axis_size("fsdp") == 4 and lax.axis_size("ctx") == 2
    four, six = shard_places(model, direct)
    values = (*four, tensor_index, context_index, 0, adapter_ids[0], *six, 0, 0)
    meta = jnp.stack([jnp.asarray(value, jnp.int32) for value in values])

    positions = (context_index * length + jnp.arange(length)).astype(f32)
    frequency = rope_base ** (-2.0 * jnp.arange(head_dim // 2).astype(f32) / head_dim)
    angles = positions[:, None] * frequency[None, :]
    cosine, sine = jnp.cos(angles), jnp.sin(angles)
    cos = jnp.concatenate([cosine] * 4, axis=1)
    sin = jnp.concatenate([-sine, sine] * 2, axis=1)
    q_gain = jnp.tile(query_gain.astype(f32), 2)[None]
    k_gain = jnp.tile(key_gain.astype(f32), 2)[None]
    a_gain = attention_gain[None]
    f_gain = feedforward_gain[None]
    seg_own = segment_ids.reshape(length, 1)
    count = lax.axis_size("ctx")
    onward = [(i, i + 1) for i in range(count - 1)]
    backward = [(i + 1, i) for i in range(count - 1)]
    turn = lambda table: jnp.swapaxes(table, 1, 2)
    qkv_downs = [turn(query_down), turn(key_down), turn(value_down)]
    qkv_lifts = [query_lift, key_lift, value_lift]
    output_first = turn(output_down)
    reduce_first = turn(reduce_down)

    kv_own = jnp.concatenate([key_weight, value_weight], axis=1)
    normed, qkv_narrow = attention_norm(meta, hid, a_gain, qkv_downs)
    if direct:
        q_across = flip(query_weight, "fsdp", 2)
        gate_half = own_half(gate_weight, 0)
        tables = (cos, sin, q_gain, k_gain, f_gain, seg_own, normed)
        kv_across = flip(after(kv_own, *tables), "fsdp", 2)
        cores = [flip(w, "fsdp", 1) for w in (gate_weight, linear_weight, reduce_weight)]
        q_side = flip(after(query_weight, q_across), "fsdp", 1)
        kv_side = flip(after(kv_own, kv_across), "fsdp", 1)
        qkv_weights = [
            query_weight, q_side, q_across,
            flip(after(q_across, *cores), "fsdp", 1),
            kv_own, kv_side, kv_across, flip(after(kv_across, *cores), "fsdp", 1),
        ]
        output_across = flip(after(output_weight, q_across, kv_across), "fsdp", 2)
        gate_across = flip(after(gate_half, q_across, kv_across), "fsdp", 2)
    else:
        qkv_weights = quarters(query_weight, 0) + quarters(kv_own, 0)
        output_weights = quarters(output_weight, 1)
        gates = six_parts(gate_weight, 0)
        linears = quarters(linear_weight, 0)
        reduces = quarters(reduce_weight, 1)

    pre, qrot, kv = qkv_forward(
        meta, normed, qkv_narrow, qkv_weights, qkv_lifts, q_gain, k_gain, cos, sin, seg_own
    )
    kv_far = lax.ppermute(kv, "ctx", onward)
    ready = after(qrot, gate_across) if direct else qrot
    att, wide, inv = attention_forward(meta, ready, kv_far, kv, log_scale)
    if direct:
        gate_other = flip(after(gate_across, att), "ctx", 1)
        linear_across = flip(after(linear_weight, att, output_across), "fsdp", 2)
        reduce_across = flip(after(reduce_weight, att, output_across), "fsdp", 2)
        output_weights = [
            output_weight, flip(after(output_weight, kv_far), "fsdp", 1), output_across,
            flip(after(output_across, kv_far), "fsdp", 1),
        ]
    branch, output_narrow = output_forward(meta, att, output_weights, output_first, output_lift)
    if direct:
        gates = [
            gate_weight, cores[0], gate_across, gate_other, flip(after(gate_across, gate_other), "fsdp", 1),
            flip(gate_other, "fsdp", 1),
        ]
        linears = [linear_weight, cores[1], linear_across, flip(linear_across, "fsdp", 1)]
        reduces = [reduce_weight, cores[2], reduce_across, flip(reduce_across, "fsdp", 1)]
    branch = lax.psum(branch, "tp")

    back, inner, gate_grad, linear_grad, n_gl_t, m_gl_t, m_r_t = ffn(
        meta, hid, branch, cot, f_gain, gates, linears, reduces,
        [turn(gate_down), turn(linear_down), reduce_first], [gate_lift, linear_lift, reduce_lift],
    )
    summed = lax.psum(back, "tp")
    ffn_part, ffn_full, n_r = ffn_adapters(
        meta, hid, branch, cot, f_gain, inner, gate_grad, linear_grad, n_gl_t, m_gl_t, m_r_t,
        reduce_first,
    )
    sets = gather_ids(after(adapter_ids, inner))
    slots = query_down.shape[0]
    ffn_full, (ffn_part,) = gather_sequences(ffn_full, [ffn_part])
    hidden = gate_lift.shape[2]
    ffn_pieces = [(0, rank * i, 0, model) for i in range(3)] + [(1, rank * i, 0, hidden) for i in range(3)]
    ffn_grads = place_sets(sets, [ffn_full, ffn_part], ffn_pieces, slots, 1024)
    out = reduce_forward(meta, inner, n_r, reduces, reduce_lift)
    out_columns = lax.psum_scatter(out, "tp", scatter_dimension=1, tiled=True)
    block_out = close(meta, hid, branch, out_columns, bf16)
    settled = after(summed, *ffn_grads)

    dop, mixed, dq_far, dkv_far, output_part, output_full = attention_backward_far(
        meta, cot, settled, att, wide, inv, output_narrow, qrot, kv_far, segment_ids,
        output_weights, output_first, output_lift, log_scale,
    )
    dkv_back = lax.ppermute(dkv_far, "ctx", backward)
    dq_t, dkv_near = attention_backward_near(
        meta, dop, mixed, qrot, kv, segment_ids, dq_far, log_scale
    )
    grad, low, qkv_full, q_part, kv_part = qkv_grads(
        meta, normed, qkv_narrow, pre, dq_t, dkv_near, dkv_back, qkv_lifts, q_gain, k_gain, cos, sin
    )
    last = qkv_backward(meta, hid, a_gain, grad, low, qkv_weights, qkv_downs)
    last_columns = lax.psum_scatter(last, "tp", scatter_dimension=1, tiled=True)
    input_grad = close(meta, cot, summed, last_columns, f32)

    q_width, kv_width = query_lift.shape[2], key_lift.shape[2]
    att_full, (att_part,) = gather_sequences(
        jnp.concatenate([qkv_full, output_full], axis=0),
        [jnp.concatenate([q_part, kv_part, output_part], axis=1)],
        block_out,
    )

    att_pieces = [(0, rank * i, 0, model) for i in range(4)] + [
        (1, 0, 0, q_width),
        (1, 0, q_width, kv_width),
        (1, 0, q_width + kv_width, kv_width),
        (1, 0, q_width + 2 * kv_width, q_width),
    ]
    att_grads = place_sets(sets, [att_full, att_part], att_pieces, slots, 1 << 33)
    return (
        block_out[None],
        input_grad[None],
        turn(att_grads[0]),
        att_grads[4],
        turn(att_grads[1]),
        att_grads[5],
        turn(att_grads[2]),
        att_grads[6],
        turn(att_grads[7]),
        att_grads[3],
        turn(ffn_grads[0]),
        ffn_grads[3],
        turn(ffn_grads[1]),
        ffn_grads[4],
        turn(ffn_grads[5]),
        ffn_grads[2],
    )


def solution(mesh):
    tokens = P("fsdp", "ctx", None)
    rows_split = P("fsdp", "tp")
    lift_split = P(None, None, "tp")
    down_split = P(None, "tp", None)
    in_specs = (
        tokens, P("fsdp", "ctx"), P("fsdp"), P(), P(), P(), P(),
        rows_split, rows_split, rows_split, P("tp", "fsdp"), rows_split, rows_split, P("tp", "fsdp"),
        P(), lift_split, P(), lift_split, P(), lift_split, down_split, P(),
        P(), lift_split, P(), lift_split, down_split, P(), tokens,
    )
    cut = P("fsdp", "ctx", "tp")
    out_specs = (
        cut, cut, P(), lift_split, P(), lift_split, P(), lift_split, down_split, P(),
        P(), lift_split, P(), lift_split, down_split, P(),
    )
    return jax.shard_map(
        on_device, mesh=mesh, in_specs=in_specs, out_specs=out_specs, check_vma=False
    )
```

```python
from functools import partial

import jax
import jax.numpy as jnp
from jax import lax
from jax.experimental import pallas as pl
from jax.experimental.pallas import tpu as pltpu
from jax.sharding import PartitionSpec as P

epsilon = 1e-05
rope_base = 1000000.0
masked = -1e30
f32 = jnp.float32
bf16 = jnp.bfloat16
lanes = 128
half = 64
rank = 16
vmem_bytes = 58 * 1024 * 1024


def nn(left, right):
    return lax.dot_general(left, right, (((1,), (0,)), ((), ())), preferred_element_type=f32)


def nt(left, right):
    return lax.dot_general(left, right, (((1,), (1,)), ((), ())), preferred_element_type=f32)


def at(ref, index):
    return pl.multiple_of(ref[index], lanes)


def fixed(shape):
    return pl.BlockSpec(shape, lambda *_: (0,) * len(shape), pipeline_mode=pl.Buffered(1))


def picked(array):
    return pl.BlockSpec(
        (1,) + array.shape[1:], lambda i, m: (m[7], 0, 0), pipeline_mode=pl.Buffered(1)
    )


def params():
    return pltpu.CompilerParams(vmem_limit_bytes=vmem_bytes)


def result(shape, dtype):
    return jax.ShapeDtypeStruct(shape, dtype)


def lane_of(shape):
    return lax.broadcasted_iota(jnp.int32, shape, len(shape) - 1)


def head_mean_matrix():
    row = lax.broadcasted_iota(jnp.int32, (lanes, lanes), 0)
    col = lax.broadcasted_iota(jnp.int32, (lanes, lanes), 1)
    return jnp.where((row // half) == (col // half), 1.0 / half, 0.0).astype(bf16)


def head_mean(values, matrix):
    high = values.astype(bf16)
    low = (values - high.astype(f32)).astype(bf16)
    return nn(high, matrix) + nn(low, matrix)


def partner(values):
    first = (lane_of(values.shape) % half) < (half // 2)
    return jnp.where(
        first,
        pltpu.roll(values, lanes - half // 2, values.ndim - 1),
        pltpu.roll(values, half // 2, values.ndim - 1),
    )


def swap_halves(values):
    return pltpu.roll(values, half, values.ndim - 1)


def norm_kernel(meta, hid, gain, aq, ak, av, normed, narrow, a_all):
    @pl.when(pl.program_id(0) == 0)
    def _():
        a_all[...] = jnp.zeros_like(a_all)
        a_all[0:rank, :] = aq[0]
        a_all[rank : 2 * rank, :] = ak[0]
        a_all[2 * rank : 3 * rank, :] = av[0]

    wide = hid[...].astype(f32)
    inverse = lax.rsqrt(jnp.mean(wide * wide, axis=-1, keepdims=True) + epsilon)
    normed[...] = (wide * inverse * gain[...].astype(f32)).astype(bf16)
    narrow[...] = nt(normed[...], a_all[...]).astype(bf16)


def attention_norm(meta, hid, gain, downs):
    length, width = hid.shape
    block = 128
    tile = lambda w: pl.BlockSpec((block, w), lambda i, m: (i, 0))
    return pl.pallas_call(
        norm_kernel,
        name="attention_norm",
        grid_spec=pltpu.PrefetchScalarGridSpec(
            num_scalar_prefetch=1,
            grid=(length // block,),
            in_specs=[tile(width), fixed(gain.shape)] + [picked(a) for a in downs],
            out_specs=[tile(width), tile(lanes)],
            scratch_shapes=[pltpu.VMEM((lanes, width), bf16)],
        ),
        out_shape=[result((length, width), bf16), result((length, lanes), bf16)],
        cost_estimate=pl.CostEstimate(flops=1024, transcendentals=0, bytes_accessed=1024),
        compiler_params=params(),
    )(meta, hid, gain, *downs)


def qkv_kernel(
    meta, normed, narrow, q0, q1, q2, q3, kv0, kv1, kv2, kv3, bq, bk, bv, qg, kg, cos, sin,
    seg, pre, qrot, kv, b_all,
):
    q_width, kv_width = bq.shape[2], bk.shape[2]

    @pl.when(pl.program_id(0) == 0)
    def _():
        b_all[...] = jnp.zeros_like(b_all)
        b_all[0:rank, 0:q_width] = bq[0]
        b_all[rank : 2 * rank, q_width : q_width + kv_width] = bk[0]
        b_all[2 * rank : 3 * rank, q_width + kv_width :] = bv[0]

    total = nn(narrow[...], b_all[...])
    q_total, kv_total = total[:, :q_width], total[:, q_width:]
    for index, (q_weight, kv_weight) in enumerate(((q0, kv0), (q1, kv1), (q2, kv2), (q3, kv3))):
        part = normed[:, pl.ds(at(meta, index), q_weight.shape[0])]
        q_total = q_total + nn(part, q_weight[...])
        kv_total = kv_total + nn(part, kv_weight[...])
    total = jnp.concatenate([q_total, kv_total], axis=1)
    pre[...] = total[:, : q_width + kv_width]
    matrix = head_mean_matrix()
    for start in range(0, q_width + kv_width, lanes):
        part = total[:, start : start + lanes]
        head_gain = qg if start < q_width else kg
        scaled = part * lax.rsqrt(head_mean(part * part, matrix) + epsilon) * head_gain[...]
        turned = (scaled * cos[...] + partner(scaled) * sin[...]).astype(bf16)
        if start < q_width:
            qrot[:, start : start + lanes] = turned
        else:
            kv[:, start - q_width : start - q_width + lanes] = turned
    kv[:, kv_width : 2 * kv_width] = total[:, q_width + kv_width :].astype(bf16)
    kv[:, 2 * kv_width :] = jnp.broadcast_to(seg[...].astype(f32), (seg.shape[0], lanes)).astype(bf16)


def qkv_forward(meta, normed, narrow, weights, lifts, q_gain, k_gain, cos, sin, seg):
    length, width = normed.shape
    q_width, kv_width = lifts[0].shape[2], lifts[1].shape[2]
    block = 256
    tile = lambda w: pl.BlockSpec((block, w), lambda i, m: (i, 0))
    return pl.pallas_call(
        qkv_kernel,
        name="qkv_forward",
        grid_spec=pltpu.PrefetchScalarGridSpec(
            num_scalar_prefetch=1,
            grid=(length // block,),
            in_specs=[tile(width), tile(lanes)]
            + [fixed(w.shape) for w in weights]
            + [picked(a) for a in lifts]
            + [fixed(q_gain.shape), fixed(k_gain.shape), tile(lanes), tile(lanes), tile(1)],
            out_specs=[tile(q_width + kv_width), tile(q_width), tile(2 * kv_width + lanes)],
            scratch_shapes=[pltpu.VMEM((lanes, q_width + 2 * kv_width), bf16)],
        ),
        out_shape=[
            result((length, q_width + kv_width), f32),
            result((length, q_width), bf16),
            result((length, 2 * kv_width + lanes), bf16),
        ],
        cost_estimate=pl.CostEstimate(flops=1024, transcendentals=0, bytes_accessed=1024),
        compiler_params=params(),
    )(meta, normed, narrow, *weights, *lifts, q_gain, k_gain, cos, sin, seg)


def spread_keys(kv, kd, v0, v1, rows, size):
    lane = lane_of((size, lanes))
    key = kv[:, 0:lanes].astype(f32)
    other = swap_halves(key)
    kd[0, rows : rows + size, :] = jnp.where(lane < half, key, other).astype(bf16)
    kd[1, rows : rows + size, :] = jnp.where(lane < half, other, key).astype(bf16)
    value = kv[:, lanes : 2 * lanes].astype(f32)
    other = swap_halves(value)
    v0[0, rows : rows + size, :] = jnp.where(lane < half, value, 1.0).astype(bf16)
    v0[1, rows : rows + size, :] = jnp.where(lane < half, other, 1.0).astype(bf16)
    v1[0, rows : rows + size, :] = jnp.where(lane < half, 1.0, other).astype(bf16)
    v1[1, rows : rows + size, :] = jnp.where(lane < half, 1.0, value).astype(bf16)


def attention_kernel(
    meta, qrot, kvf, kvn, kvq, att, wide, inv, kd, v0, v1, bias, segk, *, log_scale, block,
):
    far = kvf.shape[0]
    pairs = qrot.shape[1] // lanes
    share = pairs // 2
    step = pl.program_id(0)

    @pl.when(step == 0)
    def _():
        spread_keys(kvf, kd, v0, v1, 0, far)
        spread_keys(kvn, kd, v0, v1, far, kvn.shape[0])
        away = kvf[:, 2 * lanes :].astype(f32).T[0:8]
        segk[:, 0:far] = jnp.where(meta[5] > 0, away, -1.0)
        segk[:, far:] = kvn[:, 2 * lanes :].astype(f32).T[0:8]

    def queries(number):
        keys = far + (number + 1) * block
        key = lax.broadcasted_iota(jnp.int32, (block, keys), 1)
        query = lax.broadcasted_iota(jnp.int32, (block, keys), 0) + (far + number * block)
        segq = kvq[:, 2 * lanes :].astype(f32)[:, 0:1]
        allowed = (segq == segk[0:1, 0:keys]) & (key <= query)
        bias[:, 0:keys] = jnp.where(allowed, 0.0, masked)
        lane = lane_of((block, lanes))

        def body(pair, carry):
            group = pair // share
            place = pl.ds(pl.multiple_of(pair * lanes, lanes), lanes)
            q = qrot[:, place].astype(f32)
            q0 = jnp.where(lane < half, q, 0.0).astype(bf16)
            q1 = jnp.where(lane < half, 0.0, q).astype(bf16)
            k = kd[group, 0:keys, :]
            e0 = jnp.exp2(nt(q0, k) * log_scale + bias[:, 0:keys]).astype(bf16)
            r0 = nn(e0, v0[group, 0:keys, :])
            e1 = jnp.exp2(nt(q1, k) * log_scale + bias[:, 0:keys]).astype(bf16)
            r1 = nn(e1, v1[group, 0:keys, :])
            inverse = 1.0 / jnp.where(lane < half, swap_halves(r0), swap_halves(r1))
            out = jnp.where(lane < half, r0, r1) * inverse
            wide[:, place] = out
            inv[:, place] = inverse
            att[:, place] = out.astype(bf16)
            return carry

        lax.fori_loop(0, pairs, body, 0)

    for number in range(kvn.shape[0] // block):
        pl.when(step == number)(partial(queries, number))


def attention_forward(meta, qrot, kvf, kvn, log_scale):
    length, q_width = qrot.shape
    block = 256
    keys = kvf.shape[0] + length
    tile = lambda w: pl.BlockSpec((block, w), lambda i, m: (i, 0))
    return pl.pallas_call(
        partial(attention_kernel, log_scale=log_scale, block=block),
        name="attention_forward",
        grid_spec=pltpu.PrefetchScalarGridSpec(
            num_scalar_prefetch=1,
            grid=(length // block,),
            in_specs=[tile(q_width), fixed(kvf.shape), fixed(kvn.shape), tile(kvn.shape[1])],
            out_specs=[tile(q_width), tile(q_width), tile(q_width)],
            scratch_shapes=[
                pltpu.VMEM((2, keys, lanes), bf16),
                pltpu.VMEM((2, keys, lanes), bf16),
                pltpu.VMEM((2, keys, lanes), bf16),
                pltpu.VMEM((block, keys), f32),
                pltpu.VMEM((8, keys), f32),
            ],
        ),
        out_shape=[
            result((length, q_width), bf16),
            result((length, q_width), f32),
            result((length, q_width), f32),
        ],
        cost_estimate=pl.CostEstimate(
            flops=64 * length * keys * q_width, transcendentals=length * keys * 8,
            bytes_accessed=64 * 1024 * 1024,
        ),
        compiler_params=pltpu.CompilerParams(vmem_limit_bytes=vmem_bytes),
    )(meta, qrot, kvf, kvn, kvn)


def output_kernel(meta, att, w0, w1, w2, w3, ao, bo, branch, narrow, a_all, b_all):
    @pl.when(pl.program_id(0) == 0)
    def _():
        a_all[...] = jnp.zeros_like(a_all)
        b_all[...] = jnp.zeros_like(b_all)
        a_all[0:rank, :] = ao[0]
        b_all[0:rank, :] = bo[0]

    own = att[...]
    low = nt(own, a_all[...]).astype(bf16)
    narrow[...] = low
    for index, weight in enumerate((w0, w1, w2, w3)):
        columns = pl.ds(at(meta, index), weight.shape[1])
        branch[:, columns] = (nn(own, weight[...]) + nn(low, b_all[:, columns])).astype(bf16)


def output_forward(meta, att, weights, down, lift):
    length, q_width = att.shape
    model = lift.shape[2]
    block = 256
    tile = lambda w: pl.BlockSpec((block, w), lambda i, m: (i, 0))
    pick = lambda a: pl.BlockSpec(
        (1,) + a.shape[1:], lambda i, m: (m[7], 0, 0), pipeline_mode=pl.Buffered(1)
    )
    return pl.pallas_call(
        output_kernel,
        name="output_forward",
        grid_spec=pltpu.PrefetchScalarGridSpec(
            num_scalar_prefetch=1,
            grid=(length // block,),
            in_specs=[tile(q_width)] + [fixed(w.shape) for w in weights] + [pick(down), pick(lift)],
            out_specs=[tile(model), tile(lanes)],
            scratch_shapes=[pltpu.VMEM((lanes, q_width), bf16), pltpu.VMEM((lanes, model), bf16)],
        ),
        out_shape=[result((length, model), bf16), result((length, lanes), bf16)],
        cost_estimate=pl.CostEstimate(flops=1024, transcendentals=0, bytes_accessed=1024),
        compiler_params=pltpu.CompilerParams(vmem_limit_bytes=vmem_bytes),
    )(meta, att, *weights, down, lift)


def strip(array, width):
    return pl.BlockSpec((1, rank, width), lambda j, m: (m[7], 0, j))


def ffn_kernel(meta, hid, branch, cot, gain, *refs, shards, chunk):
    gates, linears, reduces = (refs[i:j] for i, j in zip((0,) + shards[:-1], shards))
    refs = refs[shards[-1] :]
    ag, al, ar, bg, bl, br = refs[:6]
    back, inner_out, gate_out, linear_out, n_gl_t, m_gl_t, m_r_t = refs[6:13]
    x, grad_sum, n_gl, m_gl, m_r, a_gl, b_r, b_g, b_l, a_r = refs[13:]
    step = pl.program_id(0)
    length = hid.shape[0]
    count = length // chunk

    def rows_of(index):
        return pl.ds(pl.multiple_of(index * chunk, chunk), chunk)

    def chunks(body):
        def run(index, carry):
            body(rows_of(index))
            return carry

        lax.fori_loop(0, count, run, 0)

    def normal(rows):
        middle = hid[rows, :].astype(f32) + branch[rows, :].astype(f32)
        inverse = lax.rsqrt(jnp.mean(middle * middle, axis=-1, keepdims=True) + epsilon)
        return middle, inverse

    @pl.when(step == 0)
    def _():
        for ref in (a_gl, b_r, b_g, b_l, a_r):
            ref[...] = jnp.zeros_like(ref)
        a_gl[0:rank, :] = ag[0]
        a_gl[rank : 2 * rank, :] = al[0]
        b_r[0:rank, :] = br[0]

        def body(rows):
            back_low = nt(cot[rows, :], b_r[...])
            m_r[rows, :] = back_low.astype(bf16)
            m_r_t[:, rows] = back_low.T[0:rank].astype(bf16)
            middle, inverse = normal(rows)
            x[rows, :] = (middle * inverse * gain[...].astype(f32)).astype(bf16)
            low = nt(x[rows, :], a_gl[...])
            n_gl[rows, :] = low.astype(bf16)
            n_gl_t[:, rows] = low.T[0 : 2 * rank].astype(bf16)
            m_gl[rows, :] = jnp.zeros((chunk, lanes), f32)

        chunks(body)

    b_g[0:rank, :] = bg[0]
    b_l[rank : 2 * rank, :] = bl[0]
    a_r[0:rank, :] = ar[0]

    def place(index, weight, axis):
        return pl.ds(at(meta, index), weight.shape[axis])

    def body(rows, first):
        low = n_gl[rows, :]
        gate = nn(low, b_g[...])
        linear = nn(low, b_l[...])
        for index, weight in enumerate(gates):
            gate = gate + nn(x[rows, place(8 + index, weight, 0)], weight[...])
        for index, weight in enumerate(linears):
            linear = linear + nn(x[rows, place(index, weight, 0)], weight[...])
        upstream = nn(m_r[rows, :], a_r[...])
        for index, weight in enumerate(reduces):
            upstream = upstream + nt(cot[rows, place(index, weight, 1)], weight[...])
        sigmoid = jax.nn.sigmoid(gate)
        active = gate * sigmoid
        gate_grad = (upstream * linear * sigmoid * (1.0 + gate * (1.0 - sigmoid))).astype(bf16)
        linear_grad = (upstream * active).astype(bf16)
        inner_out[rows, :] = (active * linear).astype(bf16)
        gate_out[rows, :] = gate_grad
        linear_out[rows, :] = linear_grad
        m_gl[rows, :] += nt(gate_grad, b_g[...]) + nt(linear_grad, b_l[...])
        for index, weight in enumerate(linears):
            columns = place(index, weight, 0)
            backward = nt(linear_grad, weight[...])
            if first:
                grad_sum[rows, columns] = backward
            else:
                grad_sum[rows, columns] += backward
        for index, weight in enumerate(gates):
            grad_sum[rows, place(8 + index, weight, 0)] += nt(gate_grad, weight[...])

    pl.when(step == 0)(partial(chunks, partial(body, first=True)))
    pl.when(step > 0)(partial(chunks, partial(body, first=False)))

    @pl.when(step == pl.num_programs(0) - 1)
    def _():
        def finish(rows):
            upstream = grad_sum[rows, :] + nn(m_gl[rows, :].astype(bf16), a_gl[...])
            middle, inverse = normal(rows)
            weighted = upstream * gain[...].astype(f32)
            mean = jnp.mean(weighted * middle, axis=-1, keepdims=True)
            back[rows, :] = (
                inverse * weighted - middle * (inverse * inverse * inverse * mean)
            ).astype(bf16)

        chunks(finish)
        m_gl_t[...] = m_gl[...].T[0 : 2 * rank].astype(bf16)


def ffn(
    meta, hid, branch, cot, gain, gates, linears, reduces, downs, lifts, width=512, chunk=512
):
    length, model = hid.shape
    hidden = gates[0].shape[1]
    rows = [*gates, *linears]
    shards = (len(gates), len(rows), len(rows) + len(reduces))
    column = lambda: pl.BlockSpec((length, width), lambda j, m: (0, j))
    return pl.pallas_call(
        partial(ffn_kernel, shards=shards, chunk=chunk),
        name="feed_forward",
        grid_spec=pltpu.PrefetchScalarGridSpec(
            num_scalar_prefetch=1,
            grid=(hidden // width,),
            in_specs=[fixed(hid.shape), fixed(branch.shape), fixed(cot.shape), fixed(gain.shape)]
            + [pl.BlockSpec((w.shape[0], width), lambda j, m: (0, j)) for w in rows]
            + [pl.BlockSpec((width, w.shape[1]), lambda j, m: (j, 0)) for w in reduces]
            + [picked(downs[0]), picked(downs[1]), strip(downs[2], width)]
            + [strip(lifts[0], width), strip(lifts[1], width), picked(lifts[2])],
            out_specs=[
                fixed((length, model)), column(), column(), column(),
                fixed((2 * rank, length)), fixed((2 * rank, length)), fixed((rank, length)),
            ],
            scratch_shapes=[
                pltpu.VMEM((length, model), bf16),
                pltpu.VMEM((length, model), f32),
                pltpu.VMEM((length, lanes), bf16),
                pltpu.VMEM((length, lanes), f32),
                pltpu.VMEM((length, lanes), bf16),
                pltpu.VMEM((lanes, model), bf16),
                pltpu.VMEM((lanes, model), bf16),
                pltpu.VMEM((lanes, width), bf16),
                pltpu.VMEM((lanes, width), bf16),
                pltpu.VMEM((lanes, width), bf16),
            ],
        ),
        out_shape=[result((length, model), bf16)]
        + [result((length, hidden), bf16)] * 3
        + [result((2 * rank, length), bf16)] * 2
        + [result((rank, length), bf16)],
        cost_estimate=pl.CostEstimate(
            flops=8 * length * model * hidden, transcendentals=length * hidden,
            bytes_accessed=4 * model * hidden + 14 * length * model,
        ),
        compiler_params=params(),
    )(meta, hid, branch, cot, gain, *rows, *reduces, *downs, *lifts)


def ffn_adapter_kernel(
    meta, hid, branch, cot, gain, inner, gate_grad, linear_grad, n_gl_t, m_gl_t, m_r_t, ar,
    part_pack, full_pack, n_r, low_sum, a_r,
):
    step = pl.program_id(0)

    @pl.when(step == 0)
    def _():
        a_r[...] = jnp.zeros_like(a_r)
        low_sum[...] = jnp.zeros_like(low_sum)

    a_r[0:rank, :] = ar[0]
    part_pack[0:rank, :] = nn(n_gl_t[...], gate_grad[...])[0:rank].astype(bf16)
    part_pack[rank : 2 * rank, :] = nn(n_gl_t[...], linear_grad[...])[rank:].astype(bf16)
    part_pack[2 * rank :, :] = nn(m_r_t[...], inner[...]).astype(bf16)
    low_sum[...] += nt(inner[...], a_r[...])

    @pl.when(step == pl.num_programs(0) - 1)
    def _():
        low = low_sum[...]
        n_r[...] = low.astype(bf16)
        full_pack[2 * rank :, :] = nn(low.T[0:rank].astype(bf16), cot[...]).astype(bf16)
        middle = hid[...].astype(f32) + branch[...].astype(f32)
        inverse = lax.rsqrt(jnp.mean(middle * middle, axis=-1, keepdims=True) + epsilon)
        x = (middle * inverse * gain[...].astype(f32)).astype(bf16)
        full_pack[0 : 2 * rank, :] = nn(m_gl_t[...], x).astype(bf16)


def ffn_adapters(meta, hid, branch, cot, gain, inner, gate_grad, linear_grad, n_gl_t, m_gl_t, m_r_t, down):
    length, model = hid.shape
    hidden = inner.shape[1]
    width = 512
    column = lambda: pl.BlockSpec((length, width), lambda j, m: (0, j))
    return pl.pallas_call(
        ffn_adapter_kernel,
        name="feed_forward_adapters",
        grid_spec=pltpu.PrefetchScalarGridSpec(
            num_scalar_prefetch=1,
            grid=(hidden // width,),
            in_specs=[fixed(hid.shape), fixed(branch.shape), fixed(cot.shape), fixed(gain.shape)]
            + [column(), column(), column()]
            + [fixed(n_gl_t.shape), fixed(m_gl_t.shape), fixed(m_r_t.shape), strip(down, width)],
            out_specs=[
                pl.BlockSpec((3 * rank, width), lambda j, m: (0, j)),
                fixed((3 * rank, model)),
                fixed((length, lanes)),
            ],
            scratch_shapes=[pltpu.VMEM((length, lanes), f32), pltpu.VMEM((lanes, width), bf16)],
        ),
        out_shape=[
            result((3 * rank, hidden), bf16),
            result((3 * rank, model), bf16),
            result((length, lanes), bf16),
        ],
        cost_estimate=pl.CostEstimate(
            flops=512 * length * hidden, transcendentals=0, bytes_accessed=12 * length * model
        ),
        compiler_params=params(),
    )(meta, hid, branch, cot, gain, inner, gate_grad, linear_grad, n_gl_t, m_gl_t, m_r_t, down)


def reduce_kernel(meta, inner, n_r, *refs):
    *weights, br, out, b_r = refs
    b_r[...] = jnp.zeros_like(b_r)
    b_r[0:rank, :] = br[0]
    for index, weight in enumerate(weights):
        columns = pl.ds(at(meta, index), weight.shape[1])
        out[:, columns] = (nn(inner[...], weight[...]) + nn(n_r[...], b_r[:, columns])).astype(bf16)


def reduce_forward(meta, inner, n_r, reduces, lift):
    length = inner.shape[0]
    model = lift.shape[2]
    return pl.pallas_call(
        reduce_kernel,
        name="reduce_forward",
        grid_spec=pltpu.PrefetchScalarGridSpec(
            num_scalar_prefetch=1,
            grid=(1,),
            in_specs=[fixed(inner.shape), fixed(n_r.shape)]
            + [fixed(w.shape) for w in reduces]
            + [picked(lift)],
            out_specs=fixed((length, model)),
            scratch_shapes=[pltpu.VMEM((lanes, model), bf16)],
        ),
        out_shape=result((length, model), bf16),
        cost_estimate=pl.CostEstimate(
            flops=2 * length * model * inner.shape[1], transcendentals=0,
            bytes_accessed=12 * 1024 * 1024,
        ),
        compiler_params=params(),
    )(meta, inner, n_r, *reduces, lift)


def attention_back(
    qrot, dop, mixed, kd, v0, v1, kt, bias, dq_t, dk, dv, rows, block, keys, log_scale, fresh,
):
    pairs = qrot.shape[1] // lanes
    share = pairs // 2
    lane = lane_of((block, lanes))
    queries = pl.ds(rows, block)

    def body(pair, carry):
        group = pair // share
        start = pl.multiple_of(pair * lanes, lanes)
        place = pl.ds(start, lanes)
        q = qrot[queries, place].astype(f32)
        up = dop[queries, place].astype(f32)
        mix = mixed[queries, place].astype(f32)
        k = kd[group, 0:keys, :]
        k_t = kt[group, :, 0:keys]
        dk_sum = dk[group, 0:keys, :]
        dv_sum = dv[group, 0:keys, :]
        for head, values in enumerate((v0, v1)):
            own = (lane < half) if head == 0 else (lane >= half)
            q_head = jnp.where(own, q, 0.0).astype(bf16)
            up_head = jnp.where(own, up, 0.0).astype(bf16)
            seen = jnp.where(own, up, mix).astype(bf16)
            e = jnp.exp2(nt(k, q_head) * log_scale + bias[0:keys, queries])
            ds = (e * nt(values[group, 0:keys, :], seen)).astype(bf16)
            dv_sum = dv_sum + nn(e.astype(bf16), up_head)
            dk_sum = dk_sum + nn(ds, q_head)
            piece = nn(k_t, ds)
            target = pl.ds(pl.multiple_of(start + head * half, half), half)
            if fresh:
                dq_t[target, queries] = piece
            else:
                dq_t[target, queries] += piece
        dk[group, 0:keys, :] = dk_sum
        dv[group, 0:keys, :] = dv_sum
        return carry

    lax.fori_loop(0, pairs, body, 0)


def fold_pairs(sums):
    lane = lane_of(sums.shape[1:])
    first = sums[0]
    second = sums[1]
    return jnp.where(lane < half, first + swap_halves(first), second + swap_halves(second))


def transposed_keys(kv, kt):
    key = kv[:, 0:lanes].astype(f32).T
    kt[0] = key[0:half].astype(bf16)
    kt[1] = key[half:].astype(bf16)


def far_kernel(
    meta, cot, summed, att, wide, inv, narrow, qrot, kv, segq, w0, w1, w2, w3, ao, bo,
    dop, mixed, dq_t, dkv, part_pack, full_pack,
    up, a_all, b_all, kd, v0, v1, kt, bias, dk, dv, *, log_scale, block,
):
    length = cot.shape[0]
    a_all[...] = jnp.zeros_like(a_all)
    b_all[...] = jnp.zeros_like(b_all)
    a_all[0:rank, :] = ao[0]
    b_all[0:rank, :] = bo[0]

    def body(index, carry):
        part_sum, full_sum = carry
        rows = pl.ds(pl.multiple_of(index * block, block), block)
        up[rows, :] = (cot[rows, :].astype(f32) + summed[rows, :].astype(f32)).astype(bf16)
        low = nt(up[rows, :], b_all[...])
        grad = nn(low.astype(bf16), a_all[...])
        for number, weight in enumerate((w0, w1, w2, w3)):
            columns = pl.ds(at(meta, number), weight.shape[1])
            grad = grad + nt(up[rows, columns], weight[...])
        scaled = (grad.astype(bf16).astype(f32) * inv[rows, :]).astype(bf16)
        dop[rows, :] = scaled
        inner = scaled.astype(f32) * wide[rows, :]
        for start in range(0, inner.shape[1], lanes):
            mixed[rows, start : start + lanes] = (
                -swap_halves(inner[:, start : start + lanes])
            ).astype(bf16)
        part_sum = part_sum + nn(low.T[0:rank].astype(bf16), att[rows, :])
        full_sum = full_sum + nn(narrow[rows, :].astype(f32).T[0:rank].astype(bf16), up[rows, :])
        return part_sum, full_sum

    part_sum, full_sum = lax.fori_loop(
        0,
        length // block,
        body,
        (jnp.zeros((rank, att.shape[1]), f32), jnp.zeros((rank, cot.shape[1]), f32)),
    )
    part_pack[...] = part_sum.astype(bf16)
    full_pack[...] = full_sum.astype(bf16)
    spread_keys(kv, kd, v0, v1, 0, length)
    transposed_keys(kv, kt)
    segk = jnp.where(meta[5] > 0, kv[:, 2 * lanes :].astype(f32)[:, 0:1], -1.0)
    bias[...] = jnp.where(segk == segq[...].astype(f32), 0.0, masked)
    dk[...] = jnp.zeros_like(dk)
    dv[...] = jnp.zeros_like(dv)
    for start in range(0, length, block):
        attention_back(
            qrot, dop, mixed, kd, v0, v1, kt, bias, dq_t, dk, dv, start, block, length, log_scale, True
        )
    dkv[:, 0:lanes] = (fold_pairs(dk[...]) * (half**-0.5)).astype(bf16)
    dkv[:, lanes:] = fold_pairs(dv[...]).astype(bf16)


def near_kernel(
    meta, dop, mixed, qrot, kv, segq, dq_far,
    dq_t, dkv, kd, v0, v1, kt, bias, dk, dv, *, log_scale, block,
):
    length = qrot.shape[0]
    spread_keys(kv, kd, v0, v1, 0, length)
    transposed_keys(kv, kt)
    key = lax.broadcasted_iota(jnp.int32, (length, length), 0)
    query = lax.broadcasted_iota(jnp.int32, (length, length), 1)
    segk = kv[:, 2 * lanes :].astype(f32)[:, 0:1]
    bias[...] = jnp.where((segk == segq[...].astype(f32)) & (key <= query), 0.0, masked)
    dk[...] = jnp.zeros_like(dk)
    dv[...] = jnp.zeros_like(dv)
    dq_t[...] = dq_far[...]
    for start in range(0, length, block):
        attention_back(
            qrot, dop, mixed, kd, v0, v1, kt, bias, dq_t, dk, dv, start, block, start + block,
            log_scale, False,
        )
    dkv[:, 0:lanes] = fold_pairs(dk[...]) * (half**-0.5)
    dkv[:, lanes:] = fold_pairs(dv[...])


def back_scratch(length):
    return [
        pltpu.VMEM((2, length, lanes), bf16),
        pltpu.VMEM((2, length, lanes), bf16),
        pltpu.VMEM((2, length, lanes), bf16),
        pltpu.VMEM((2, half, length), bf16),
        pltpu.VMEM((length, length), f32),
        pltpu.VMEM((2, length, lanes), f32),
        pltpu.VMEM((2, length, lanes), f32),
    ]


def attention_backward_far(
    meta, cot, summed, att, wide, inv, narrow, qrot, kv, segq, weights, down, lift, log_scale
):
    length, model = cot.shape
    q_width = qrot.shape[1]
    pick = lambda a: pl.BlockSpec(
        (1,) + a.shape[1:], lambda i, m: (m[7], 0, 0), pipeline_mode=pl.Buffered(1)
    )
    plain = (cot, summed, att, wide, inv, narrow, qrot, kv, segq, *weights)
    shapes = [
        result((length, q_width), bf16),
        result((length, q_width), bf16),
        result((q_width, length), f32),
        result((length, 2 * lanes), bf16),
        result((rank, q_width), bf16),
        result((rank, model), bf16),
    ]
    return pl.pallas_call(
        partial(far_kernel, log_scale=log_scale, block=256),
        name="attention_backward_far",
        grid_spec=pltpu.PrefetchScalarGridSpec(
            num_scalar_prefetch=1,
            grid=(1,),
            in_specs=[fixed(a.shape) for a in plain] + [pick(down), pick(lift)],
            out_specs=[fixed(s.shape) for s in shapes],
            scratch_shapes=[
                pltpu.VMEM((length, model), bf16),
                pltpu.VMEM((lanes, q_width), bf16),
                pltpu.VMEM((lanes, model), bf16),
            ]
            + back_scratch(length),
        ),
        out_shape=shapes,
        cost_estimate=pl.CostEstimate(
            flops=20 * length * length * q_width, transcendentals=length * length * 8,
            bytes_accessed=16 * 1024 * 1024,
        ),
        compiler_params=pltpu.CompilerParams(vmem_limit_bytes=vmem_bytes),
    )(meta, *plain, down, lift)


def attention_backward_near(meta, dop, mixed, qrot, kv, segq, dq_far, log_scale):
    length, q_width = qrot.shape
    plain = (dop, mixed, qrot, kv, segq, dq_far)
    shapes = [result((q_width, length), f32), result((length, 2 * lanes), f32)]
    return pl.pallas_call(
        partial(near_kernel, log_scale=log_scale, block=256),
        name="attention_backward_near",
        grid_spec=pltpu.PrefetchScalarGridSpec(
            num_scalar_prefetch=1,
            grid=(1,),
            in_specs=[fixed(a.shape) for a in plain],
            out_specs=[fixed(s.shape) for s in shapes],
            scratch_shapes=back_scratch(length),
        ),
        out_shape=shapes,
        cost_estimate=pl.CostEstimate(
            flops=20 * length * length * q_width, transcendentals=length * length * 8,
            bytes_accessed=6 * 1024 * 1024,
        ),
        compiler_params=pltpu.CompilerParams(vmem_limit_bytes=vmem_bytes),
    )(meta, *plain)


def qkv_grad_kernel(
    meta, normed, narrow, pre, dq_t, dkv_near, dkv_back, bq, bk, bv, qg, kg, cos, sin,
    grad, low_out, down_pack, q_lift, kv_lift, b_all, down_sum, lift_sum,
):
    q_width, kv_width = bq.shape[2], bk.shape[2]
    step = pl.program_id(0)

    @pl.when(step == 0)
    def _():
        b_all[...] = jnp.zeros_like(b_all)
        b_all[0:rank, 0:q_width] = bq[0]
        b_all[rank : 2 * rank, q_width : q_width + kv_width] = bk[0]
        b_all[2 * rank : 3 * rank, q_width + kv_width :] = bv[0]
        down_sum[...] = jnp.zeros_like(down_sum)
        lift_sum[...] = jnp.zeros_like(lift_sum)

    matrix = head_mean_matrix()
    dkv = dkv_near[...] + dkv_back[...].astype(f32)
    for start in range(0, q_width + kv_width, lanes):
        if start < q_width:
            upstream = dq_t[start : start + lanes, :].T * (half**-0.5)
        else:
            upstream = dkv[:, start - q_width : start - q_width + lanes]
        upstream = upstream * cos[...] - partner(upstream) * sin[...]
        value = pre[:, start : start + lanes]
        inverse = lax.rsqrt(head_mean(value * value, matrix) + epsilon)
        weighted = upstream * (qg if start < q_width else kg)[...]
        mean = head_mean(weighted * value, matrix)
        grad[:, start : start + lanes] = (
            inverse * weighted - value * (inverse * inverse * inverse * mean)
        ).astype(bf16)
    grad[:, q_width + kv_width :] = dkv[:, kv_width:].astype(bf16)
    own = grad[...]
    low = nt(own, b_all[...])
    low_out[...] = low.astype(bf16)
    down_sum[...] += nn(low.T[0 : 3 * rank].astype(bf16), normed[...])
    lift_sum[...] += nn(narrow[...].astype(f32).T[0 : 3 * rank].astype(bf16), own)

    @pl.when(step == pl.num_programs(0) - 1)
    def _():
        down_pack[...] = down_sum[...].astype(bf16)
        q_lift[...] = lift_sum[0:rank, 0:q_width].astype(bf16)
        kv_lift[:, 0:kv_width] = lift_sum[rank : 2 * rank, q_width : q_width + kv_width].astype(bf16)
        kv_lift[:, kv_width:] = lift_sum[2 * rank :, q_width + kv_width :].astype(bf16)


def qkv_grads(
    meta, normed, narrow, pre, dq_t, dkv_near, dkv_back, lifts, q_gain, k_gain, cos, sin
):
    length, width = normed.shape
    q_width, kv_width = lifts[0].shape[2], lifts[1].shape[2]
    every = q_width + 2 * kv_width
    block = 256
    tile = lambda w: pl.BlockSpec((block, w), lambda i, m: (i, 0))
    return pl.pallas_call(
        qkv_grad_kernel,
        name="qkv_grads",
        grid_spec=pltpu.PrefetchScalarGridSpec(
            num_scalar_prefetch=1,
            grid=(length // block,),
            in_specs=[
                tile(width), tile(lanes), tile(q_width + kv_width),
                pl.BlockSpec((q_width, block), lambda i, m: (0, i)), tile(2 * kv_width),
                tile(2 * kv_width),
            ]
            + [picked(a) for a in lifts]
            + [fixed(q_gain.shape), fixed(k_gain.shape), tile(lanes), tile(lanes)],
            out_specs=[
                tile(every), tile(lanes), fixed((3 * rank, width)), fixed((rank, q_width)),
                fixed((rank, 2 * kv_width)),
            ],
            scratch_shapes=[
                pltpu.VMEM((lanes, every), bf16),
                pltpu.VMEM((3 * rank, width), f32),
                pltpu.VMEM((3 * rank, every), f32),
            ],
        ),
        out_shape=[
            result((length, every), bf16),
            result((length, lanes), bf16),
            result((3 * rank, width), bf16),
            result((rank, q_width), bf16),
            result((rank, 2 * kv_width), bf16),
        ],
        cost_estimate=pl.CostEstimate(
            flops=2 * length * width * every // 8, transcendentals=0, bytes_accessed=8 * 1024 * 1024
        ),
        compiler_params=params(),
    )(
        meta, normed, narrow, pre, dq_t, dkv_near, dkv_back, *lifts, q_gain, k_gain, cos, sin
    )


def qkv_back_kernel(
    meta, hid, gain, grad, low, q0, q1, q2, q3, kv0, kv1, kv2, kv3, aq, ak, av, back, a_all, total,
):
    @pl.when(pl.program_id(0) == 0)
    def _():
        a_all[...] = jnp.zeros_like(a_all)
        a_all[0:rank, :] = aq[0]
        a_all[rank : 2 * rank, :] = ak[0]
        a_all[2 * rank : 3 * rank, :] = av[0]

    q_width = q0.shape[1]
    q_own, kv_own = grad[:, :q_width], grad[:, q_width:]
    for index, (q_weight, kv_weight) in enumerate(((q0, kv0), (q1, kv1), (q2, kv2), (q3, kv3))):
        columns = pl.ds(at(meta, index), q_weight.shape[0])
        total[:, columns] = (
            nt(q_own, q_weight[...]) + nt(kv_own, kv_weight[...]) + nn(low[...], a_all[:, columns])
        )
    wide = hid[...].astype(f32)
    inverse = lax.rsqrt(jnp.mean(wide * wide, axis=-1, keepdims=True) + epsilon)
    weighted = total[...] * gain[...].astype(f32)
    mean = jnp.mean(weighted * wide, axis=-1, keepdims=True)
    back[...] = (inverse * weighted - wide * (inverse * inverse * inverse * mean)).astype(bf16)


def qkv_backward(meta, hid, gain, grad, low, weights, downs):
    length, width = hid.shape
    every = grad.shape[1]
    block = 256
    tile = lambda w: pl.BlockSpec((block, w), lambda i, m: (i, 0))
    return pl.pallas_call(
        qkv_back_kernel,
        name="qkv_backward",
        grid_spec=pltpu.PrefetchScalarGridSpec(
            num_scalar_prefetch=1,
            grid=(length // block,),
            in_specs=[tile(width), fixed(gain.shape), tile(every), tile(lanes)]
            + [fixed(w.shape) for w in weights]
            + [picked(a) for a in downs],
            out_specs=tile(width),
            scratch_shapes=[pltpu.VMEM((lanes, width), bf16), pltpu.VMEM((block, width), f32)],
        ),
        out_shape=result((length, width), bf16),
        cost_estimate=pl.CostEstimate(
            flops=2 * length * width * every, transcendentals=0, bytes_accessed=8 * 1024 * 1024
        ),
        compiler_params=params(),
    )(meta, hid, gain, grad, low, *weights, *downs)


def place_kernel(sets, *refs, pieces):
    inputs = refs[: len(refs) - len(pieces)]
    outputs = refs[len(inputs) :]
    slots = outputs[0].shape[0]
    for out in outputs:
        out[...] = jnp.zeros_like(out)
    for sequence in range(inputs[0].shape[0]):
        slot = sets[sequence] - pl.program_id(0) * slots

        @pl.when((slot >= 0) & (slot < slots))
        def _():
            for (source, row, column), out in zip(pieces, outputs):
                piece = inputs[source][sequence, row : row + rank, column : column + out.shape[2]]
                out[slot] += piece.astype(f32)


def place_sets(sets, gathered, pieces, slots, weight):
    shapes = [result((slots, rank, width), f32) for _, _, _, width in pieces]
    return pl.pallas_call(
        partial(place_kernel, pieces=[p[:3] for p in pieces]),
        name="place_sets",
        grid_spec=pltpu.PrefetchScalarGridSpec(
            num_scalar_prefetch=1,
            grid=(2,),
            in_specs=[fixed(g.shape) for g in gathered],
            out_specs=[
                pl.BlockSpec((slots // 2,) + s.shape[1:], lambda i, m: (i, 0, 0)) for s in shapes
            ],
        ),
        out_shape=shapes,
        cost_estimate=pl.CostEstimate(flops=weight, transcendentals=0, bytes_accessed=8 * 1024 * 1024),
        compiler_params=params(),
    )(sets, *gathered)


def close_kernel(meta, first, second, reduced, out):
    out[...] = (
        first[...].astype(f32) + second[...].astype(f32) + reduced[...].astype(f32)
    ).astype(out.dtype)


def close(meta, first, second, reduced, dtype):
    length, width = reduced.shape
    block = 256
    columns = pl.BlockSpec((block, width), lambda i, m: (i, m[4]))
    tile = pl.BlockSpec((block, width), lambda i, m: (i, 0))
    return pl.pallas_call(
        close_kernel,
        name="close",
        grid_spec=pltpu.PrefetchScalarGridSpec(
            num_scalar_prefetch=1,
            grid=(length // block,),
            in_specs=[columns, columns, tile],
            out_specs=tile,
        ),
        out_shape=result(reduced.shape, dtype),
        cost_estimate=pl.CostEstimate(flops=0, transcendentals=0, bytes_accessed=4 * 1024 * 1024),
        compiler_params=params(),
    )(meta, first, second, reduced)


def flip(array, axis, bit):
    count = lax.axis_size(axis)
    return lax.ppermute(array, axis, [(i, i ^ bit) for i in range(count)])


def quarters(weight, axis):
    full = lax.all_gather(weight, "fsdp", axis=axis, tiled=True)
    return jnp.split(full, 4, axis=axis)


def after(array, *others):
    return lax.optimization_barrier((array, *others))[0]


def own_half(weight, axis):
    size = weight.shape[axis] // 2
    return lax.dynamic_slice_in_dim(weight, lax.axis_index("ctx") * size, size, axis)


def six_parts(weight, axis):
    shards = quarters(weight, axis)
    return shards[:2] + jnp.split(shards[2], 2, axis=axis) + jnp.split(shards[3], 2, axis=axis)


def shard_places(width, direct):
    unit = width // 4
    part = unit // 2
    if direct:
        four = [(lax.axis_index("fsdp") ^ bit) * unit for bit in range(4)]
        near = lax.axis_index("ctx") * part
    else:
        four, near = [0, unit, 2 * unit, 3 * unit], 0
    away = part - near
    return four, [four[0], four[1], four[2] + near, four[2] + away, four[3] + near, four[3] + away]


def pick_side(low, high, bit, axis):
    return jnp.where(
        bit == 0, jnp.concatenate([low, high], axis=axis), jnp.concatenate([high, low], axis=axis)
    )


def halve(array, axis, bit, stride):
    size = array.shape[-1] // 2
    keep = lax.dynamic_slice_in_dim(array, bit * size, size, array.ndim - 1)
    give = lax.dynamic_slice_in_dim(array, (1 - bit) * size, size, array.ndim - 1)
    taken = flip(give, axis, stride)
    return (keep.astype(f32) + taken.astype(f32)).astype(bf16)


def double(array, axis, bit, stride):
    taken = flip(array, axis, stride)
    return pick_side(array, taken, bit, array.ndim - 1)


def gather_sequences(full, part, *others):
    fsdp = lax.axis_size("fsdp")
    if fsdp != 4 or lax.axis_size("ctx") != 2 or lax.axis_size("tp") != 4:
        full = lax.psum(full, ("ctx", "tp"))
        part = [lax.psum(p, "ctx") for p in part]
        return (
            lax.all_gather(full, "fsdp", axis=0),
            [lax.all_gather(p, "fsdp", axis=0) for p in part],
        )
    own, side, place = lax.axis_index("fsdp"), lax.axis_index("ctx"), lax.axis_index("tp")
    full = halve(full, "ctx", side, 1)
    part = [halve(p, "ctx", side, 1) for p in part]
    full = halve(full, "tp", place % 2, 1)
    full = halve(full, "tp", place // 2, 2)

    def both(array, bit, stride):
        taken = flip(array, "fsdp", stride)
        return pick_side(array, taken, bit, 0)

    full = after(full, *others) if others else full
    full = both(full[None], own // 2, 2)
    part = [both(p[None], own // 2, 2) for p in part]
    full = double(full, "tp", place // 2, 2)
    full = double(full, "tp", place % 2, 1)
    full = double(full, "ctx", side, 1)
    part = [double(p, "ctx", side, 1) for p in part]

    def cores(array):
        taken = flip(array, "fsdp", 1)
        even = own % 2 == 0
        pairs = [jnp.where(even, array[i], taken[i]) for i in range(2)]
        others = [jnp.where(even, taken[i], array[i]) for i in range(2)]
        return jnp.stack([pairs[0], others[0], pairs[1], others[1]])

    return cores(full), [cores(p) for p in part]


def gather_ids(ids):
    if lax.axis_size("fsdp") != 4:
        return lax.all_gather(ids, "fsdp", tiled=True)
    own = lax.axis_index("fsdp")
    two = pick_side(ids, flip(ids, "fsdp", 1), own % 2, 0)
    return pick_side(two, flip(two, "fsdp", 2), own // 2, 0)


def on_device(
    hidden_in, segment_ids, adapter_ids, attention_gain, query_gain, key_gain, feedforward_gain,
    query_weight, key_weight, value_weight, output_weight, gate_weight, linear_weight, reduce_weight,
    query_down, query_lift, key_down, key_lift, value_down, value_lift, output_down, output_lift,
    gate_down, gate_lift, linear_down, linear_lift, reduce_down, reduce_lift, output_cotangent,
):
    _, length, model = hidden_in.shape
    head_dim = query_gain.shape[0]
    log_scale = head_dim**-0.5 * 1.4426950408889634
    context_index = lax.axis_index("ctx")
    tensor_index = lax.axis_index("tp")
    hid = hidden_in[0]
    cot = output_cotangent[0]
    direct = lax.axis_size("fsdp") == 4 and lax.axis_size("ctx") == 2
    four, six = shard_places(model, direct)
    values = (*four, tensor_index, context_index, 0, adapter_ids[0], *six, 0, 0)
    meta = jnp.stack([jnp.asarray(value, jnp.int32) for value in values])

    positions = (context_index * length + jnp.arange(length)).astype(f32)
    frequency = rope_base ** (-2.0 * jnp.arange(head_dim // 2).astype(f32) / head_dim)
    angles = positions[:, None] * frequency[None, :]
    cosine, sine = jnp.cos(angles), jnp.sin(angles)
    cos = jnp.concatenate([cosine] * 4, axis=1)
    sin = jnp.concatenate([-sine, sine] * 2, axis=1)
    q_gain = jnp.tile(query_gain.astype(f32), 2)[None]
    k_gain = jnp.tile(key_gain.astype(f32), 2)[None]
    a_gain = attention_gain[None]
    f_gain = feedforward_gain[None]
    seg_own = segment_ids.reshape(length, 1)
    count = lax.axis_size("ctx")
    onward = [(i, i + 1) for i in range(count - 1)]
    backward = [(i + 1, i) for i in range(count - 1)]
    turn = lambda table: jnp.swapaxes(table, 1, 2)
    qkv_downs = [turn(query_down), turn(key_down), turn(value_down)]
    qkv_lifts = [query_lift, key_lift, value_lift]
    output_first = turn(output_down)
    reduce_first = turn(reduce_down)

    kv_own = jnp.concatenate([key_weight, value_weight], axis=1)
    normed, qkv_narrow = attention_norm(meta, hid, a_gain, qkv_downs)
    if direct:
        q_across = flip(query_weight, "fsdp", 2)
        gate_half = own_half(gate_weight, 0)
        tables = (cos, sin, q_gain, k_gain, f_gain, seg_own, normed)
        kv_across = flip(after(kv_own, *tables), "fsdp", 2)
        cores = [flip(w, "fsdp", 1) for w in (gate_weight, linear_weight, reduce_weight)]
        q_side = flip(after(query_weight, q_across), "fsdp", 1)
        kv_side = flip(after(kv_own, kv_across), "fsdp", 1)
        qkv_weights = [
            query_weight, q_side, q_across,
            flip(after(q_across, *cores), "fsdp", 1),
            kv_own, kv_side, kv_across, flip(after(kv_across, *cores), "fsdp", 1),
        ]
        output_across = flip(after(output_weight, q_across, kv_across), "fsdp", 2)
        gate_across = flip(after(gate_half, q_across, kv_across), "fsdp", 2)
    else:
        qkv_weights = quarters(query_weight, 0) + quarters(kv_own, 0)
        output_weights = quarters(output_weight, 1)
        gates = six_parts(gate_weight, 0)
        linears = quarters(linear_weight, 0)
        reduces = quarters(reduce_weight, 1)

    pre, qrot, kv = qkv_forward(
        meta, normed, qkv_narrow, qkv_weights, qkv_lifts, q_gain, k_gain, cos, sin, seg_own
    )
    kv_far = lax.ppermute(kv, "ctx", onward)
    ready = after(qrot, gate_across) if direct else qrot
    att, wide, inv = attention_forward(meta, ready, kv_far, kv, log_scale)
    if direct:
        gate_other = flip(after(gate_across, att), "ctx", 1)
        linear_across = flip(after(linear_weight, att, output_across), "fsdp", 2)
        reduce_across = flip(after(reduce_weight, att, output_across), "fsdp", 2)
        output_weights = [
            output_weight, flip(after(output_weight, kv_far), "fsdp", 1), output_across,
            flip(after(output_across, kv_far), "fsdp", 1),
        ]
    branch, output_narrow = output_forward(meta, att, output_weights, output_first, output_lift)
    if direct:
        gates = [
            gate_weight, cores[0], gate_across, gate_other, flip(after(gate_across, gate_other), "fsdp", 1),
            flip(gate_other, "fsdp", 1),
        ]
        linears = [linear_weight, cores[1], linear_across, flip(linear_across, "fsdp", 1)]
        reduces = [reduce_weight, cores[2], reduce_across, flip(reduce_across, "fsdp", 1)]
    branch = lax.psum(branch, "tp")

    back, inner, gate_grad, linear_grad, n_gl_t, m_gl_t, m_r_t = ffn(
        meta, hid, branch, cot, f_gain, gates, linears, reduces,
        [turn(gate_down), turn(linear_down), reduce_first], [gate_lift, linear_lift, reduce_lift],
    )
    summed = lax.psum(back, "tp")
    ffn_part, ffn_full, n_r = ffn_adapters(
        meta, hid, branch, cot, f_gain, inner, gate_grad, linear_grad, n_gl_t, m_gl_t, m_r_t,
        reduce_first,
    )
    sets = gather_ids(after(adapter_ids, inner))
    slots = query_down.shape[0]
    ffn_full, (ffn_part,) = gather_sequences(ffn_full, [ffn_part])
    hidden = gate_lift.shape[2]
    ffn_pieces = [(0, rank * i, 0, model) for i in range(3)] + [(1, rank * i, 0, hidden) for i in range(3)]
    ffn_grads = place_sets(sets, [ffn_full, ffn_part], ffn_pieces, slots, 1024)
    out = reduce_forward(meta, inner, n_r, reduces, reduce_lift)
    out_columns = lax.psum_scatter(out, "tp", scatter_dimension=1, tiled=True)
    block_out = close(meta, hid, branch, out_columns, bf16)
    settled = after(summed, *ffn_grads)

    dop, mixed, dq_far, dkv_far, output_part, output_full = attention_backward_far(
        meta, cot, settled, att, wide, inv, output_narrow, qrot, kv_far, segment_ids,
        output_weights, output_first, output_lift, log_scale,
    )
    dkv_back = lax.ppermute(dkv_far, "ctx", backward)
    dq_t, dkv_near = attention_backward_near(
        meta, dop, mixed, qrot, kv, segment_ids, dq_far, log_scale
    )
    grad, low, qkv_full, q_part, kv_part = qkv_grads(
        meta, normed, qkv_narrow, pre, dq_t, dkv_near, dkv_back, qkv_lifts, q_gain, k_gain, cos, sin
    )
    last = qkv_backward(meta, hid, a_gain, grad, low, qkv_weights, qkv_downs)
    last_columns = lax.psum_scatter(last, "tp", scatter_dimension=1, tiled=True)
    input_grad = close(meta, cot, summed, last_columns, f32)

    q_width, kv_width = query_lift.shape[2], key_lift.shape[2]
    att_full, (att_part,) = gather_sequences(
        jnp.concatenate([qkv_full, output_full], axis=0),
        [jnp.concatenate([q_part, kv_part, output_part], axis=1)],
        block_out,
    )

    att_pieces = [(0, rank * i, 0, model) for i in range(4)] + [
        (1, 0, 0, q_width),
        (1, 0, q_width, kv_width),
        (1, 0, q_width + kv_width, kv_width),
        (1, 0, q_width + 2 * kv_width, q_width),
    ]
    att_grads = place_sets(sets, [att_full, att_part], att_pieces, slots, 1 << 33)
    return (
        block_out[None],
        input_grad[None],
        turn(att_grads[0]),
        att_grads[4],
        turn(att_grads[1]),
        att_grads[5],
        turn(att_grads[2]),
        att_grads[6],
        turn(att_grads[7]),
        att_grads[3],
        turn(ffn_grads[0]),
        ffn_grads[3],
        turn(ffn_grads[1]),
        ffn_grads[4],
        turn(ffn_grads[5]),
        ffn_grads[2],
    )


def solution(mesh):
    tokens = P("fsdp", "ctx", None)
    rows_split = P("fsdp", "tp")
    lift_split = P(None, None, "tp")
    down_split = P(None, "tp", None)
    in_specs = (
        tokens, P("fsdp", "ctx"), P("fsdp"), P(), P(), P(), P(),
        rows_split, rows_split, rows_split, P("tp", "fsdp"), rows_split, rows_split, P("tp", "fsdp"),
        P(), lift_split, P(), lift_split, P(), lift_split, down_split, P(),
        P(), lift_split, P(), lift_split, down_split, P(), tokens,
    )
    cut = P("fsdp", "ctx", "tp")
    out_specs = (
        cut, cut, P(), lift_split, P(), lift_split, P(), lift_split, down_split, P(),
        P(), lift_split, P(), lift_split, down_split, P(),
    )
    return jax.shard_map(
        on_device, mesh=mesh, in_specs=in_specs, out_specs=out_specs, check_vma=False
    )
```

```python
from functools import partial

import jax
import jax.numpy as jnp
from jax import lax
from jax.experimental import pallas as pl
from jax.experimental.pallas import tpu as pltpu
from jax.sharding import PartitionSpec as P

epsilon = 1e-05
rope_base = 1000000.0
masked = -1e30
f32 = jnp.float32
bf16 = jnp.bfloat16
lanes = 128
half = 64
rank = 16
vmem_bytes = 58 * 1024 * 1024


def nn(left, right):
    return lax.dot_general(left, right, (((1,), (0,)), ((), ())), preferred_element_type=f32)


def nt(left, right):
    return lax.dot_general(left, right, (((1,), (1,)), ((), ())), preferred_element_type=f32)


def at(ref, index):
    return pl.multiple_of(ref[index], lanes)


def fixed(shape):
    return pl.BlockSpec(shape, lambda *_: (0,) * len(shape), pipeline_mode=pl.Buffered(1))


def picked(array):
    return pl.BlockSpec(
        (1,) + array.shape[1:], lambda i, m: (m[7], 0, 0), pipeline_mode=pl.Buffered(1)
    )


def params():
    return pltpu.CompilerParams(vmem_limit_bytes=vmem_bytes)


def result(shape, dtype):
    return jax.ShapeDtypeStruct(shape, dtype)


def lane_of(shape):
    return lax.broadcasted_iota(jnp.int32, shape, len(shape) - 1)


def head_mean_matrix():
    row = lax.broadcasted_iota(jnp.int32, (lanes, lanes), 0)
    col = lax.broadcasted_iota(jnp.int32, (lanes, lanes), 1)
    return jnp.where((row // half) == (col // half), 1.0 / half, 0.0).astype(bf16)


def head_mean(values, matrix):
    high = values.astype(bf16)
    low = (values - high.astype(f32)).astype(bf16)
    return nn(high, matrix) + nn(low, matrix)


def partner(values):
    first = (lane_of(values.shape) % half) < (half // 2)
    return jnp.where(
        first,
        pltpu.roll(values, lanes - half // 2, values.ndim - 1),
        pltpu.roll(values, half // 2, values.ndim - 1),
    )


def swap_halves(values):
    return pltpu.roll(values, half, values.ndim - 1)


def norm_kernel(meta, hid, gain, aq, ak, av, normed, narrow, a_all):
    @pl.when(pl.program_id(0) == 0)
    def _():
        a_all[...] = jnp.zeros_like(a_all)
        a_all[0:rank, :] = aq[0]
        a_all[rank : 2 * rank, :] = ak[0]
        a_all[2 * rank : 3 * rank, :] = av[0]

    wide = hid[...].astype(f32)
    inverse = lax.rsqrt(jnp.mean(wide * wide, axis=-1, keepdims=True) + epsilon)
    normed[...] = (wide * inverse * gain[...].astype(f32)).astype(bf16)
    narrow[...] = nt(normed[...], a_all[...]).astype(bf16)


def attention_norm(meta, hid, gain, downs):
    length, width = hid.shape
    block = 128
    tile = lambda w: pl.BlockSpec((block, w), lambda i, m: (i, 0))
    return pl.pallas_call(
        norm_kernel,
        name="attention_norm",
        grid_spec=pltpu.PrefetchScalarGridSpec(
            num_scalar_prefetch=1,
            grid=(length // block,),
            in_specs=[tile(width), fixed(gain.shape)] + [picked(a) for a in downs],
            out_specs=[tile(width), tile(lanes)],
            scratch_shapes=[pltpu.VMEM((lanes, width), bf16)],
        ),
        out_shape=[result((length, width), bf16), result((length, lanes), bf16)],
        cost_estimate=pl.CostEstimate(flops=1024, transcendentals=0, bytes_accessed=1024),
        compiler_params=params(),
    )(meta, hid, gain, *downs)


def qkv_kernel(
    meta, normed, narrow, q0, q1, q2, q3, kv0, kv1, kv2, kv3, bq, bk, bv, qg, kg, cos, sin,
    seg, pre, qrot, kv, b_all,
):
    q_width, kv_width = bq.shape[2], bk.shape[2]

    @pl.when(pl.program_id(0) == 0)
    def _():
        b_all[...] = jnp.zeros_like(b_all)
        b_all[0:rank, 0:q_width] = bq[0]
        b_all[rank : 2 * rank, q_width : q_width + kv_width] = bk[0]
        b_all[2 * rank : 3 * rank, q_width + kv_width :] = bv[0]

    total = nn(narrow[...], b_all[...])
    q_total, kv_total = total[:, :q_width], total[:, q_width:]
    for index, (q_weight, kv_weight) in enumerate(((q0, kv0), (q1, kv1), (q2, kv2), (q3, kv3))):
        part = normed[:, pl.ds(at(meta, index), q_weight.shape[0])]
        q_total = q_total + nn(part, q_weight[...])
        kv_total = kv_total + nn(part, kv_weight[...])
    total = jnp.concatenate([q_total, kv_total], axis=1)
    pre[...] = total[:, : q_width + kv_width]
    matrix = head_mean_matrix()
    for start in range(0, q_width + kv_width, lanes):
        part = total[:, start : start + lanes]
        head_gain = qg if start < q_width else kg
        scaled = part * lax.rsqrt(head_mean(part * part, matrix) + epsilon) * head_gain[...]
        turned = (scaled * cos[...] + partner(scaled) * sin[...]).astype(bf16)
        if start < q_width:
            qrot[:, start : start + lanes] = turned
        else:
            kv[:, start - q_width : start - q_width + lanes] = turned
    kv[:, kv_width : 2 * kv_width] = total[:, q_width + kv_width :].astype(bf16)
    kv[:, 2 * kv_width :] = jnp.broadcast_to(seg[...].astype(f32), (seg.shape[0], lanes)).astype(bf16)


def qkv_forward(meta, normed, narrow, weights, lifts, q_gain, k_gain, cos, sin, seg):
    length, width = normed.shape
    q_width, kv_width = lifts[0].shape[2], lifts[1].shape[2]
    block = 256
    tile = lambda w: pl.BlockSpec((block, w), lambda i, m: (i, 0))
    return pl.pallas_call(
        qkv_kernel,
        name="qkv_forward",
        grid_spec=pltpu.PrefetchScalarGridSpec(
            num_scalar_prefetch=1,
            grid=(length // block,),
            in_specs=[tile(width), tile(lanes)]
            + [fixed(w.shape) for w in weights]
            + [picked(a) for a in lifts]
            + [fixed(q_gain.shape), fixed(k_gain.shape), tile(lanes), tile(lanes), tile(1)],
            out_specs=[tile(q_width + kv_width), tile(q_width), tile(2 * kv_width + lanes)],
            scratch_shapes=[pltpu.VMEM((lanes, q_width + 2 * kv_width), bf16)],
        ),
        out_shape=[
            result((length, q_width + kv_width), f32),
            result((length, q_width), bf16),
            result((length, 2 * kv_width + lanes), bf16),
        ],
        cost_estimate=pl.CostEstimate(flops=1024, transcendentals=0, bytes_accessed=1024),
        compiler_params=params(),
    )(meta, normed, narrow, *weights, *lifts, q_gain, k_gain, cos, sin, seg)


def spread_keys(kv, kd, v0, v1, rows, size):
    lane = lane_of((size, lanes))
    key = kv[:, 0:lanes].astype(f32)
    other = swap_halves(key)
    kd[0, rows : rows + size, :] = jnp.where(lane < half, key, other).astype(bf16)
    kd[1, rows : rows + size, :] = jnp.where(lane < half, other, key).astype(bf16)
    value = kv[:, lanes : 2 * lanes].astype(f32)
    other = swap_halves(value)
    v0[0, rows : rows + size, :] = jnp.where(lane < half, value, 1.0).astype(bf16)
    v0[1, rows : rows + size, :] = jnp.where(lane < half, other, 1.0).astype(bf16)
    v1[0, rows : rows + size, :] = jnp.where(lane < half, 1.0, other).astype(bf16)
    v1[1, rows : rows + size, :] = jnp.where(lane < half, 1.0, value).astype(bf16)


def attention_kernel(
    meta, qrot, kvf, kvn, kvq, att, wide, inv, kd, v0, v1, bias, segk, *, log_scale, block,
):
    far = kvf.shape[0]
    pairs = qrot.shape[1] // lanes
    share = pairs // 2
    step = pl.program_id(0)

    @pl.when(step == 0)
    def _():
        spread_keys(kvf, kd, v0, v1, 0, far)
        spread_keys(kvn, kd, v0, v1, far, kvn.shape[0])
        away = kvf[:, 2 * lanes :].astype(f32).T[0:8]
        segk[:, 0:far] = jnp.where(meta[5] > 0, away, -1.0)
        segk[:, far:] = kvn[:, 2 * lanes :].astype(f32).T[0:8]

    def queries(number):
        keys = far + (number + 1) * block
        key = lax.broadcasted_iota(jnp.int32, (block, keys), 1)
        query = lax.broadcasted_iota(jnp.int32, (block, keys), 0) + (far + number * block)
        segq = kvq[:, 2 * lanes :].astype(f32)[:, 0:1]
        allowed = (segq == segk[0:1, 0:keys]) & (key <= query)
        bias[:, 0:keys] = jnp.where(allowed, 0.0, masked)
        lane = lane_of((block, lanes))

        def body(pair, carry):
            group = pair // share
            place = pl.ds(pl.multiple_of(pair * lanes, lanes), lanes)
            q = qrot[:, place].astype(f32)
            q0 = jnp.where(lane < half, q, 0.0).astype(bf16)
            q1 = jnp.where(lane < half, 0.0, q).astype(bf16)
            k = kd[group, 0:keys, :]
            e0 = jnp.exp2(nt(q0, k) * log_scale + bias[:, 0:keys]).astype(bf16)
            r0 = nn(e0, v0[group, 0:keys, :])
            e1 = jnp.exp2(nt(q1, k) * log_scale + bias[:, 0:keys]).astype(bf16)
            r1 = nn(e1, v1[group, 0:keys, :])
            inverse = 1.0 / jnp.where(lane < half, swap_halves(r0), swap_halves(r1))
            out = jnp.where(lane < half, r0, r1) * inverse
            wide[:, place] = out
            inv[:, place] = inverse
            att[:, place] = out.astype(bf16)
            return carry

        lax.fori_loop(0, pairs, body, 0)

    for number in range(kvn.shape[0] // block):
        pl.when(step == number)(partial(queries, number))


def attention_forward(meta, qrot, kvf, kvn, log_scale):
    length, q_width = qrot.shape
    block = 256
    keys = kvf.shape[0] + length
    tile = lambda w: pl.BlockSpec((block, w), lambda i, m: (i, 0))
    return pl.pallas_call(
        partial(attention_kernel, log_scale=log_scale, block=block),
        name="attention_forward",
        grid_spec=pltpu.PrefetchScalarGridSpec(
            num_scalar_prefetch=1,
            grid=(length // block,),
            in_specs=[tile(q_width), fixed(kvf.shape), fixed(kvn.shape), tile(kvn.shape[1])],
            out_specs=[tile(q_width), tile(q_width), tile(q_width)],
            scratch_shapes=[
                pltpu.VMEM((2, keys, lanes), bf16),
                pltpu.VMEM((2, keys, lanes), bf16),
                pltpu.VMEM((2, keys, lanes), bf16),
                pltpu.VMEM((block, keys), f32),
                pltpu.VMEM((8, keys), f32),
            ],
        ),
        out_shape=[
            result((length, q_width), bf16),
            result((length, q_width), f32),
            result((length, q_width), f32),
        ],
        cost_estimate=pl.CostEstimate(
            flops=64 * length * keys * q_width, transcendentals=length * keys * 8,
            bytes_accessed=64 * 1024 * 1024,
        ),
        compiler_params=pltpu.CompilerParams(vmem_limit_bytes=vmem_bytes),
    )(meta, qrot, kvf, kvn, kvn)


def output_kernel(meta, att, w0, w1, w2, w3, ao, bo, branch, narrow, a_all, b_all):
    @pl.when(pl.program_id(0) == 0)
    def _():
        a_all[...] = jnp.zeros_like(a_all)
        b_all[...] = jnp.zeros_like(b_all)
        a_all[0:rank, :] = ao[0]
        b_all[0:rank, :] = bo[0]

    own = att[...]
    low = nt(own, a_all[...]).astype(bf16)
    narrow[...] = low
    for index, weight in enumerate((w0, w1, w2, w3)):
        columns = pl.ds(at(meta, index), weight.shape[1])
        branch[:, columns] = (nn(own, weight[...]) + nn(low, b_all[:, columns])).astype(bf16)


def output_forward(meta, att, weights, down, lift):
    length, q_width = att.shape
    model = lift.shape[2]
    block = 256
    tile = lambda w: pl.BlockSpec((block, w), lambda i, m: (i, 0))
    pick = lambda a: pl.BlockSpec(
        (1,) + a.shape[1:], lambda i, m: (m[7], 0, 0), pipeline_mode=pl.Buffered(1)
    )
    return pl.pallas_call(
        output_kernel,
        name="output_forward",
        grid_spec=pltpu.PrefetchScalarGridSpec(
            num_scalar_prefetch=1,
            grid=(length // block,),
            in_specs=[tile(q_width)] + [fixed(w.shape) for w in weights] + [pick(down), pick(lift)],
            out_specs=[tile(model), tile(lanes)],
            scratch_shapes=[pltpu.VMEM((lanes, q_width), bf16), pltpu.VMEM((lanes, model), bf16)],
        ),
        out_shape=[result((length, model), bf16), result((length, lanes), bf16)],
        cost_estimate=pl.CostEstimate(flops=1024, transcendentals=0, bytes_accessed=1024),
        compiler_params=pltpu.CompilerParams(vmem_limit_bytes=vmem_bytes),
    )(meta, att, *weights, down, lift)


def strip(array, width):
    return pl.BlockSpec((1, rank, width), lambda j, m: (m[7], 0, j))


def ffn_kernel(meta, hid, branch, cot, gain, *refs, shards, chunk):
    gates, linears, reduces = (refs[i:j] for i, j in zip((0,) + shards[:-1], shards))
    refs = refs[shards[-1] :]
    ag, al, ar, bg, bl, br = refs[:6]
    back, inner_out, gate_out, linear_out, n_gl_t, m_gl_t, m_r_t = refs[6:13]
    x, grad_sum, n_gl, m_gl, m_r, a_gl, b_r, b_g, b_l, a_r = refs[13:]
    step = pl.program_id(0)
    length = hid.shape[0]
    count = length // chunk

    def rows_of(index):
        return pl.ds(pl.multiple_of(index * chunk, chunk), chunk)

    def chunks(body):
        def run(index, carry):
            body(rows_of(index))
            return carry

        lax.fori_loop(0, count, run, 0)

    def normal(rows):
        middle = hid[rows, :].astype(f32) + branch[rows, :].astype(f32)
        inverse = lax.rsqrt(jnp.mean(middle * middle, axis=-1, keepdims=True) + epsilon)
        return middle, inverse

    @pl.when(step == 0)
    def _():
        for ref in (a_gl, b_r, b_g, b_l, a_r):
            ref[...] = jnp.zeros_like(ref)
        a_gl[0:rank, :] = ag[0]
        a_gl[rank : 2 * rank, :] = al[0]
        b_r[0:rank, :] = br[0]

        def body(rows):
            back_low = nt(cot[rows, :], b_r[...])
            m_r[rows, :] = back_low.astype(bf16)
            m_r_t[:, rows] = back_low.T[0:rank].astype(bf16)
            middle, inverse = normal(rows)
            x[rows, :] = (middle * inverse * gain[...].astype(f32)).astype(bf16)
            low = nt(x[rows, :], a_gl[...])
            n_gl[rows, :] = low.astype(bf16)
            n_gl_t[:, rows] = low.T[0 : 2 * rank].astype(bf16)
            m_gl[rows, :] = jnp.zeros((chunk, lanes), f32)

        chunks(body)

    b_g[0:rank, :] = bg[0]
    b_l[rank : 2 * rank, :] = bl[0]
    a_r[0:rank, :] = ar[0]

    def place(index, weight, axis):
        return pl.ds(at(meta, index), weight.shape[axis])

    def body(rows, first):
        low = n_gl[rows, :]
        gate = nn(low, b_g[...])
        linear = nn(low, b_l[...])
        for index, weight in enumerate(gates):
            gate = gate + nn(x[rows, place(8 + index, weight, 0)], weight[...])
        for index, weight in enumerate(linears):
            linear = linear + nn(x[rows, place(index, weight, 0)], weight[...])
        upstream = nn(m_r[rows, :], a_r[...])
        for index, weight in enumerate(reduces):
            upstream = upstream + nt(cot[rows, place(index, weight, 1)], weight[...])
        sigmoid = jax.nn.sigmoid(gate)
        active = gate * sigmoid
        gate_grad = (upstream * linear * sigmoid * (1.0 + gate * (1.0 - sigmoid))).astype(bf16)
        linear_grad = (upstream * active).astype(bf16)
        inner_out[rows, :] = (active * linear).astype(bf16)
        gate_out[rows, :] = gate_grad
        linear_out[rows, :] = linear_grad
        m_gl[rows, :] += nt(gate_grad, b_g[...]) + nt(linear_grad, b_l[...])
        for index, weight in enumerate(linears):
            columns = place(index, weight, 0)
            backward = nt(linear_grad, weight[...])
            if first:
                grad_sum[rows, columns] = backward
            else:
                grad_sum[rows, columns] += backward
        for index, weight in enumerate(gates):
            grad_sum[rows, place(8 + index, weight, 0)] += nt(gate_grad, weight[...])

    pl.when(step == 0)(partial(chunks, partial(body, first=True)))
    pl.when(step > 0)(partial(chunks, partial(body, first=False)))

    @pl.when(step == pl.num_programs(0) - 1)
    def _():
        def finish(rows):
            upstream = grad_sum[rows, :] + nn(m_gl[rows, :].astype(bf16), a_gl[...])
            middle, inverse = normal(rows)
            weighted = upstream * gain[...].astype(f32)
            mean = jnp.mean(weighted * middle, axis=-1, keepdims=True)
            back[rows, :] = (
                inverse * weighted - middle * (inverse * inverse * inverse * mean)
            ).astype(bf16)

        chunks(finish)
        m_gl_t[...] = m_gl[...].T[0 : 2 * rank].astype(bf16)


def ffn(
    meta, hid, branch, cot, gain, gates, linears, reduces, downs, lifts, width=512, chunk=512
):
    length, model = hid.shape
    hidden = gates[0].shape[1]
    rows = [*gates, *linears]
    shards = (len(gates), len(rows), len(rows) + len(reduces))
    column = lambda: pl.BlockSpec((length, width), lambda j, m: (0, j))
    return pl.pallas_call(
        partial(ffn_kernel, shards=shards, chunk=chunk),
        name="feed_forward",
        grid_spec=pltpu.PrefetchScalarGridSpec(
            num_scalar_prefetch=1,
            grid=(hidden // width,),
            in_specs=[fixed(hid.shape), fixed(branch.shape), fixed(cot.shape), fixed(gain.shape)]
            + [pl.BlockSpec((w.shape[0], width), lambda j, m: (0, j)) for w in rows]
            + [pl.BlockSpec((width, w.shape[1]), lambda j, m: (j, 0)) for w in reduces]
            + [picked(downs[0]), picked(downs[1]), strip(downs[2], width)]
            + [strip(lifts[0], width), strip(lifts[1], width), picked(lifts[2])],
            out_specs=[
                fixed((length, model)), column(), column(), column(),
                fixed((2 * rank, length)), fixed((2 * rank, length)), fixed((rank, length)),
            ],
            scratch_shapes=[
                pltpu.VMEM((length, model), bf16),
                pltpu.VMEM((length, model), f32),
                pltpu.VMEM((length, lanes), bf16),
                pltpu.VMEM((length, lanes), f32),
                pltpu.VMEM((length, lanes), bf16),
                pltpu.VMEM((lanes, model), bf16),
                pltpu.VMEM((lanes, model), bf16),
                pltpu.VMEM((lanes, width), bf16),
                pltpu.VMEM((lanes, width), bf16),
                pltpu.VMEM((lanes, width), bf16),
            ],
        ),
        out_shape=[result((length, model), bf16)]
        + [result((length, hidden), bf16)] * 3
        + [result((2 * rank, length), bf16)] * 2
        + [result((rank, length), bf16)],
        cost_estimate=pl.CostEstimate(
            flops=8 * length * model * hidden, transcendentals=length * hidden,
            bytes_accessed=4 * model * hidden + 14 * length * model,
        ),
        compiler_params=params(),
    )(meta, hid, branch, cot, gain, *rows, *reduces, *downs, *lifts)


def ffn_adapter_kernel(
    meta, hid, branch, cot, gain, inner, gate_grad, linear_grad, n_gl_t, m_gl_t, m_r_t, ar,
    part_pack, full_pack, n_r, low_sum, a_r,
):
    step = pl.program_id(0)

    @pl.when(step == 0)
    def _():
        a_r[...] = jnp.zeros_like(a_r)
        low_sum[...] = jnp.zeros_like(low_sum)

    a_r[0:rank, :] = ar[0]
    part_pack[0:rank, :] = nn(n_gl_t[...], gate_grad[...])[0:rank].astype(bf16)
    part_pack[rank : 2 * rank, :] = nn(n_gl_t[...], linear_grad[...])[rank:].astype(bf16)
    part_pack[2 * rank :, :] = nn(m_r_t[...], inner[...]).astype(bf16)
    low_sum[...] += nt(inner[...], a_r[...])

    @pl.when(step == pl.num_programs(0) - 1)
    def _():
        low = low_sum[...]
        n_r[...] = low.astype(bf16)
        full_pack[2 * rank :, :] = nn(low.T[0:rank].astype(bf16), cot[...]).astype(bf16)
        middle = hid[...].astype(f32) + branch[...].astype(f32)
        inverse = lax.rsqrt(jnp.mean(middle * middle, axis=-1, keepdims=True) + epsilon)
        x = (middle * inverse * gain[...].astype(f32)).astype(bf16)
        full_pack[0 : 2 * rank, :] = nn(m_gl_t[...], x).astype(bf16)


def ffn_adapters(meta, hid, branch, cot, gain, inner, gate_grad, linear_grad, n_gl_t, m_gl_t, m_r_t, down):
    length, model = hid.shape
    hidden = inner.shape[1]
    width = 512
    column = lambda: pl.BlockSpec((length, width), lambda j, m: (0, j))
    return pl.pallas_call(
        ffn_adapter_kernel,
        name="feed_forward_adapters",
        grid_spec=pltpu.PrefetchScalarGridSpec(
            num_scalar_prefetch=1,
            grid=(hidden // width,),
            in_specs=[fixed(hid.shape), fixed(branch.shape), fixed(cot.shape), fixed(gain.shape)]
            + [column(), column(), column()]
            + [fixed(n_gl_t.shape), fixed(m_gl_t.shape), fixed(m_r_t.shape), strip(down, width)],
            out_specs=[
                pl.BlockSpec((3 * rank, width), lambda j, m: (0, j)),
                fixed((3 * rank, model)),
                fixed((length, lanes)),
            ],
            scratch_shapes=[pltpu.VMEM((length, lanes), f32), pltpu.VMEM((lanes, width), bf16)],
        ),
        out_shape=[
            result((3 * rank, hidden), bf16),
            result((3 * rank, model), bf16),
            result((length, lanes), bf16),
        ],
        cost_estimate=pl.CostEstimate(
            flops=512 * length * hidden, transcendentals=0, bytes_accessed=12 * length * model
        ),
        compiler_params=params(),
    )(meta, hid, branch, cot, gain, inner, gate_grad, linear_grad, n_gl_t, m_gl_t, m_r_t, down)


def reduce_kernel(meta, inner, n_r, *refs):
    *weights, br, out, b_r = refs
    b_r[...] = jnp.zeros_like(b_r)
    b_r[0:rank, :] = br[0]
    for index, weight in enumerate(weights):
        columns = pl.ds(at(meta, index), weight.shape[1])
        out[:, columns] = (nn(inner[...], weight[...]) + nn(n_r[...], b_r[:, columns])).astype(bf16)


def reduce_forward(meta, inner, n_r, reduces, lift):
    length = inner.shape[0]
    model = lift.shape[2]
    return pl.pallas_call(
        reduce_kernel,
        name="reduce_forward",
        grid_spec=pltpu.PrefetchScalarGridSpec(
            num_scalar_prefetch=1,
            grid=(1,),
            in_specs=[fixed(inner.shape), fixed(n_r.shape)]
            + [fixed(w.shape) for w in reduces]
            + [picked(lift)],
            out_specs=fixed((length, model)),
            scratch_shapes=[pltpu.VMEM((lanes, model), bf16)],
        ),
        out_shape=result((length, model), bf16),
        cost_estimate=pl.CostEstimate(
            flops=2 * length * model * inner.shape[1], transcendentals=0,
            bytes_accessed=12 * 1024 * 1024,
        ),
        compiler_params=params(),
    )(meta, inner, n_r, *reduces, lift)


def attention_back(
    qrot, dop, mixed, kd, v0, v1, kt, bias, dq_t, dk, dv, rows, block, keys, log_scale, fresh,
):
    pairs = qrot.shape[1] // lanes
    share = pairs // 2
    lane = lane_of((block, lanes))
    queries = pl.ds(rows, block)

    def body(pair, carry):
        group = pair // share
        start = pl.multiple_of(pair * lanes, lanes)
        place = pl.ds(start, lanes)
        q = qrot[queries, place].astype(f32)
        up = dop[queries, place].astype(f32)
        mix = mixed[queries, place].astype(f32)
        k = kd[group, 0:keys, :]
        k_t = kt[group, :, 0:keys]
        dk_sum = dk[group, 0:keys, :]
        dv_sum = dv[group, 0:keys, :]
        for head, values in enumerate((v0, v1)):
            own = (lane < half) if head == 0 else (lane >= half)
            q_head = jnp.where(own, q, 0.0).astype(bf16)
            up_head = jnp.where(own, up, 0.0).astype(bf16)
            seen = jnp.where(own, up, mix).astype(bf16)
            e = jnp.exp2(nt(k, q_head) * log_scale + bias[0:keys, queries])
            ds = (e * nt(values[group, 0:keys, :], seen)).astype(bf16)
            dv_sum = dv_sum + nn(e.astype(bf16), up_head)
            dk_sum = dk_sum + nn(ds, q_head)
            piece = nn(k_t, ds)
            target = pl.ds(pl.multiple_of(start + head * half, half), half)
            if fresh:
                dq_t[target, queries] = piece
            else:
                dq_t[target, queries] += piece
        dk[group, 0:keys, :] = dk_sum
        dv[group, 0:keys, :] = dv_sum
        return carry

    lax.fori_loop(0, pairs, body, 0)


def fold_pairs(sums):
    lane = lane_of(sums.shape[1:])
    first = sums[0]
    second = sums[1]
    return jnp.where(lane < half, first + swap_halves(first), second + swap_halves(second))


def transposed_keys(kv, kt):
    key = kv[:, 0:lanes].astype(f32).T
    kt[0] = key[0:half].astype(bf16)
    kt[1] = key[half:].astype(bf16)


def far_kernel(
    meta, cot, summed, att, wide, inv, narrow, qrot, kv, segq, w0, w1, w2, w3, ao, bo,
    dop, mixed, dq_t, dkv, part_pack, full_pack,
    up, a_all, b_all, kd, v0, v1, kt, bias, dk, dv, *, log_scale, block,
):
    length = cot.shape[0]
    a_all[...] = jnp.zeros_like(a_all)
    b_all[...] = jnp.zeros_like(b_all)
    a_all[0:rank, :] = ao[0]
    b_all[0:rank, :] = bo[0]

    def body(index, carry):
        part_sum, full_sum = carry
        rows = pl.ds(pl.multiple_of(index * block, block), block)
        up[rows, :] = (cot[rows, :].astype(f32) + summed[rows, :].astype(f32)).astype(bf16)
        low = nt(up[rows, :], b_all[...])
        grad = nn(low.astype(bf16), a_all[...])
        for number, weight in enumerate((w0, w1, w2, w3)):
            columns = pl.ds(at(meta, number), weight.shape[1])
            grad = grad + nt(up[rows, columns], weight[...])
        scaled = (grad.astype(bf16).astype(f32) * inv[rows, :]).astype(bf16)
        dop[rows, :] = scaled
        inner = scaled.astype(f32) * wide[rows, :]
        for start in range(0, inner.shape[1], lanes):
            mixed[rows, start : start + lanes] = (
                -swap_halves(inner[:, start : start + lanes])
            ).astype(bf16)
        part_sum = part_sum + nn(low.T[0:rank].astype(bf16), att[rows, :])
        full_sum = full_sum + nn(narrow[rows, :].astype(f32).T[0:rank].astype(bf16), up[rows, :])
        return part_sum, full_sum

    part_sum, full_sum = lax.fori_loop(
        0,
        length // block,
        body,
        (jnp.zeros((rank, att.shape[1]), f32), jnp.zeros((rank, cot.shape[1]), f32)),
    )
    part_pack[...] = part_sum.astype(bf16)
    full_pack[...] = full_sum.astype(bf16)
    spread_keys(kv, kd, v0, v1, 0, length)
    transposed_keys(kv, kt)
    segk = jnp.where(meta[5] > 0, kv[:, 2 * lanes :].astype(f32)[:, 0:1], -1.0)
    bias[...] = jnp.where(segk == segq[...].astype(f32), 0.0, masked)
    dk[...] = jnp.zeros_like(dk)
    dv[...] = jnp.zeros_like(dv)
    for start in range(0, length, block):
        attention_back(
            qrot, dop, mixed, kd, v0, v1, kt, bias, dq_t, dk, dv, start, block, length, log_scale, True
        )
    dkv[:, 0:lanes] = (fold_pairs(dk[...]) * (half**-0.5)).astype(bf16)
    dkv[:, lanes:] = fold_pairs(dv[...]).astype(bf16)


def near_kernel(
    meta, dop, mixed, qrot, kv, segq, dq_far,
    dq_t, dkv, kd, v0, v1, kt, bias, dk, dv, *, log_scale, block,
):
    length = qrot.shape[0]
    spread_keys(kv, kd, v0, v1, 0, length)
    transposed_keys(kv, kt)
    key = lax.broadcasted_iota(jnp.int32, (length, length), 0)
    query = lax.broadcasted_iota(jnp.int32, (length, length), 1)
    segk = kv[:, 2 * lanes :].astype(f32)[:, 0:1]
    bias[...] = jnp.where((segk == segq[...].astype(f32)) & (key <= query), 0.0, masked)
    dk[...] = jnp.zeros_like(dk)
    dv[...] = jnp.zeros_like(dv)
    dq_t[...] = dq_far[...]
    for start in range(0, length, block):
        attention_back(
            qrot, dop, mixed, kd, v0, v1, kt, bias, dq_t, dk, dv, start, block, start + block,
            log_scale, False,
        )
    dkv[:, 0:lanes] = fold_pairs(dk[...]) * (half**-0.5)
    dkv[:, lanes:] = fold_pairs(dv[...])


def back_scratch(length):
    return [
        pltpu.VMEM((2, length, lanes), bf16),
        pltpu.VMEM((2, length, lanes), bf16),
        pltpu.VMEM((2, length, lanes), bf16),
        pltpu.VMEM((2, half, length), bf16),
        pltpu.VMEM((length, length), f32),
        pltpu.VMEM((2, length, lanes), f32),
        pltpu.VMEM((2, length, lanes), f32),
    ]


def attention_backward_far(
    meta, cot, summed, att, wide, inv, narrow, qrot, kv, segq, weights, down, lift, log_scale
):
    length, model = cot.shape
    q_width = qrot.shape[1]
    pick = lambda a: pl.BlockSpec(
        (1,) + a.shape[1:], lambda i, m: (m[7], 0, 0), pipeline_mode=pl.Buffered(1)
    )
    plain = (cot, summed, att, wide, inv, narrow, qrot, kv, segq, *weights)
    shapes = [
        result((length, q_width), bf16),
        result((length, q_width), bf16),
        result((q_width, length), f32),
        result((length, 2 * lanes), bf16),
        result((rank, q_width), bf16),
        result((rank, model), bf16),
    ]
    return pl.pallas_call(
        partial(far_kernel, log_scale=log_scale, block=256),
        name="attention_backward_far",
        grid_spec=pltpu.PrefetchScalarGridSpec(
            num_scalar_prefetch=1,
            grid=(1,),
            in_specs=[fixed(a.shape) for a in plain] + [pick(down), pick(lift)],
            out_specs=[fixed(s.shape) for s in shapes],
            scratch_shapes=[
                pltpu.VMEM((length, model), bf16),
                pltpu.VMEM((lanes, q_width), bf16),
                pltpu.VMEM((lanes, model), bf16),
            ]
            + back_scratch(length),
        ),
        out_shape=shapes,
        cost_estimate=pl.CostEstimate(
            flops=20 * length * length * q_width, transcendentals=length * length * 8,
            bytes_accessed=16 * 1024 * 1024,
        ),
        compiler_params=pltpu.CompilerParams(vmem_limit_bytes=vmem_bytes),
    )(meta, *plain, down, lift)


def attention_backward_near(meta, dop, mixed, qrot, kv, segq, dq_far, log_scale):
    length, q_width = qrot.shape
    plain = (dop, mixed, qrot, kv, segq, dq_far)
    shapes = [result((q_width, length), f32), result((length, 2 * lanes), f32)]
    return pl.pallas_call(
        partial(near_kernel, log_scale=log_scale, block=256),
        name="attention_backward_near",
        grid_spec=pltpu.PrefetchScalarGridSpec(
            num_scalar_prefetch=1,
            grid=(1,),
            in_specs=[fixed(a.shape) for a in plain],
            out_specs=[fixed(s.shape) for s in shapes],
            scratch_shapes=back_scratch(length),
        ),
        out_shape=shapes,
        cost_estimate=pl.CostEstimate(
            flops=20 * length * length * q_width, transcendentals=length * length * 8,
            bytes_accessed=6 * 1024 * 1024,
        ),
        compiler_params=pltpu.CompilerParams(vmem_limit_bytes=vmem_bytes),
    )(meta, *plain)


def qkv_grad_kernel(
    meta, normed, narrow, pre, dq_t, dkv_near, dkv_back, bq, bk, bv, qg, kg, cos, sin,
    grad, low_out, down_pack, q_lift, kv_lift, b_all, down_sum, lift_sum,
):
    q_width, kv_width = bq.shape[2], bk.shape[2]
    step = pl.program_id(0)

    @pl.when(step == 0)
    def _():
        b_all[...] = jnp.zeros_like(b_all)
        b_all[0:rank, 0:q_width] = bq[0]
        b_all[rank : 2 * rank, q_width : q_width + kv_width] = bk[0]
        b_all[2 * rank : 3 * rank, q_width + kv_width :] = bv[0]
        down_sum[...] = jnp.zeros_like(down_sum)
        lift_sum[...] = jnp.zeros_like(lift_sum)

    matrix = head_mean_matrix()
    dkv = dkv_near[...] + dkv_back[...].astype(f32)
    for start in range(0, q_width + kv_width, lanes):
        if start < q_width:
            upstream = dq_t[start : start + lanes, :].T * (half**-0.5)
        else:
            upstream = dkv[:, start - q_width : start - q_width + lanes]
        upstream = upstream * cos[...] - partner(upstream) * sin[...]
        value = pre[:, start : start + lanes]
        inverse = lax.rsqrt(head_mean(value * value, matrix) + epsilon)
        weighted = upstream * (qg if start < q_width else kg)[...]
        mean = head_mean(weighted * value, matrix)
        grad[:, start : start + lanes] = (
            inverse * weighted - value * (inverse * inverse * inverse * mean)
        ).astype(bf16)
    grad[:, q_width + kv_width :] = dkv[:, kv_width:].astype(bf16)
    own = grad[...]
    low = nt(own, b_all[...])
    low_out[...] = low.astype(bf16)
    down_sum[...] += nn(low.T[0 : 3 * rank].astype(bf16), normed[...])
    lift_sum[...] += nn(narrow[...].astype(f32).T[0 : 3 * rank].astype(bf16), own)

    @pl.when(step == pl.num_programs(0) - 1)
    def _():
        down_pack[...] = down_sum[...].astype(bf16)
        q_lift[...] = lift_sum[0:rank, 0:q_width].astype(bf16)
        kv_lift[:, 0:kv_width] = lift_sum[rank : 2 * rank, q_width : q_width + kv_width].astype(bf16)
        kv_lift[:, kv_width:] = lift_sum[2 * rank :, q_width + kv_width :].astype(bf16)


def qkv_grads(
    meta, normed, narrow, pre, dq_t, dkv_near, dkv_back, lifts, q_gain, k_gain, cos, sin
):
    length, width = normed.shape
    q_width, kv_width = lifts[0].shape[2], lifts[1].shape[2]
    every = q_width + 2 * kv_width
    block = 256
    tile = lambda w: pl.BlockSpec((block, w), lambda i, m: (i, 0))
    return pl.pallas_call(
        qkv_grad_kernel,
        name="qkv_grads",
        grid_spec=pltpu.PrefetchScalarGridSpec(
            num_scalar_prefetch=1,
            grid=(length // block,),
            in_specs=[
                tile(width), tile(lanes), tile(q_width + kv_width),
                pl.BlockSpec((q_width, block), lambda i, m: (0, i)), tile(2 * kv_width),
                tile(2 * kv_width),
            ]
            + [picked(a) for a in lifts]
            + [fixed(q_gain.shape), fixed(k_gain.shape), tile(lanes), tile(lanes)],
            out_specs=[
                tile(every), tile(lanes), fixed((3 * rank, width)), fixed((rank, q_width)),
                fixed((rank, 2 * kv_width)),
            ],
            scratch_shapes=[
                pltpu.VMEM((lanes, every), bf16),
                pltpu.VMEM((3 * rank, width), f32),
                pltpu.VMEM((3 * rank, every), f32),
            ],
        ),
        out_shape=[
            result((length, every), bf16),
            result((length, lanes), bf16),
            result((3 * rank, width), bf16),
            result((rank, q_width), bf16),
            result((rank, 2 * kv_width), bf16),
        ],
        cost_estimate=pl.CostEstimate(
            flops=2 * length * width * every // 8, transcendentals=0, bytes_accessed=8 * 1024 * 1024
        ),
        compiler_params=params(),
    )(
        meta, normed, narrow, pre, dq_t, dkv_near, dkv_back, *lifts, q_gain, k_gain, cos, sin
    )


def qkv_back_kernel(
    meta, hid, gain, grad, low, q0, q1, q2, q3, kv0, kv1, kv2, kv3, aq, ak, av, back, a_all, total,
):
    @pl.when(pl.program_id(0) == 0)
    def _():
        a_all[...] = jnp.zeros_like(a_all)
        a_all[0:rank, :] = aq[0]
        a_all[rank : 2 * rank, :] = ak[0]
        a_all[2 * rank : 3 * rank, :] = av[0]

    q_width = q0.shape[1]
    q_own, kv_own = grad[:, :q_width], grad[:, q_width:]
    for index, (q_weight, kv_weight) in enumerate(((q0, kv0), (q1, kv1), (q2, kv2), (q3, kv3))):
        columns = pl.ds(at(meta, index), q_weight.shape[0])
        total[:, columns] = (
            nt(q_own, q_weight[...]) + nt(kv_own, kv_weight[...]) + nn(low[...], a_all[:, columns])
        )
    wide = hid[...].astype(f32)
    inverse = lax.rsqrt(jnp.mean(wide * wide, axis=-1, keepdims=True) + epsilon)
    weighted = total[...] * gain[...].astype(f32)
    mean = jnp.mean(weighted * wide, axis=-1, keepdims=True)
    back[...] = (inverse * weighted - wide * (inverse * inverse * inverse * mean)).astype(bf16)


def qkv_backward(meta, hid, gain, grad, low, weights, downs):
    length, width = hid.shape
    every = grad.shape[1]
    block = 256
    tile = lambda w: pl.BlockSpec((block, w), lambda i, m: (i, 0))
    return pl.pallas_call(
        qkv_back_kernel,
        name="qkv_backward",
        grid_spec=pltpu.PrefetchScalarGridSpec(
            num_scalar_prefetch=1,
            grid=(length // block,),
            in_specs=[tile(width), fixed(gain.shape), tile(every), tile(lanes)]
            + [fixed(w.shape) for w in weights]
            + [picked(a) for a in downs],
            out_specs=tile(width),
            scratch_shapes=[pltpu.VMEM((lanes, width), bf16), pltpu.VMEM((block, width), f32)],
        ),
        out_shape=result((length, width), bf16),
        cost_estimate=pl.CostEstimate(
            flops=2 * length * width * every, transcendentals=0, bytes_accessed=8 * 1024 * 1024
        ),
        compiler_params=params(),
    )(meta, hid, gain, grad, low, *weights, *downs)


def place_kernel(sets, *refs, pieces):
    inputs = refs[: len(refs) - len(pieces)]
    outputs = refs[len(inputs) :]
    slots = outputs[0].shape[0]
    for out in outputs:
        out[...] = jnp.zeros_like(out)
    for sequence in range(inputs[0].shape[0]):
        slot = sets[sequence] - pl.program_id(0) * slots

        @pl.when((slot >= 0) & (slot < slots))
        def _():
            for (source, row, column), out in zip(pieces, outputs):
                piece = inputs[source][sequence, row : row + rank, column : column + out.shape[2]]
                out[slot] += piece.astype(f32)


def place_sets(sets, gathered, pieces, slots, weight):
    shapes = [result((slots, rank, width), f32) for _, _, _, width in pieces]
    return pl.pallas_call(
        partial(place_kernel, pieces=[p[:3] for p in pieces]),
        name="place_sets",
        grid_spec=pltpu.PrefetchScalarGridSpec(
            num_scalar_prefetch=1,
            grid=(2,),
            in_specs=[fixed(g.shape) for g in gathered],
            out_specs=[
                pl.BlockSpec((slots // 2,) + s.shape[1:], lambda i, m: (i, 0, 0)) for s in shapes
            ],
        ),
        out_shape=shapes,
        cost_estimate=pl.CostEstimate(flops=weight, transcendentals=0, bytes_accessed=8 * 1024 * 1024),
        compiler_params=params(),
    )(sets, *gathered)


def close_kernel(meta, first, second, reduced, out):
    out[...] = (
        first[...].astype(f32) + second[...].astype(f32) + reduced[...].astype(f32)
    ).astype(out.dtype)


def close(meta, first, second, reduced, dtype):
    length, width = reduced.shape
    block = 256
    columns = pl.BlockSpec((block, width), lambda i, m: (i, m[4]))
    tile = pl.BlockSpec((block, width), lambda i, m: (i, 0))
    return pl.pallas_call(
        close_kernel,
        name="close",
        grid_spec=pltpu.PrefetchScalarGridSpec(
            num_scalar_prefetch=1,
            grid=(length // block,),
            in_specs=[columns, columns, tile],
            out_specs=tile,
        ),
        out_shape=result(reduced.shape, dtype),
        cost_estimate=pl.CostEstimate(flops=0, transcendentals=0, bytes_accessed=4 * 1024 * 1024),
        compiler_params=params(),
    )(meta, first, second, reduced)


def flip(array, axis, bit):
    count = lax.axis_size(axis)
    return lax.ppermute(array, axis, [(i, i ^ bit) for i in range(count)])


def quarters(weight, axis):
    full = lax.all_gather(weight, "fsdp", axis=axis, tiled=True)
    return jnp.split(full, 4, axis=axis)


def after(array, *others):
    return lax.optimization_barrier((array, *others))[0]


def own_half(weight, axis):
    size = weight.shape[axis] // 2
    return lax.dynamic_slice_in_dim(weight, lax.axis_index("ctx") * size, size, axis)


def six_parts(weight, axis):
    shards = quarters(weight, axis)
    return shards[:2] + jnp.split(shards[2], 2, axis=axis) + jnp.split(shards[3], 2, axis=axis)


def shard_places(width, direct):
    unit = width // 4
    part = unit // 2
    if direct:
        four = [(lax.axis_index("fsdp") ^ bit) * unit for bit in range(4)]
        near = lax.axis_index("ctx") * part
    else:
        four, near = [0, unit, 2 * unit, 3 * unit], 0
    away = part - near
    return four, [four[0], four[1], four[2] + near, four[2] + away, four[3] + near, four[3] + away]


def pick_side(low, high, bit, axis):
    return jnp.where(
        bit == 0, jnp.concatenate([low, high], axis=axis), jnp.concatenate([high, low], axis=axis)
    )


def halve(array, axis, bit, stride):
    size = array.shape[-1] // 2
    keep = lax.dynamic_slice_in_dim(array, bit * size, size, array.ndim - 1)
    give = lax.dynamic_slice_in_dim(array, (1 - bit) * size, size, array.ndim - 1)
    taken = flip(give, axis, stride)
    return (keep.astype(f32) + taken.astype(f32)).astype(bf16)


def double(array, axis, bit, stride):
    taken = flip(array, axis, stride)
    return pick_side(array, taken, bit, array.ndim - 1)


def gather_sequences(full, part, *others):
    fsdp = lax.axis_size("fsdp")
    if fsdp != 4 or lax.axis_size("ctx") != 2 or lax.axis_size("tp") != 4:
        full = lax.psum(full, ("ctx", "tp"))
        part = [lax.psum(p, "ctx") for p in part]
        return (
            lax.all_gather(full, "fsdp", axis=0),
            [lax.all_gather(p, "fsdp", axis=0) for p in part],
        )
    own, side, place = lax.axis_index("fsdp"), lax.axis_index("ctx"), lax.axis_index("tp")
    full = halve(full, "ctx", side, 1)
    part = [halve(p, "ctx", side, 1) for p in part]
    full = halve(full, "tp", place % 2, 1)
    full = halve(full, "tp", place // 2, 2)

    def both(array, bit, stride):
        taken = flip(array, "fsdp", stride)
        return pick_side(array, taken, bit, 0)

    full = after(full, *others) if others else full
    full = both(full[None], own // 2, 2)
    part = [both(p[None], own // 2, 2) for p in part]
    full = double(full, "tp", place // 2, 2)
    full = double(full, "tp", place % 2, 1)
    full = double(full, "ctx", side, 1)
    part = [double(p, "ctx", side, 1) for p in part]

    def cores(array):
        taken = flip(array, "fsdp", 1)
        even = own % 2 == 0
        pairs = [jnp.where(even, array[i], taken[i]) for i in range(2)]
        others = [jnp.where(even, taken[i], array[i]) for i in range(2)]
        return jnp.stack([pairs[0], others[0], pairs[1], others[1]])

    return cores(full), [cores(p) for p in part]


def gather_ids(ids):
    if lax.axis_size("fsdp") != 4:
        return lax.all_gather(ids, "fsdp", tiled=True)
    own = lax.axis_index("fsdp")
    two = pick_side(ids, flip(ids, "fsdp", 1), own % 2, 0)
    return pick_side(two, flip(two, "fsdp", 2), own // 2, 0)


def on_device(
    hidden_in, segment_ids, adapter_ids, attention_gain, query_gain, key_gain, feedforward_gain,
    query_weight, key_weight, value_weight, output_weight, gate_weight, linear_weight, reduce_weight,
    query_down, query_lift, key_down, key_lift, value_down, value_lift, output_down, output_lift,
    gate_down, gate_lift, linear_down, linear_lift, reduce_down, reduce_lift, output_cotangent,
):
    _, length, model = hidden_in.shape
    head_dim = query_gain.shape[0]
    log_scale = head_dim**-0.5 * 1.4426950408889634
    context_index = lax.axis_index("ctx")
    tensor_index = lax.axis_index("tp")
    hid = hidden_in[0]
    cot = output_cotangent[0]
    direct = lax.axis_size("fsdp") == 4 and lax.axis_size("ctx") == 2
    four, six = shard_places(model, direct)
    values = (*four, tensor_index, context_index, 0, adapter_ids[0], *six, 0, 0)
    meta = jnp.stack([jnp.asarray(value, jnp.int32) for value in values])

    positions = (context_index * length + jnp.arange(length)).astype(f32)
    frequency = rope_base ** (-2.0 * jnp.arange(head_dim // 2).astype(f32) / head_dim)
    angles = positions[:, None] * frequency[None, :]
    cosine, sine = jnp.cos(angles), jnp.sin(angles)
    cos = jnp.concatenate([cosine] * 4, axis=1)
    sin = jnp.concatenate([-sine, sine] * 2, axis=1)
    q_gain = jnp.tile(query_gain.astype(f32), 2)[None]
    k_gain = jnp.tile(key_gain.astype(f32), 2)[None]
    a_gain = attention_gain[None]
    f_gain = feedforward_gain[None]
    seg_own = segment_ids.reshape(length, 1)
    count = lax.axis_size("ctx")
    onward = [(i, i + 1) for i in range(count - 1)]
    backward = [(i + 1, i) for i in range(count - 1)]
    turn = lambda table: jnp.swapaxes(table, 1, 2)
    qkv_downs = [turn(query_down), turn(key_down), turn(value_down)]
    qkv_lifts = [query_lift, key_lift, value_lift]
    output_first = turn(output_down)
    reduce_first = turn(reduce_down)

    kv_own = jnp.concatenate([key_weight, value_weight], axis=1)
    normed, qkv_narrow = attention_norm(meta, hid, a_gain, qkv_downs)
    if direct:
        q_across = flip(query_weight, "fsdp", 2)
        gate_half = own_half(gate_weight, 0)
        tables = (cos, sin, q_gain, k_gain, f_gain, seg_own, normed)
        kv_across = flip(after(kv_own, *tables), "fsdp", 2)
        cores = [flip(w, "fsdp", 1) for w in (gate_weight, linear_weight, reduce_weight)]
        q_side = flip(after(query_weight, q_across), "fsdp", 1)
        kv_side = flip(after(kv_own, kv_across), "fsdp", 1)
        qkv_weights = [
            query_weight, q_side, q_across,
            flip(after(q_across, *cores), "fsdp", 1),
            kv_own, kv_side, kv_across, flip(after(kv_across, *cores), "fsdp", 1),
        ]
        output_across = flip(after(output_weight, q_across, kv_across), "fsdp", 2)
        gate_across = flip(after(gate_half, q_across, kv_across), "fsdp", 2)
    else:
        qkv_weights = quarters(query_weight, 0) + quarters(kv_own, 0)
        output_weights = quarters(output_weight, 1)
        gates = six_parts(gate_weight, 0)
        linears = quarters(linear_weight, 0)
        reduces = quarters(reduce_weight, 1)

    pre, qrot, kv = qkv_forward(
        meta, normed, qkv_narrow, qkv_weights, qkv_lifts, q_gain, k_gain, cos, sin, seg_own
    )
    kv_far = lax.ppermute(kv, "ctx", onward)
    ready = after(qrot, output_across) if direct else qrot
    att, wide, inv = attention_forward(meta, ready, kv_far, kv, log_scale)
    if direct:
        gate_other = flip(after(gate_across, att), "ctx", 1)
        linear_across = flip(after(linear_weight, att, output_across, gate_across), "fsdp", 2)
        reduce_across = flip(after(reduce_weight, att, output_across, gate_across), "fsdp", 2)
        output_weights = [
            output_weight, flip(after(output_weight, kv_far), "fsdp", 1), output_across,
            flip(after(output_across, kv_far), "fsdp", 1),
        ]
    branch, output_narrow = output_forward(meta, att, output_weights, output_first, output_lift)
    if direct:
        gates = [
            gate_weight, cores[0], gate_across, gate_other, flip(after(gate_across, gate_other), "fsdp", 1),
            flip(gate_other, "fsdp", 1),
        ]
        linears = [linear_weight, cores[1], linear_across, flip(linear_across, "fsdp", 1)]
        reduces = [reduce_weight, cores[2], reduce_across, flip(reduce_across, "fsdp", 1)]
    branch = lax.psum(branch, "tp")

    back, inner, gate_grad, linear_grad, n_gl_t, m_gl_t, m_r_t = ffn(
        meta, hid, branch, cot, f_gain, gates, linears, reduces,
        [turn(gate_down), turn(linear_down), reduce_first], [gate_lift, linear_lift, reduce_lift],
    )
    summed = lax.psum(back, "tp")
    ffn_part, ffn_full, n_r = ffn_adapters(
        meta, hid, branch, cot, f_gain, inner, gate_grad, linear_grad, n_gl_t, m_gl_t, m_r_t,
        reduce_first,
    )
    sets = gather_ids(after(adapter_ids, inner))
    slots = query_down.shape[0]
    ffn_full, (ffn_part,) = gather_sequences(ffn_full, [ffn_part])
    hidden = gate_lift.shape[2]
    ffn_pieces = [(0, rank * i, 0, model) for i in range(3)] + [(1, rank * i, 0, hidden) for i in range(3)]
    ffn_grads = place_sets(sets, [ffn_full, ffn_part], ffn_pieces, slots, 1024)
    out = reduce_forward(meta, inner, n_r, reduces, reduce_lift)
    out_columns = lax.psum_scatter(out, "tp", scatter_dimension=1, tiled=True)
    block_out = close(meta, hid, branch, out_columns, bf16)
    settled = after(summed, *ffn_grads)

    dop, mixed, dq_far, dkv_far, output_part, output_full = attention_backward_far(
        meta, cot, settled, att, wide, inv, output_narrow, qrot, kv_far, segment_ids,
        output_weights, output_first, output_lift, log_scale,
    )
    dkv_back = lax.ppermute(dkv_far, "ctx", backward)
    dq_t, dkv_near = attention_backward_near(
        meta, dop, mixed, qrot, kv, segment_ids, dq_far, log_scale
    )
    grad, low, qkv_full, q_part, kv_part = qkv_grads(
        meta, normed, qkv_narrow, pre, dq_t, dkv_near, dkv_back, qkv_lifts, q_gain, k_gain, cos, sin
    )
    last = qkv_backward(meta, hid, a_gain, grad, low, qkv_weights, qkv_downs)
    last_columns = lax.psum_scatter(last, "tp", scatter_dimension=1, tiled=True)
    input_grad = close(meta, cot, summed, last_columns, f32)

    q_width, kv_width = query_lift.shape[2], key_lift.shape[2]
    att_full, (att_part,) = gather_sequences(
        jnp.concatenate([qkv_full, output_full], axis=0),
        [jnp.concatenate([q_part, kv_part, output_part], axis=1)],
        block_out,
    )

    att_pieces = [(0, rank * i, 0, model) for i in range(4)] + [
        (1, 0, 0, q_width),
        (1, 0, q_width, kv_width),
        (1, 0, q_width + kv_width, kv_width),
        (1, 0, q_width + 2 * kv_width, q_width),
    ]
    att_grads = place_sets(sets, [att_full, att_part], att_pieces, slots, 1 << 33)
    return (
        block_out[None],
        input_grad[None],
        turn(att_grads[0]),
        att_grads[4],
        turn(att_grads[1]),
        att_grads[5],
        turn(att_grads[2]),
        att_grads[6],
        turn(att_grads[7]),
        att_grads[3],
        turn(ffn_grads[0]),
        ffn_grads[3],
        turn(ffn_grads[1]),
        ffn_grads[4],
        turn(ffn_grads[5]),
        ffn_grads[2],
    )


def solution(mesh):
    tokens = P("fsdp", "ctx", None)
    rows_split = P("fsdp", "tp")
    lift_split = P(None, None, "tp")
    down_split = P(None, "tp", None)
    in_specs = (
        tokens, P("fsdp", "ctx"), P("fsdp"), P(), P(), P(), P(),
        rows_split, rows_split, rows_split, P("tp", "fsdp"), rows_split, rows_split, P("tp", "fsdp"),
        P(), lift_split, P(), lift_split, P(), lift_split, down_split, P(),
        P(), lift_split, P(), lift_split, down_split, P(), tokens,
    )
    cut = P("fsdp", "ctx", "tp")
    out_specs = (
        cut, cut, P(), lift_split, P(), lift_split, P(), lift_split, down_split, P(),
        P(), lift_split, P(), lift_split, down_split, P(),
    )
    return jax.shard_map(
        on_device, mesh=mesh, in_specs=in_specs, out_specs=out_specs, check_vma=False
    )
```
